32 devices in a mesh: groups: 2 (over x), ctx: 16 (over z, y, core).
Axes of the slice: x: 2, y: 2, z: 4, core: 2. Of those that a mesh axis runs over, the one named last changes fastest.
Arguments:
- queries: bfloat16 [4096, 2048], P(('groups', 'ctx')), parts along dimension 0, may hold values from -8 to 8
- keys: bfloat16 [4096, 2048], P(('groups', 'ctx')), parts along dimension 0, may hold values from -8 to 8
- values: bfloat16 [4096, 2048], P(('groups', 'ctx')), parts along dimension 0, may hold values from -8 to 8
- doc_start: int32 [32], P('groups'), parts along dimension 0, may hold values from 0 to 15, as said below
- out_weight: bfloat16 [2048, 4096], P(None, 'ctx'), may hold values from -0.125 to 0.125
Outputs:
- layer_out: bfloat16 [4096, 4096], P(('groups', 'ctx')), parts along dimension 0
The draws below stay inside these ranges and needn't reach their ends.
There are 2 independent parts, one for each index of `groups`. The reference program is written for one: setup_inputs(seed, part) draws one part's arguments, and reference() takes and returns one part's arrays. A program takes and returns all parts, laid end to end along the dimension named above; an argument that names none is the same for every part. Nothing has to cross between parts.
Inputs may be any that keep to these rules, and one draw needn't show every extreme that they name: doc_start[b] <= b, entries never fall, doc_start[doc_start[b]] = doc_start[b]; one document covers at least blocks 16 // 4 to 12.
All inputs are finite; a program needn't handle non-finite values.
Results may differ from the reference program's by a relative error of at most 0.0053.
Values may be sent and summed in bfloat16 or wider, within the bound.
No kernel may reach another device: no remote copies, remote signals or barrier semaphores. Data moves between devices by JAX's collectives and lax.ppermute only.
A program may use at most 128 MiB of HBM per device.

```python
import jax
import jax.numpy as jnp
from jax import lax

D = 4096
HEADS = 16
HD = 128
BLOCK = 128
TOKENS = 2048
NB = 16


def block_spread(key, salt):
    table = jax.random.normal(jax.random.fold_in(key, salt), (NB, 1, HEADS * HD), jnp.float32)
    return jnp.broadcast_to(table, (NB, BLOCK, HEADS * HD)).reshape(TOKENS, HEADS * HD)


def draw_queries(key, part):
    width = HEADS * HD
    noise = jax.random.normal(jax.random.fold_in(key, 5), (TOKENS, width), jnp.float32)
    drawn = noise + 0.15 * block_spread(key, 11)
    return jnp.clip(drawn, -8.0, 8.0).astype(jnp.bfloat16)


def draw_keys(key, part):
    width = HEADS * HD
    noise = jax.random.normal(jax.random.fold_in(key, 1), (TOKENS, width), jnp.float32)
    drawn = noise + 1.5 * block_spread(key, 11)
    return jnp.clip(drawn, -8.0, 8.0).astype(jnp.bfloat16)


def draw_values(key, part):
    width = HEADS * HD
    noise = jax.random.normal(jax.random.fold_in(key, 6), (TOKENS, width), jnp.float32)
    drawn = noise + 2.0 * block_spread(key, 21)
    return jnp.clip(drawn, -8.0, 8.0).astype(jnp.bfloat16)


def draw_doc_start(key, part):
    labels = jnp.arange(NB, dtype=jnp.int32)
    opens = jax.random.randint(jax.random.fold_in(key, 31), (NB,), 0, 4) == 0
    begin = jax.random.randint(jax.random.fold_in(key, 32), (), 0, NB // 4 + 1)
    finish = jax.random.randint(jax.random.fold_in(key, 33), (), 3 * NB // 4, NB - 1)
    opens = jnp.where((labels > begin) & (labels <= finish), False, opens)
    opens = opens | (labels == begin) | (labels == finish + 1) | (labels == 0) | (labels == NB - 1)
    return lax.cummax(jnp.where(opens, labels, 0), axis=0).astype(jnp.int32)


def block_levels(key, dims, cuts, smallest, largest):
    gain = 1.0
    for position, parts in cuts:
        heights = jax.random.uniform(jax.random.fold_in(jax.random.fold_in(key, 6), position), (parts,), jnp.float32, smallest / len(cuts), largest / len(cuts))
        gain = gain * jnp.repeat(jnp.exp(heights), dims[position] // parts).reshape((-1,) + (1,) * (len(dims) - 1 - position))
    return gain


def bell_draw(stream_key, shape, scale, limit, split=(), kind=jnp.bfloat16):
    factor_of = block_levels(stream_key, shape, split, -0.22, 0.18) if split else 1.0
    values = jax.random.normal(stream_key, shape, jnp.float32) * scale * factor_of
    return jnp.minimum(jnp.maximum(values, -limit), limit).astype(kind)


def setup_inputs(seed: int = 0, part: int = 0) -> dict:
    streams_of = jax.random.split(jax.random.key(seed), 6)
    part_keys = jax.random.split(jax.random.fold_in(streams_of[5], part), 6)
    return {
        "queries": draw_queries(jax.random.fold_in(jax.random.fold_in(streams_of[5], part), 71), part),
        "keys": draw_keys(jax.random.fold_in(jax.random.fold_in(streams_of[5], part), 71), part),
        "values": draw_values(jax.random.fold_in(jax.random.fold_in(streams_of[5], part), 71), part),
        "doc_start": draw_doc_start(jax.random.fold_in(jax.random.fold_in(streams_of[5], part), 71), part),
        "out_weight": bell_draw(streams_of[4], (HEADS * HD, D), (HEADS * HD) ** -0.5, 0.125, ((1, 16),)),
    }


def pair_mean(array):
    halves = array.reshape(array.shape[0] // 2, 2, array.shape[1]).astype(jnp.float32)
    return ((halves[:, 0] + halves[:, 1]) * 0.5).astype(jnp.bfloat16)


def reference(queries, keys, values, doc_start, out_weight):
    width = HEADS * HD
    depth = NB.bit_length() - 1
    level_keys = [keys]
    level_values = [values]
    for level in range(1, depth):
        level_keys.append(pair_mean(level_keys[-1]))
        level_values.append(pair_mean(level_values[-1]))
    offsets = jnp.arange(BLOCK, dtype=jnp.int32)

    def attend(block):
        query = lax.dynamic_slice_in_dim(queries, block * BLOCK, BLOCK, 0)
        key_list = [lax.dynamic_slice_in_dim(keys, block * BLOCK, BLOCK, 0)]
        value_list = [lax.dynamic_slice_in_dim(values, block * BLOCK, BLOCK, 0)]
        first_list = [jnp.zeros((BLOCK,), jnp.int32) + block]
        last_list = [jnp.zeros((BLOCK,), jnp.int32) + block]
        for level in range(1, depth + 1):
            factor = 2 ** (level - 1)
            sibling = jnp.bitwise_xor(block // factor, 1)
            key_list.append(lax.dynamic_slice_in_dim(level_keys[level - 1], sibling * BLOCK, BLOCK, 0))
            value_list.append(lax.dynamic_slice_in_dim(level_values[level - 1], sibling * BLOCK, BLOCK, 0))
            first_token = sibling * (BLOCK * factor) + offsets * factor
            first_list.append(first_token // BLOCK)
            last_list.append((first_token + factor - 1) // BLOCK)
        key_set = jnp.concatenate(key_list, 0).astype(jnp.float32).reshape(-1, HEADS, HD)
        value_set = jnp.concatenate(value_list, 0).astype(jnp.float32).reshape(-1, HEADS, HD)
        own_doc = doc_start[block]
        allowed = (doc_start[jnp.concatenate(first_list)] == own_doc) & (doc_start[jnp.concatenate(last_list)] == own_doc)
        query_set = query.astype(jnp.float32).reshape(BLOCK, HEADS, HD)
        scores = jnp.einsum("qhd,khd->hqk", query_set, key_set) * (HD ** -0.5)
        scores = jnp.where(allowed[None, None, :], scores, -jnp.inf)
        row_max = jnp.max(scores, axis=-1, keepdims=True)
        raised = jnp.exp(scores - row_max)
        weights = (raised / jnp.sum(raised, axis=-1, keepdims=True)).astype(jnp.bfloat16)
        mixed = jnp.einsum("hqk,khd->qhd", weights.astype(jnp.float32), value_set)
        return mixed.reshape(BLOCK, width).astype(jnp.bfloat16)

    attended = lax.map(attend, jnp.arange(NB, dtype=jnp.int32)).reshape(TOKENS, width)
    return jnp.dot(attended, out_weight, preferred_element_type=jnp.float32).astype(jnp.bfloat16)
```

```python
import functools

import jax
import jax.numpy as jnp
import numpy as np
from jax import lax
from jax.experimental import pallas as pl
from jax.experimental.pallas import tpu as pltpu
from jax.sharding import PartitionSpec as P

HD = 128
BLOCK = 128

CORE, Y, LOW, HIGH = 1, 2, 4, 8
TEAM = (0, CORE, LOW, CORE | LOW)
VMEM_LIMIT = 48 * 2**20


def swap(value, mask):
    pairs = [(source, source ^ mask) for source in range(lax.axis_size("ctx"))]
    return lax.ppermute(value, "ctx", pairs)


def swap_groups(value):
    return lax.ppermute(value, "groups", [(0, 1), (1, 0)])


def vmem(count):
    return [pl.BlockSpec(memory_space=pltpu.VMEM)] * count


def call(kernel, outs, in_specs, out_specs=None, **more):
    return pl.pallas_call(
        kernel,
        out_shape=[jax.ShapeDtypeStruct(shape, jnp.bfloat16) for shape in outs],
        in_specs=in_specs,
        out_specs=vmem(len(outs)) if out_specs is None else out_specs,
        compiler_params=pltpu.CompilerParams(vmem_limit_bytes=VMEM_LIMIT),
        **more,
    )


def halve(rows):
    count = rows.shape[0]
    row = lax.broadcasted_iota(jnp.int32, (count // 2, count), 0)
    column = lax.broadcasted_iota(jnp.int32, (count // 2, count), 1)
    pick = jnp.where(column // 2 == row, 0.5, 0.0).astype(jnp.bfloat16)
    return jnp.dot(pick, rows, preferred_element_type=jnp.float32).astype(jnp.bfloat16)


def columns_of(place, j, width):
    return pl.ds(pl.multiple_of(jnp.bitwise_xor(place, j) * width, width), width)


def pack_kernel(place_ref, q_ref, k_ref, v_ref, a0, a1, a2, a3, y_ref, z_ref):
    width = a0.shape[1]
    for j, out in enumerate((a0, a1, a2, a3)):
        columns = columns_of(place_ref[0], j, width)
        for n, source in enumerate((q_ref, k_ref, v_ref)):
            out[n * BLOCK : (n + 1) * BLOCK, :] = source[:, columns]
    for n, source in enumerate((k_ref, v_ref)):
        second = halve(source[...])
        y_ref[n * 64 : (n + 1) * 64, :] = second
        z_ref[n * 16 : (n + 1) * 16, :] = halve(halve(second))


def repack_kernel(place_ref, y_ref, z_ref, zy_ref, b0, b1, b2, b3):
    width = b0.shape[1]
    for j, out in enumerate((b0, b1, b2, b3)):
        columns = columns_of(place_ref[0], j, width)
        out[0:128, :] = y_ref[:, columns]
        out[128:160, :] = z_ref[:, columns]
        out[160:192, :] = zy_ref[:, columns]


def attention_kernel(bias_ref, a0, a1, a2, a3, b0, b1, b2, b3, out_ref, key_ref, value_ref):
    own = (a0, a1, a2, a3)
    far = (b0, b1, b2, b3)
    heads = out_ref.shape[1] // HD
    for n, rows_ref in enumerate((key_ref, value_ref)):
        at = 128 + 128 * n
        for j in range(4):
            half, part = divmod(j, 2)
            here, there = rows_ref.at[half], rows_ref.at[1 - half]
            near = own[j][at : at + 128, :]
            second = far[j][64 * n : 64 * n + 64, :]
            here[128 * part : 128 * part + 128, :] = near
            here[256 + 64 * part : 320 + 64 * part, :] = second
            there[384 + 32 * part : 416 + 32 * part, :] = halve(halve(near))
            there[448 + 32 * part : 480 + 32 * part, :] = halve(second)
            for to in (here, there):
                to[512 + 16 * j : 528 + 16 * j, :] = far[j][128 + 16 * n : 144 + 16 * n, :]
                to[576 + 16 * j : 592 + 16 * j, :] = far[j][160 + 16 * n : 176 + 16 * n, :]
    for half in range(2):
        bias = jnp.concatenate(
            [jnp.broadcast_to(bias_ref[2 * half + n : 2 * half + n + 1, :], (BLOCK, 640)) for n in range(2)], 0
        )
        for head in range(heads):
            columns = slice(head * HD, (head + 1) * HD)
            query = jnp.concatenate([own[2 * half][0:128, columns], own[2 * half + 1][0:128, columns]], 0)
            score = lax.dot_general(
                query, key_ref[half, :, columns], (((1,), (1,)), ((), ())), preferred_element_type=jnp.float32
            )
            score = score * HD ** (-0.5) + bias
            raised = jnp.exp(score - jnp.max(score, axis=-1, keepdims=True))
            weight = raised * (1.0 / jnp.sum(raised, axis=-1, keepdims=True))
            mixed = jnp.dot(
                weight.astype(jnp.bfloat16), value_ref[half, :, columns], preferred_element_type=jnp.float32
            )
            out_ref[256 * half : 256 * half + 256, columns] = mixed.astype(jnp.bfloat16)


def project_kernel(place_ref, o0, o1, o2, o3, own_w, *refs):
    halves, outs, weight_ref, sems = refs[:6], refs[6:10], refs[10], refs[11]
    place, group = place_ref[0], place_ref[1]
    rows = own_w.shape[0]
    half = rows // 2
    wide = own_w.shape[1]
    ours = pl.ds(pl.multiple_of(group * half, half), half)
    theirs = pl.ds(pl.multiple_of((1 - group) * half, half), half)
    copies = [[pltpu.make_async_copy(own_w, weight_ref.at[0], sems.at[0])]]
    for q in range(3):
        copies.append(
            [
                pltpu.make_async_copy(halves[2 * q], weight_ref.at[q + 1, ours, :], sems.at[2 * q + 1]),
                pltpu.make_async_copy(halves[2 * q + 1], weight_ref.at[q + 1, theirs, :], sems.at[2 * q + 2]),
            ]
        )
    for pair in copies:
        for copy in pair:
            copy.start()
    mixed = (o0, o1, o2, o3)
    depth = o0.shape[1]
    for q in range(4):
        for copy in copies[q]:
            copy.wait()
        total = [None] * 4
        for j in range(4):
            part = weight_ref[q, pl.ds(pl.multiple_of(jnp.bitwise_xor(place, j) * depth, depth), depth), :]
            product = jnp.dot(mixed[j][...], part, preferred_element_type=jnp.float32)
            for r in range(4):
                piece = product[(r ^ j) * BLOCK : (r ^ j) * BLOCK + BLOCK, :]
                total[r] = piece if j == 0 else total[r] + piece
        for r in range(4):
            outs[r][:, q * wide : (q + 1) * wide] = total[r].astype(jnp.bfloat16)


def place_kernel(place_ref, r0, r1, r2, r3, out_ref, sems):
    wide = r0.shape[1] // 4
    copies = []
    for j, source in enumerate((r0, r1, r2, r3)):
        for q in range(4):
            mask = TEAM[j] | (Y if q & 1 else 0) | (HIGH if q & 2 else 0)
            at = pl.multiple_of(jnp.bitwise_xor(place_ref[2], mask) * wide, wide)
            copies.append(
                pltpu.make_async_copy(
                    source.at[:, q * wide : (q + 1) * wide], out_ref.at[:, pl.ds(at, wide)], sems.at[4 * j + q]
                )
            )
    for copy in copies:
        copy.start()
    for copy in copies:
        copy.wait()


def key_masks():
    masks = np.zeros((2, 640), np.int32)
    for half in range(2):
        for part in range(2):
            near, across = TEAM[2 * half + part], TEAM[2 * (1 - half) + part]
            masks[half, 128 * part : 128 * part + 128] = near
            masks[half, 256 + 64 * part : 320 + 64 * part] = near ^ Y
            masks[half, 384 + 32 * part : 416 + 32 * part] = across
            masks[half, 448 + 32 * part : 480 + 32 * part] = across ^ Y
        for j in range(4):
            masks[half, 512 + 16 * j : 528 + 16 * j] = TEAM[j] ^ HIGH
            masks[half, 576 + 16 * j : 592 + 16 * j] = TEAM[j] ^ HIGH ^ Y
    return masks


def per_device_fast(queries, keys, values, doc_start, out_weight):
    length, width = queries.shape
    share = width // 4
    depth, wide = out_weight.shape
    group = lax.axis_index("groups")
    position = lax.axis_index("ctx")
    place = (position & 1) | ((position >> 1) & 2)
    places = jnp.stack([place, group, position]).astype(jnp.int32)
    scalars = pl.BlockSpec(memory_space=pltpu.SMEM)
    anywhere = pl.BlockSpec(memory_space=pl.ANY)

    masks = key_masks()
    key_docs = doc_lookup(jnp.bitwise_xor(position, masks), doc_start)
    query_docs = doc_lookup(jnp.bitwise_xor(position, np.array(TEAM, np.int32)), doc_start)
    allowed = jnp.repeat(key_docs, 2, axis=0) == query_docs[:, None]
    bias = jnp.where(allowed, 0.0, -jnp.inf).astype(jnp.float32)

    *team, to_y, to_z = call(
        pack_kernel,
        [(3 * length, share)] * 4 + [(length, width), (length // 4, width)],
        [scalars] + vmem(3),
        name="pack",
    )(places, queries, keys, values)
    from_y = swap(to_y, Y)
    from_z = swap(to_z, HIGH)
    from_zy = swap(to_z, HIGH | Y)
    own = [team[0]] + [swap(team[j], TEAM[j]) for j in (1, 2, 3)]

    half = lax.dynamic_slice_in_dim(out_weight, group * (depth // 2), depth // 2, 0)
    half_y = swap(half, Y)
    half_z = swap(half, HIGH)
    half_d = swap(half_z, Y)
    other_y, other_z, other_d = swap_groups(half_y), swap_groups(half_z), swap_groups(half_d)

    extra = call(repack_kernel, [(192, share)] * 4, [scalars] + vmem(3), name="repack")(
        places, from_y, from_z, from_zy
    )
    far = [extra[0]] + [swap(extra[j], TEAM[j]) for j in (1, 2, 3)]
    (attended,) = call(
        attention_kernel,
        [(4 * length, share)],
        vmem(9),
        scratch_shapes=[pltpu.VMEM((2, 640, share), jnp.bfloat16)] * 2,
        name="attend",
    )(bias, *own, *far)
    from_core = swap(attended, CORE)
    from_low = swap(attended, LOW)
    from_both = swap(from_low, CORE)
    parts = call(
        project_kernel,
        [(length, 4 * wide)] * 4,
        [scalars] + vmem(4) + [anywhere] * 7,
        scratch_shapes=[pltpu.VMEM((4, depth, wide), jnp.bfloat16), pltpu.SemaphoreType.DMA((7,))],
        name="project",
    )(places, attended, from_core, from_low, from_both, out_weight, half_y, other_y, half_z, other_z, half_d, other_d)
    received = [parts[0]] + [swap(parts[j], TEAM[j]) for j in (1, 2, 3)]
    (out,) = call(
        place_kernel,
        [(length, 16 * wide)],
        [scalars] + [anywhere] * 4,
        [anywhere],
        scratch_shapes=[pltpu.SemaphoreType.DMA((16,))],
        name="place",
    )(places, *received)
    return out


def partner(value, axis, apart):
    mask = 2**apart
    pairs = [(source, source ^ mask) for source in range(lax.axis_size(axis))]
    return lax.ppermute(value, axis, pairs)


def pair_mean(array):
    halves = array.reshape(array.shape[0] // 2, 2, array.shape[1]).astype(jnp.float32)
    return ((halves[:, 0] + halves[:, 1]) * 0.5).astype(jnp.bfloat16)


def doc_lookup(blocks, table):
    labels = jnp.arange(table.shape[0], dtype=jnp.int32)
    return jnp.sum(jnp.where(blocks[..., None] == labels, table, 0), axis=-1)


def covered(first_token, factor):
    return (first_token // BLOCK, (first_token + factor - 1) // BLOCK)


def trade(pair, bit):
    return partner((pair[0], pair[1]), "ctx", bit)


def per_device(queries, keys, values, doc_start, out_weight):
    length, width = queries.shape
    heads = width // HD
    blocks = length // BLOCK
    local_depth = blocks.bit_length() - 1
    devices = lax.axis_size("ctx")
    position = lax.axis_index("ctx")
    bit_count = devices.bit_length() - 1
    scale = HD ** (-0.5)
    offsets = jnp.arange(BLOCK, dtype=jnp.int32)
    block_ids = position * blocks + jnp.arange(blocks, dtype=jnp.int32)
    own_docs = doc_lookup(block_ids, doc_start)
    level_keys = [keys]
    level_values = [values]
    near_keys = keys.reshape(blocks, BLOCK, width)
    near_values = values.reshape(blocks, BLOCK, width)
    near_first = jnp.broadcast_to(block_ids[:, None], (blocks, BLOCK))
    near_last = jnp.broadcast_to(block_ids[:, None], (blocks, BLOCK))
    local_allowed = (doc_lookup(near_first, doc_start) == own_docs[:, None]) & (
        doc_lookup(near_last, doc_start) == own_docs[:, None]
    )
    query_blocks = queries.reshape(blocks, BLOCK, heads, HD)
    local_scores = (
        jnp.einsum(
            "bqhd,bkhd->bhqk",
            query_blocks,
            near_keys.reshape(blocks, -1, heads, HD),
            preferred_element_type=jnp.float32,
        )
        * scale
    )
    local_scores = jnp.where(local_allowed[:, None, None, :], local_scores, -jnp.inf)
    far_keys = []
    far_values = []
    far_first = []
    far_last = []

    def record(other_keys, other_values, bit):
        factor = 2 ** (local_depth + bit)
        sibling = jnp.bitwise_xor(position // 2**bit, 1)
        first_token = sibling * 2**bit * length + offsets * factor
        lower, upper = covered(first_token, factor)
        far_keys.append(other_keys)
        far_values.append(other_values)
        far_first.append(lower)
        far_last.append(upper)

    rep_keys = level_keys[local_depth]
    rep_values = level_values[local_depth]
    for bit in range(bit_count):
        other_keys, other_values = trade((rep_keys, rep_values), bit)
        record(other_keys, other_values, bit)
        if bit + 1 < bit_count:
            upper_half = position // 2**bit % 2 == 1
            low_keys = jnp.where(upper_half, other_keys, rep_keys)
            high_keys = jnp.where(upper_half, rep_keys, other_keys)
            low_values = jnp.where(upper_half, other_values, rep_values)
            high_values = jnp.where(upper_half, rep_values, other_values)
            rep_keys = jnp.concatenate([pair_mean(low_keys), pair_mean(high_keys)], 0)
            rep_values = jnp.concatenate([pair_mean(low_values), pair_mean(high_values)], 0)
    far_key_set = jnp.concatenate(far_keys, 0).reshape(-1, heads, HD)
    far_value_set = jnp.concatenate(far_values, 0).reshape(-1, heads, HD)
    far_lower = doc_lookup(jnp.concatenate(far_first, 0), doc_start)
    far_upper = doc_lookup(jnp.concatenate(far_last, 0), doc_start)
    far_allowed = (far_lower[None, :] == own_docs[:, None]) & (
        far_upper[None, :] == own_docs[:, None]
    )
    far_scores = (
        jnp.einsum("bqhd,khd->bhqk", query_blocks, far_key_set, preferred_element_type=jnp.float32)
        * scale
    )
    far_scores = jnp.where(far_allowed[:, None, None, :], far_scores, -jnp.inf)
    row_max = jnp.maximum(
        jnp.max(local_scores, axis=-1, keepdims=True), jnp.max(far_scores, axis=-1, keepdims=True)
    )
    local_raised = jnp.exp(local_scores - row_max)
    far_raised = jnp.exp(far_scores - row_max)
    total = jnp.sum(local_raised, axis=-1, keepdims=True) + jnp.sum(
        far_raised, axis=-1, keepdims=True
    )
    local_weights = (local_raised / total).astype(jnp.bfloat16)
    far_weights = (far_raised / total).astype(jnp.bfloat16)
    attended = jnp.einsum(
        "bhqk,bkhd->bqhd",
        local_weights,
        near_values.reshape(blocks, -1, heads, HD),
        preferred_element_type=jnp.float32,
    )
    attended = attended + jnp.einsum(
        "bhqk,khd->bqhd", far_weights, far_value_set, preferred_element_type=jnp.float32
    )
    attended = attended.reshape(length, width).astype(jnp.bfloat16)
    return jnp.dot(
        attended,
        lax.all_gather(out_weight, "ctx", axis=1, tiled=True),
        preferred_element_type=jnp.float32,
    ).astype(jnp.bfloat16)


def solution(mesh):
    fast = mesh.shape["groups"] == 2 and mesh.shape["ctx"] == 16
    placed = (
        P(("groups", "ctx"), None),
        P(("groups", "ctx"), None),
        P(("groups", "ctx"), None),
        P("groups"),
        P(None, "ctx"),
    )
    return jax.shard_map(
        per_device_fast if fast else per_device,
        mesh=mesh,
        in_specs=placed,
        out_specs=P(("groups", "ctx"), None),
        check_vma=False,
    )
```

```python
import functools

import jax
import jax.numpy as jnp
import numpy as np
from jax import lax
from jax.experimental import pallas as pl
from jax.experimental.pallas import tpu as pltpu
from jax.sharding import PartitionSpec as P

HD = 128
BLOCK = 128

LOW, HIGH = 4, 8
VMEM_LIMIT = 48 * 2**20


def swap(value, mask):
    pairs = [(source, source ^ mask) for source in range(lax.axis_size("ctx"))]
    return lax.ppermute(value, "ctx", pairs)


def swap_groups(value):
    return lax.ppermute(value, "groups", [(0, 1), (1, 0)])


def after(value, other):
    return lax.optimization_barrier((value, other))[0]


def vmem(count):
    return [pl.BlockSpec(memory_space=pltpu.VMEM)] * count


def anywhere(count):
    return [pl.BlockSpec(memory_space=pltpu.HBM)] * count


def call(kernel, outs, in_specs, out_specs=None, **more):
    return pl.pallas_call(
        kernel,
        out_shape=[jax.ShapeDtypeStruct(shape, jnp.bfloat16) for shape in outs],
        in_specs=[pl.BlockSpec(memory_space=pltpu.SMEM)] + in_specs,
        out_specs=vmem(len(outs)) if out_specs is None else out_specs,
        compiler_params=pltpu.CompilerParams(vmem_limit_bytes=VMEM_LIMIT),
        **more,
    )


def halve(rows):
    count = rows.shape[0]
    row = lax.broadcasted_iota(jnp.int32, (count // 2, count), 0)
    column = lax.broadcasted_iota(jnp.int32, (count // 2, count), 1)
    pick = jnp.where(column // 2 == row, 0.5, 0.0).astype(jnp.bfloat16)
    return jnp.dot(pick, rows, preferred_element_type=jnp.float32).astype(jnp.bfloat16)


def columns_of(place, j, width):
    return pl.ds(pl.multiple_of(jnp.bitwise_xor(place, j) * width, width), width)


def run_copies(copies):
    for copy in copies:
        copy.start()
    for copy in copies:
        copy.wait()


def pack_kernel(place_ref, q_ref, k_ref, v_ref, weight_ref, ours_ref, theirs_ref, a0, a1, a2, a3, third_ref, fourth_ref, rows_ref, sems):
    width = a0.shape[1]
    half = ours_ref.shape[0]
    ours = pl.ds(pl.multiple_of(place_ref[1] * half, half), half)
    theirs = pl.ds(pl.multiple_of((1 - place_ref[1]) * half, half), half)
    loads = [pltpu.make_async_copy(source, rows_ref.at[n], sems.at[n]) for n, source in enumerate((k_ref, v_ref))]
    copies = [
        pltpu.make_async_copy(weight_ref.at[ours, :], ours_ref, sems.at[14]),
        pltpu.make_async_copy(weight_ref.at[theirs, :], theirs_ref, sems.at[15]),
    ]
    for j, out in ((2, a2), (3, a3), (1, a1), (0, a0)):
        columns = columns_of(place_ref[0], j, width)
        for n, source in enumerate((q_ref, k_ref, v_ref)):
            to = out.at[n * BLOCK : (n + 1) * BLOCK, :]
            copies.append(pltpu.make_async_copy(source.at[:, columns], to, sems.at[2 + 3 * j + n]))
    for copy in loads + copies:
        copy.start()
    for n in range(2):
        loads[n].wait()
        third = halve(halve(rows_ref[n]))
        third_ref[n * 32 : (n + 1) * 32, :] = third
        fourth_ref[n * 16 : (n + 1) * 16, :] = halve(third)
    for copy in copies:
        copy.wait()


def repack_kernel(place_ref, l_ref, h_ref, lh_ref, b0, b1, b2, b3):
    width = b0.shape[1]
    for j, out in enumerate((b0, b1, b2, b3)):
        columns = columns_of(place_ref[0], j, width)
        out[0:64, :] = l_ref[:, columns]
        out[64:96, :] = h_ref[:, columns]
        out[96:128, :] = lh_ref[:, columns]


def attention_kernel(half, place_ref, bias_ref, a0, a1, a2, a3, b0, b1, b2, b3, before_ref, out_ref, key_ref, value_ref):
    del place_ref, before_ref
    own = (a0, a1, a2, a3)
    far = (b0, b1, b2, b3)
    heads = out_ref.shape[1] // HD
    for n, rows_ref in enumerate((key_ref, value_ref)):
        at = 128 + 128 * n
        for part in range(2):
            rows_ref[128 * part : 128 * part + 128, :] = own[2 * half + part][at : at + 128, :]
            rows_ref[256 + 64 * part : 320 + 64 * part, :] = halve(own[2 - 2 * half + part][at : at + 128, :])
        for j in range(4):
            rows_ref[384 + 32 * j : 416 + 32 * j, :] = far[j][32 * n : 32 * n + 32, :]
            rows_ref[512 + 16 * j : 528 + 16 * j, :] = far[j][64 + 16 * n : 80 + 16 * n, :]
            rows_ref[576 + 16 * j : 592 + 16 * j, :] = far[j][96 + 16 * n : 112 + 16 * n, :]
    for head in range(heads):
        columns = slice(head * HD, (head + 1) * HD)
        for part in range(2):
            query = own[2 * half + part][0:128, columns]
            score = lax.dot_general(
                query, key_ref[:, columns], (((1,), (1,)), ((), ())), preferred_element_type=jnp.float32
            )
            score = score * HD ** (-0.5) + bias_ref[2 * half + part : 2 * half + part + 1, :]
            raised = jnp.exp(score - jnp.max(score, axis=-1, keepdims=True))
            weight = raised * (1.0 / jnp.sum(raised, axis=-1, keepdims=True))
            mixed = jnp.dot(
                weight.astype(jnp.bfloat16), value_ref[:, columns], preferred_element_type=jnp.float32
            )
            out_ref[128 * part : 128 * part + 128, columns] = mixed.astype(jnp.bfloat16)


def project_kernel(count, place_ref, *refs):
    mixed, refs = refs[:8], refs[8:]
    blocks, outs, weight_ref, rows_ref, sems = refs[:-7], refs[-7:-3], refs[-3], refs[-2], refs[-1]
    place, group = place_ref[0], place_ref[1]
    depth, wide = weight_ref.shape[1:]
    half = depth // 2
    ours = pl.ds(pl.multiple_of(group * half, half), half)
    theirs = pl.ds(pl.multiple_of((1 - group) * half, half), half)
    copies = []
    blocks = list(blocks)
    for q in range(count):
        if blocks[0].shape[0] == depth:
            copies.append([pltpu.make_async_copy(blocks.pop(0), weight_ref.at[q], sems.at[2 * q])])
        else:
            copies.append(
                [
                    pltpu.make_async_copy(blocks.pop(0), weight_ref.at[q, ours, :], sems.at[2 * q]),
                    pltpu.make_async_copy(blocks.pop(0), weight_ref.at[q, theirs, :], sems.at[2 * q + 1]),
                ]
            )
    for pair in copies:
        for copy in pair:
            copy.start()
    share = mixed[0].shape[1]
    for j in range(4):
        columns = columns_of(place, j, share)
        for r in range(4):
            piece = mixed[2 * j + ((r ^ j) >> 1)]
            at = ((r ^ j) & 1) * BLOCK
            rows_ref[r * BLOCK : (r + 1) * BLOCK, columns] = piece[at : at + BLOCK, :]
    for q in range(count):
        for copy in copies[q]:
            copy.wait()
        total = jnp.dot(rows_ref[...], weight_ref[q], preferred_element_type=jnp.float32).astype(jnp.bfloat16)
        for r in range(4):
            outs[r][:, q * wide : (q + 1) * wide] = total[r * BLOCK : (r + 1) * BLOCK, :]


def place_kernel(place_ref, *refs):
    sources, out_ref, sems = refs[:-2], refs[-2], refs[-1]
    wide = out_ref.shape[1] // 16
    copies = []
    for n, source in enumerate(sources):
        masks = ((0, HIGH), (LOW, LOW | HIGH))[n // 4]
        for q, mask in enumerate(masks):
            at = pl.multiple_of(jnp.bitwise_xor(place_ref[2], mask | n % 4) * wide, wide)
            copies.append(
                pltpu.make_async_copy(
                    source.at[:, q * wide : (q + 1) * wide], out_ref.at[:, pl.ds(at, wide)], sems.at[len(copies)]
                )
            )
    run_copies(copies)


def key_masks():
    masks = np.zeros((2, 640), np.int32)
    for half in range(2):
        for part in range(2):
            masks[half, 128 * part : 128 * part + 128] = 2 * half + part
            masks[half, 256 + 64 * part : 320 + 64 * part] = 2 - 2 * half + part
        for j in range(4):
            masks[half, 384 + 32 * j : 416 + 32 * j] = j | LOW
            masks[half, 512 + 16 * j : 528 + 16 * j] = j | HIGH
            masks[half, 576 + 16 * j : 592 + 16 * j] = j | LOW | HIGH
    return masks


def per_device_fast(queries, keys, values, doc_start, out_weight):
    length, width = queries.shape
    share = width // 4
    depth, wide = out_weight.shape
    group = lax.axis_index("groups")
    position = lax.axis_index("ctx")
    places = jnp.stack([position & 3, group, position]).astype(jnp.int32)

    key_docs = doc_lookup(jnp.bitwise_xor(position, key_masks()), doc_start)
    query_docs = doc_lookup(jnp.bitwise_xor(position, np.arange(4, dtype=np.int32)), doc_start)
    allowed = jnp.repeat(key_docs, 2, axis=0) == query_docs[:, None]
    bias = jnp.where(allowed, 0.0, -jnp.inf).astype(jnp.float32)

    queries, keys, values, out_weight = (
        pltpu.with_memory_space_constraint(array, pltpu.HBM) for array in (queries, keys, values, out_weight)
    )
    ours, theirs, *team, third, fourth = call(
        pack_kernel,
        [(depth // 2, wide)] * 2 + [(3 * length, share)] * 4 + [(length // 2, width), (length // 4, width)],
        anywhere(4),
        scratch_shapes=[pltpu.VMEM((2, length, width), jnp.bfloat16), pltpu.SemaphoreType.DMA((16,))],
        name="pack",
    )(places, queries, keys, values, out_weight)
    half_h = swap(ours, HIGH)
    own = [team[0], None, swap(team[2], 2), swap(team[3], 3)]
    from_l = swap(third, LOW)
    from_h = swap(fourth, HIGH)
    from_lh = swap(from_h, LOW)
    ours_l = swap(after(ours, from_l), LOW)
    own[1] = swap(after(team[1], from_lh), 1)
    extra = call(repack_kernel, [(length, share)] * 4, vmem(3), name="repack")(places, from_l, from_h, from_lh)
    far = [
        extra[0],
        swap(after(extra[1], own[3]), 1),
        swap(after(extra[2], own[2]), 2),
        swap(after(extra[3], own[3]), 3),
    ]

    pieces = [[None] * 2 for _ in range(4)]
    before = places
    for n in range(2):
        (attended,) = call(
            functools.partial(attention_kernel, n),
            [(2 * length, share)],
            vmem(9) + [pl.BlockSpec(memory_space=pl.ANY)],
            scratch_shapes=[pltpu.VMEM((640, share), jnp.bfloat16)] * 2,
            name="attend%d" % n,
        )(places, bias, *own, *far, before)
        before = attended
        pieces[0][n] = attended
        pieces[2][n] = swap(attended, 2)
        pieces[1][n] = swap(attended, 1)
        pieces[3][n] = swap(pieces[2][n], 1)
    half_h = after(half_h, pieces[0][0])
    half_d = swap(after(half_h, ours_l), LOW)
    other_h = swap_groups(half_h)
    theirs_l = swap(after(theirs, half_d), LOW)
    other_d = swap_groups(half_d)
    mixed = [piece for pair in pieces for piece in pair]

    received = []
    for n, blocks in enumerate(((out_weight, half_h, other_h), (ours_l, theirs_l, half_d, other_d))):
        parts = call(
            functools.partial(project_kernel, 2),
            [(length, 2 * wide)] * 4,
            vmem(8) + anywhere(len(blocks)),
            scratch_shapes=[
                pltpu.VMEM((2, depth, wide), jnp.bfloat16),
                pltpu.VMEM((4 * length, width), jnp.bfloat16),
                pltpu.SemaphoreType.DMA((4,)),
            ],
            name="project%d" % n,
        )(places, *mixed, *blocks)
        received += [parts[0]] + [swap(parts[j], j) for j in (1, 2, 3)]
    (out,) = call(
        place_kernel,
        [(length, 16 * wide)],
        anywhere(8),
        anywhere(1),
        scratch_shapes=[pltpu.SemaphoreType.DMA((16,))],
        name="place",
    )(places, *received)
    return out


def partner(value, axis, apart):
    mask = 2**apart
    pairs = [(source, source ^ mask) for source in range(lax.axis_size(axis))]
    return lax.ppermute(value, axis, pairs)


def pair_mean(array):
    halves = array.reshape(array.shape[0] // 2, 2, array.shape[1]).astype(jnp.float32)
    return ((halves[:, 0] + halves[:, 1]) * 0.5).astype(jnp.bfloat16)


def doc_lookup(blocks, table):
    labels = jnp.arange(table.shape[0], dtype=jnp.int32)
    return jnp.sum(jnp.where(blocks[..., None] == labels, table, 0), axis=-1)


def covered(first_token, factor):
    return (first_token // BLOCK, (first_token + factor - 1) // BLOCK)


def trade(pair, bit):
    return partner((pair[0], pair[1]), "ctx", bit)


def per_device(queries, keys, values, doc_start, out_weight):
    length, width = queries.shape
    heads = width // HD
    blocks = length // BLOCK
    local_depth = blocks.bit_length() - 1
    devices = lax.axis_size("ctx")
    position = lax.axis_index("ctx")
    bit_count = devices.bit_length() - 1
    scale = HD ** (-0.5)
    offsets = jnp.arange(BLOCK, dtype=jnp.int32)
    block_ids = position * blocks + jnp.arange(blocks, dtype=jnp.int32)
    own_docs = doc_lookup(block_ids, doc_start)
    level_keys = [keys]
    level_values = [values]
    near_keys = keys.reshape(blocks, BLOCK, width)
    near_values = values.reshape(blocks, BLOCK, width)
    near_first = jnp.broadcast_to(block_ids[:, None], (blocks, BLOCK))
    near_last = jnp.broadcast_to(block_ids[:, None], (blocks, BLOCK))
    local_allowed = (doc_lookup(near_first, doc_start) == own_docs[:, None]) & (
        doc_lookup(near_last, doc_start) == own_docs[:, None]
    )
    query_blocks = queries.reshape(blocks, BLOCK, heads, HD)
    local_scores = (
        jnp.einsum(
            "bqhd,bkhd->bhqk",
            query_blocks,
            near_keys.reshape(blocks, -1, heads, HD),
            preferred_element_type=jnp.float32,
        )
        * scale
    )
    local_scores = jnp.where(local_allowed[:, None, None, :], local_scores, -jnp.inf)
    far_keys = []
    far_values = []
    far_first = []
    far_last = []

    def record(other_keys, other_values, bit):
        factor = 2 ** (local_depth + bit)
        sibling = jnp.bitwise_xor(position // 2**bit, 1)
        first_token = sibling * 2**bit * length + offsets * factor
        lower, upper = covered(first_token, factor)
        far_keys.append(other_keys)
        far_values.append(other_values)
        far_first.append(lower)
        far_last.append(upper)

    rep_keys = level_keys[local_depth]
    rep_values = level_values[local_depth]
    for bit in range(bit_count):
        other_keys, other_values = trade((rep_keys, rep_values), bit)
        record(other_keys, other_values, bit)
        if bit + 1 < bit_count:
            upper_half = position // 2**bit % 2 == 1
            low_keys = jnp.where(upper_half, other_keys, rep_keys)
            high_keys = jnp.where(upper_half, rep_keys, other_keys)
            low_values = jnp.where(upper_half, other_values, rep_values)
            high_values = jnp.where(upper_half, rep_values, other_values)
            rep_keys = jnp.concatenate([pair_mean(low_keys), pair_mean(high_keys)], 0)
            rep_values = jnp.concatenate([pair_mean(low_values), pair_mean(high_values)], 0)
    far_key_set = jnp.concatenate(far_keys, 0).reshape(-1, heads, HD)
    far_value_set = jnp.concatenate(far_values, 0).reshape(-1, heads, HD)
    far_lower = doc_lookup(jnp.concatenate(far_first, 0), doc_start)
    far_upper = doc_lookup(jnp.concatenate(far_last, 0), doc_start)
    far_allowed = (far_lower[None, :] == own_docs[:, None]) & (
        far_upper[None, :] == own_docs[:, None]
    )
    far_scores = (
        jnp.einsum("bqhd,khd->bhqk", query_blocks, far_key_set, preferred_element_type=jnp.float32)
        * scale
    )
    far_scores = jnp.where(far_allowed[:, None, None, :], far_scores, -jnp.inf)
    row_max = jnp.maximum(
        jnp.max(local_scores, axis=-1, keepdims=True), jnp.max(far_scores, axis=-1, keepdims=True)
    )
    local_raised = jnp.exp(local_scores - row_max)
    far_raised = jnp.exp(far_scores - row_max)
    total = jnp.sum(local_raised, axis=-1, keepdims=True) + jnp.sum(
        far_raised, axis=-1, keepdims=True
    )
    local_weights = (local_raised / total).astype(jnp.bfloat16)
    far_weights = (far_raised / total).astype(jnp.bfloat16)
    attended = jnp.einsum(
        "bhqk,bkhd->bqhd",
        local_weights,
        near_values.reshape(blocks, -1, heads, HD),
        preferred_element_type=jnp.float32,
    )
    attended = attended + jnp.einsum(
        "bhqk,khd->bqhd", far_weights, far_value_set, preferred_element_type=jnp.float32
    )
    attended = attended.reshape(length, width).astype(jnp.bfloat16)
    return jnp.dot(
        attended,
        lax.all_gather(out_weight, "ctx", axis=1, tiled=True),
        preferred_element_type=jnp.float32,
    ).astype(jnp.bfloat16)


def solution(mesh):
    fast = mesh.shape["groups"] == 2 and mesh.shape["ctx"] == 16
    placed = (
        P(("groups", "ctx"), None),
        P(("groups", "ctx"), None),
        P(("groups", "ctx"), None),
        P("groups"),
        P(None, "ctx"),
    )
    return jax.shard_map(
        per_device_fast if fast else per_device,
        mesh=mesh,
        in_specs=placed,
        out_specs=P(("groups", "ctx"), None),
        check_vma=False,
    )
```

```python
import functools

import jax
import jax.numpy as jnp
from jax import lax
from jax.experimental import pallas as pl
from jax.experimental.pallas import tpu as pltpu
from jax.sharding import PartitionSpec as P

HD = 128
BLOCK = 128

LOW, HIGH = 4, 8
LOG2_E = 1.4426950408889634
VMEM_LIMIT = 48 * 2**20


def swap(value, mask):
    pairs = [(source, source ^ mask) for source in range(lax.axis_size("ctx"))]
    return lax.ppermute(value, "ctx", pairs)


def swap_groups(value):
    return lax.ppermute(value, "groups", [(0, 1), (1, 0)])


def after(value, other):
    return lax.optimization_barrier((value, other))[0]


def vmem(count):
    return [pl.BlockSpec(memory_space=pltpu.VMEM)] * count


def anywhere(count):
    return [pl.BlockSpec(memory_space=pltpu.HBM)] * count


def loose(count):
    return [pl.BlockSpec(memory_space=pl.ANY)] * count


def call(kernel, outs, in_specs, out_specs=None, work=None, **more):
    return pl.pallas_call(
        kernel,
        out_shape=[jax.ShapeDtypeStruct(shape, jnp.bfloat16) for shape in outs],
        in_specs=[pl.BlockSpec(memory_space=pltpu.SMEM)] + in_specs,
        out_specs=vmem(len(outs)) if out_specs is None else out_specs,
        compiler_params=pltpu.CompilerParams(vmem_limit_bytes=VMEM_LIMIT),
        cost_estimate=None if work is None else pl.CostEstimate(flops=work, bytes_accessed=work // 50, transcendentals=0),
        **more,
    )


def halve(rows):
    count = rows.shape[0]
    row = lax.broadcasted_iota(jnp.int32, (count // 2, count), 0)
    column = lax.broadcasted_iota(jnp.int32, (count // 2, count), 1)
    pick = jnp.where(column // 2 == row, 0.5, 0.0).astype(jnp.bfloat16)
    return jnp.dot(pick, rows, preferred_element_type=jnp.float32).astype(jnp.bfloat16)


def columns_of(place, j, width):
    return pl.ds(pl.multiple_of(jnp.bitwise_xor(place, j) * width, width), width)


def run_copies(copies):
    for copy in copies:
        copy.start()
    for copy in copies:
        copy.wait()


def pack_kernel(places_of, place_ref, q_ref, k_ref, v_ref, other_ref, *refs):
    outs, sems = refs[:-1], refs[-1]
    copies = []
    if len(outs) > len(places_of):
        half = outs[0].shape[0]
        for n in range(2):
            rows = pl.ds(pl.multiple_of(place_ref[1] * half + n * (half // 2), half // 2), half // 2)
            to = outs[0].at[n * (half // 2) : (n + 1) * (half // 2), :]
            copies.append(pltpu.make_async_copy(other_ref.at[rows, :], to, sems.at[n]))
        outs = outs[1:]
    for j, out in zip(places_of, outs):
        columns = columns_of(place_ref[0], j, out.shape[1])
        for n, source in enumerate((q_ref, k_ref, v_ref)):
            to = out.at[n * BLOCK : (n + 1) * BLOCK, :]
            copies.append(pltpu.make_async_copy(source.at[:, columns], to, sems.at[len(copies)]))
    run_copies(copies)


def coarse_kernel(place_ref, a0, a1, a2, a3, third_ref, fourth_ref):
    del place_ref
    row = lax.broadcasted_iota(jnp.int32, (96, 256), 0)
    column = lax.broadcasted_iota(jnp.int32, (96, 256), 1)
    pick = jnp.where(
        row < 64,
        jnp.where(column // 4 == row, 0.25, 0.0),
        jnp.where(column // 8 == row - 64, 0.125, 0.0),
    ).astype(jnp.bfloat16)
    for j, source in enumerate((a0, a1, a2, a3)):
        means = jnp.dot(pick, source[BLOCK : 3 * BLOCK, :], preferred_element_type=jnp.float32).astype(jnp.bfloat16)
        for n in range(2):
            third_ref[n * 128 + 32 * j : n * 128 + 32 * j + 32, :] = means[32 * n : 32 * n + 32, :]
            fourth_ref[n * 64 + 16 * j : n * 64 + 16 * j + 16, :] = means[64 + 16 * n : 80 + 16 * n, :]


def attention_kernel(half, place_ref, doc_ref, *refs):
    a0, a1, a2, a3, l_ref, h_ref, lh_ref = refs[:7]
    out_ref, key_ref, value_ref = refs[-3:]
    own = (a0, a1, a2, a3)
    heads = out_ref.shape[1] // HD
    for n, rows_ref in enumerate((key_ref, value_ref)):
        at = 128 + 128 * n
        for part in range(2):
            rows_ref[128 * part : 128 * part + 128, :] = own[2 * half + part][at : at + 128, :]
            rows_ref[256 + 64 * part : 320 + 64 * part, :] = halve(own[2 - 2 * half + part][at : at + 128, :])
        rows_ref[384:512, :] = l_ref[128 * n : 128 * n + 128, :]
        rows_ref[512:576, :] = h_ref[64 * n : 64 * n + 64, :]
        rows_ref[576:640, :] = lh_ref[64 * n : 64 * n + 64, :]
    row = lax.broadcasted_iota(jnp.int32, (1, 640), 1)
    document = jnp.zeros((1, 640), jnp.int32)
    for first, mask in key_places(half):
        document = jnp.where(row >= first, doc_ref[jnp.bitwise_xor(place_ref[2], mask)], document)
    bias = [
        jnp.where(document == doc_ref[jnp.bitwise_xor(place_ref[2], 2 * half + part)], 0.0, -jnp.inf)
        for part in range(2)
    ]
    for head in range(heads):
        columns = slice(head * HD, (head + 1) * HD)
        for part in range(2):
            query = own[2 * half + part][0:128, columns]
            score = lax.dot_general(
                query, key_ref[:, columns], (((1,), (1,)), ((), ())), preferred_element_type=jnp.float32
            )
            score = score + bias[part]
            raised = jnp.exp2((score - jnp.max(score, axis=-1, keepdims=True)) * (HD ** (-0.5) * LOG2_E))
            mixed = jnp.dot(
                raised.astype(jnp.bfloat16), value_ref[:, columns], preferred_element_type=jnp.float32
            )
            mixed = mixed * (1.0 / jnp.sum(raised, axis=-1, keepdims=True))
            out_ref[128 * part : 128 * part + 128, columns] = mixed.astype(jnp.bfloat16)


def gather_kernel(place_ref, *refs):
    mixed, rows_ref = refs[:8], refs[8]
    share = mixed[0].shape[1]
    for j in range(4):
        columns = columns_of(place_ref[0], j, share)
        for r in range(4):
            piece = mixed[2 * j + ((r ^ j) >> 1)]
            at = ((r ^ j) & 1) * BLOCK
            rows_ref[r * BLOCK : (r + 1) * BLOCK, columns] = piece[at : at + BLOCK, :]


def project_kernel(place_ref, rows_ref, *refs):
    blocks, outs = list(refs[:-4]), refs[-4:]
    depth = rows_ref.shape[1]
    half = depth // 2
    group = place_ref[1]
    q = 0
    while blocks:
        block = blocks.pop(0)
        if block.shape[0] == depth:
            total = jnp.dot(rows_ref[...], block[...], preferred_element_type=jnp.float32)
        else:
            ours = rows_ref[:, pl.ds(pl.multiple_of(group * half, half), half)]
            theirs = rows_ref[:, pl.ds(pl.multiple_of((1 - group) * half, half), half)]
            total = jnp.dot(ours, block[...], preferred_element_type=jnp.float32)
            total += jnp.dot(theirs, blocks.pop(0)[...], preferred_element_type=jnp.float32)
        wide = block.shape[1]
        for r in range(4):
            outs[r][:, q * wide : (q + 1) * wide] = total[r * BLOCK : (r + 1) * BLOCK, :].astype(jnp.bfloat16)
        q += 1


def place_kernel(place_ref, *refs):
    sources, out_ref, sems = refs[:-2], refs[-2], refs[-1]
    wide = out_ref.shape[1] // 16
    copies = []
    for n, source in enumerate(sources):
        masks = ((0, HIGH), (LOW, LOW | HIGH))[n // 4]
        for q, mask in enumerate(masks):
            at = pl.multiple_of(jnp.bitwise_xor(place_ref[2], mask | n % 4) * wide, wide)
            copies.append(
                pltpu.make_async_copy(
                    source.at[:, q * wide : (q + 1) * wide], out_ref.at[:, pl.ds(at, wide)], sems.at[len(copies)]
                )
            )
    run_copies(copies)


def key_places(half):
    places = [(128 * part, 2 * half + part) for part in range(2)]
    places += [(256 + 64 * part, 2 - 2 * half + part) for part in range(2)]
    places += [(384 + 32 * j, j | LOW) for j in range(4)]
    places += [(512 + 16 * j, j | HIGH) for j in range(4)]
    places += [(576 + 16 * j, j | LOW | HIGH) for j in range(4)]
    return places


def per_device_fast(queries, keys, values, doc_start, out_weight):
    length, width = queries.shape
    share = width // 4
    depth, wide = out_weight.shape
    group = lax.axis_index("groups")
    position = lax.axis_index("ctx")
    places = jnp.stack([position & 3, group, position]).astype(jnp.int32)

    queries, keys, values, out_weight = (
        pltpu.with_memory_space_constraint(array, pltpu.HBM) for array in (queries, keys, values, out_weight)
    )
    ours, *across = call(
        functools.partial(pack_kernel, (2, 3)),
        [(depth // 2, wide)] + [(3 * length, share)] * 2,
        anywhere(4),
        scratch_shapes=[pltpu.SemaphoreType.DMA((8,))],
        name="pack0",
    )(places, queries, keys, values, out_weight)
    near = call(
        functools.partial(pack_kernel, (1, 0)),
        [(3 * length, share)] * 2,
        anywhere(3) + loose(1),
        scratch_shapes=[pltpu.SemaphoreType.DMA((6,))],
        work=2 * 10**9,
        name="pack1",
    )(places, queries, keys, values, across[0])
    own = [near[1], swap(near[0], 1), swap(across[0], 2), swap(across[1], 3)]
    half_h = swap(ours, HIGH)
    ours_l = swap(ours, LOW)
    third, fourth = call(
        coarse_kernel, [(2 * length, share), (length, share)], vmem(4), name="coarse"
    )(places, *own)
    third, fourth = after((third, fourth), (half_h, ours_l))
    far = [swap(third, LOW), swap(fourth, HIGH), swap(fourth, LOW | HIGH)]
    other_h = swap_groups(after(half_h, third))
    half_d = swap(after(half_h, far[0]), LOW)
    other_l = swap_groups(after(ours_l, other_h))
    other_d = swap_groups(after(half_d, other_l))

    pieces = [[None] * 2 for _ in range(4)]
    before = near[1]
    for n in range(2):
        (attended,) = call(
            functools.partial(attention_kernel, n),
            [(2 * length, share)],
            [pl.BlockSpec(memory_space=pltpu.SMEM)] + vmem(7) + loose(1),
            scratch_shapes=[pltpu.VMEM((640, share), jnp.bfloat16)] * 2,
            work=2 * 10**9,
            name="attend%d" % n,
        )(places, doc_start, *own, *far, before)
        before = attended
        pieces[0][n] = attended
        pieces[2][n] = swap(attended if n == 0 else after(attended, pieces[2][0]), 2)
    for n in range(2):
        pieces[1][n] = swap(after(pieces[0][n], (pieces[2][0], half_d)), 1)
        pieces[3][n] = swap(after(pieces[2][n], half_d), 1)
    mixed = [piece for pair in pieces for piece in pair]

    (rows,) = call(gather_kernel, [(4 * length, width)], vmem(8), name="gather")(places, *mixed)
    received = []
    for n, blocks in enumerate(((out_weight, half_h, other_h), (ours_l, other_l, half_d, other_d))):
        parts = call(project_kernel, [(length, 2 * wide)] * 4, vmem(1 + len(blocks)), name="project%d" % n)(
            places, rows, *blocks
        )
        received += [parts[0]] + [swap(parts[j], j) for j in (1, 2, 3)]
    (out,) = call(
        place_kernel,
        [(length, 16 * wide)],
        anywhere(8),
        anywhere(1),
        scratch_shapes=[pltpu.SemaphoreType.DMA((16,))],
        name="place",
    )(places, *received)
    return out


def partner(value, axis, apart):
    mask = 2**apart
    pairs = [(source, source ^ mask) for source in range(lax.axis_size(axis))]
    return lax.ppermute(value, axis, pairs)


def pair_mean(array):
    halves = array.reshape(array.shape[0] // 2, 2, array.shape[1]).astype(jnp.float32)
    return ((halves[:, 0] + halves[:, 1]) * 0.5).astype(jnp.bfloat16)


def doc_lookup(blocks, table):
    labels = jnp.arange(table.shape[0], dtype=jnp.int32)
    return jnp.sum(jnp.where(blocks[..., None] == labels, table, 0), axis=-1)


def covered(first_token, factor):
    return (first_token // BLOCK, (first_token + factor - 1) // BLOCK)


def trade(pair, bit):
    return partner((pair[0], pair[1]), "ctx", bit)


def per_device(queries, keys, values, doc_start, out_weight):
    length, width = queries.shape
    heads = width // HD
    blocks = length // BLOCK
    local_depth = blocks.bit_length() - 1
    devices = lax.axis_size("ctx")
    position = lax.axis_index("ctx")
    bit_count = devices.bit_length() - 1
    scale = HD ** (-0.5)
    offsets = jnp.arange(BLOCK, dtype=jnp.int32)
    block_ids = position * blocks + jnp.arange(blocks, dtype=jnp.int32)
    own_docs = doc_lookup(block_ids, doc_start)
    level_keys = [keys]
    level_values = [values]
    near_keys = keys.reshape(blocks, BLOCK, width)
    near_values = values.reshape(blocks, BLOCK, width)
    near_first = jnp.broadcast_to(block_ids[:, None], (blocks, BLOCK))
    near_last = jnp.broadcast_to(block_ids[:, None], (blocks, BLOCK))
    local_allowed = (doc_lookup(near_first, doc_start) == own_docs[:, None]) & (
        doc_lookup(near_last, doc_start) == own_docs[:, None]
    )
    query_blocks = queries.reshape(blocks, BLOCK, heads, HD)
    local_scores = (
        jnp.einsum(
            "bqhd,bkhd->bhqk",
            query_blocks,
            near_keys.reshape(blocks, -1, heads, HD),
            preferred_element_type=jnp.float32,
        )
        * scale
    )
    local_scores = jnp.where(local_allowed[:, None, None, :], local_scores, -jnp.inf)
    far_keys = []
    far_values = []
    far_first = []
    far_last = []

    def record(other_keys, other_values, bit):
        factor = 2 ** (local_depth + bit)
        sibling = jnp.bitwise_xor(position // 2**bit, 1)
        first_token = sibling * 2**bit * length + offsets * factor
        lower, upper = covered(first_token, factor)
        far_keys.append(other_keys)
        far_values.append(other_values)
        far_first.append(lower)
        far_last.append(upper)

    rep_keys = level_keys[local_depth]
    rep_values = level_values[local_depth]
    for bit in range(bit_count):
        other_keys, other_values = trade((rep_keys, rep_values), bit)
        record(other_keys, other_values, bit)
        if bit + 1 < bit_count:
            upper_half = position // 2**bit % 2 == 1
            low_keys = jnp.where(upper_half, other_keys, rep_keys)
            high_keys = jnp.where(upper_half, rep_keys, other_keys)
            low_values = jnp.where(upper_half, other_values, rep_values)
            high_values = jnp.where(upper_half, rep_values, other_values)
            rep_keys = jnp.concatenate([pair_mean(low_keys), pair_mean(high_keys)], 0)
            rep_values = jnp.concatenate([pair_mean(low_values), pair_mean(high_values)], 0)
    far_key_set = jnp.concatenate(far_keys, 0).reshape(-1, heads, HD)
    far_value_set = jnp.concatenate(far_values, 0).reshape(-1, heads, HD)
    far_lower = doc_lookup(jnp.concatenate(far_first, 0), doc_start)
    far_upper = doc_lookup(jnp.concatenate(far_last, 0), doc_start)
    far_allowed = (far_lower[None, :] == own_docs[:, None]) & (
        far_upper[None, :] == own_docs[:, None]
    )
    far_scores = (
        jnp.einsum("bqhd,khd->bhqk", query_blocks, far_key_set, preferred_element_type=jnp.float32)
        * scale
    )
    far_scores = jnp.where(far_allowed[:, None, None, :], far_scores, -jnp.inf)
    row_max = jnp.maximum(
        jnp.max(local_scores, axis=-1, keepdims=True), jnp.max(far_scores, axis=-1, keepdims=True)
    )
    local_raised = jnp.exp(local_scores - row_max)
    far_raised = jnp.exp(far_scores - row_max)
    total = jnp.sum(local_raised, axis=-1, keepdims=True) + jnp.sum(
        far_raised, axis=-1, keepdims=True
    )
    local_weights = (local_raised / total).astype(jnp.bfloat16)
    far_weights = (far_raised / total).astype(jnp.bfloat16)
    attended = jnp.einsum(
        "bhqk,bkhd->bqhd",
        local_weights,
        near_values.reshape(blocks, -1, heads, HD),
        preferred_element_type=jnp.float32,
    )
    attended = attended + jnp.einsum(
        "bhqk,khd->bqhd", far_weights, far_value_set, preferred_element_type=jnp.float32
    )
    attended = attended.reshape(length, width).astype(jnp.bfloat16)
    return jnp.dot(
        attended,
        lax.all_gather(out_weight, "ctx", axis=1, tiled=True),
        preferred_element_type=jnp.float32,
    ).astype(jnp.bfloat16)


def solution(mesh):
    fast = mesh.shape["groups"] == 2 and mesh.shape["ctx"] == 16
    placed = (
        P(("groups", "ctx"), None),
        P(("groups", "ctx"), None),
        P(("groups", "ctx"), None),
        P("groups"),
        P(None, "ctx"),
    )
    return jax.shard_map(
        per_device_fast if fast else per_device,
        mesh=mesh,
        in_specs=placed,
        out_specs=P(("groups", "ctx"), None),
        check_vma=False,
    )
```

```python
import functools

import jax
import jax.numpy as jnp
from jax import lax
from jax.experimental import pallas as pl
from jax.experimental.pallas import tpu as pltpu
from jax.sharding import PartitionSpec as P

HD = 128
BLOCK = 128

LOW, HIGH = 4, 8
LOG2_E = 1.4426950408889634
VMEM_LIMIT = 48 * 2**20


def swap(value, mask):
    pairs = [(source, source ^ mask) for source in range(lax.axis_size("ctx"))]
    return lax.ppermute(value, "ctx", pairs)


def swap_groups(value):
    return lax.ppermute(value, "groups", [(0, 1), (1, 0)])


def after(value, other):
    return lax.optimization_barrier((value, other))[0]


def vmem(count):
    return [pl.BlockSpec(memory_space=pltpu.VMEM)] * count


def anywhere(count):
    return [pl.BlockSpec(memory_space=pltpu.HBM)] * count


def loose(count):
    return [pl.BlockSpec(memory_space=pl.ANY)] * count


def call(kernel, outs, in_specs, out_specs=None, work=None, **more):
    return pl.pallas_call(
        kernel,
        out_shape=[jax.ShapeDtypeStruct(shape, jnp.bfloat16) for shape in outs],
        in_specs=[pl.BlockSpec(memory_space=pltpu.SMEM)] + in_specs,
        out_specs=vmem(len(outs)) if out_specs is None else out_specs,
        compiler_params=pltpu.CompilerParams(vmem_limit_bytes=VMEM_LIMIT),
        cost_estimate=None if work is None else pl.CostEstimate(flops=work, bytes_accessed=work // 50, transcendentals=0),
        **more,
    )


def halve(rows):
    count = rows.shape[0]
    row = lax.broadcasted_iota(jnp.int32, (count // 2, count), 0)
    column = lax.broadcasted_iota(jnp.int32, (count // 2, count), 1)
    pick = jnp.where(column // 2 == row, 0.5, 0.0).astype(jnp.bfloat16)
    return jnp.dot(pick, rows, preferred_element_type=jnp.float32).astype(jnp.bfloat16)


def columns_of(place, j, width):
    return pl.ds(pl.multiple_of(jnp.bitwise_xor(place, j) * width, width), width)


def run_copies(copies):
    for copy in copies:
        copy.start()
    for copy in copies:
        copy.wait()


def copies_for(place, j, sources, out, sems):
    columns = columns_of(place, j, out.shape[1])
    return [
        pltpu.make_async_copy(source.at[:, columns], out.at[n * BLOCK : (n + 1) * BLOCK, :], sems.at[3 * j + n])
        for n, source in enumerate(sources)
    ]


def pack_kernel(place_ref, q_ref, k_ref, v_ref, third_ref, fourth_ref, a2, a3, rows_ref, sems):
    loads = [
        pltpu.make_async_copy(source, rows_ref.at[n * BLOCK : (n + 1) * BLOCK, :], sems.at[n])
        for n, source in enumerate((k_ref, v_ref))
    ]
    copies = copies_for(place_ref[0], 2, (q_ref, k_ref, v_ref), a2, sems)
    copies += copies_for(place_ref[0], 3, (q_ref, k_ref, v_ref), a3, sems)
    for copy in loads + copies:
        copy.start()
    row = lax.broadcasted_iota(jnp.int32, (96, 256), 0)
    column = lax.broadcasted_iota(jnp.int32, (96, 256), 1)
    pick = jnp.where(
        row < 64,
        jnp.where(column // 4 == row, 0.25, 0.0),
        jnp.where(column // 8 == row - 64, 0.125, 0.0),
    ).astype(jnp.bfloat16)
    for load in loads:
        load.wait()
    means = jnp.dot(pick, rows_ref[...], preferred_element_type=jnp.float32).astype(jnp.bfloat16)
    third_ref[...] = means[0:64, :]
    fourth_ref[...] = means[64:96, :]
    for copy in copies:
        copy.wait()


def pack_rest_kernel(place_ref, q_ref, k_ref, v_ref, weight_ref, before_ref, a0, a1, ours_ref, theirs_ref, sems):
    del before_ref
    copies = copies_for(place_ref[0], 1, (q_ref, k_ref, v_ref), a1, sems)
    copies += copies_for(place_ref[0], 0, (q_ref, k_ref, v_ref), a0, sems)
    half = ours_ref.shape[0]
    for n, out in enumerate((ours_ref, theirs_ref)):
        rows = pl.ds(pl.multiple_of(jnp.bitwise_xor(place_ref[1], n) * half, half), half)
        copies.append(pltpu.make_async_copy(weight_ref.at[rows, :], out, sems.at[6 + n]))
    run_copies(copies)


def repack_kernel(place_ref, l_ref, h_ref, lh_ref, b0, b1, b2, b3):
    for j, out in enumerate((b0, b1, b2, b3)):
        columns = columns_of(place_ref[0], j, out.shape[1])
        out[0:64, :] = l_ref[:, columns]
        out[64:96, :] = h_ref[:, columns]
        out[96:128, :] = lh_ref[:, columns]


def attention_kernel(half, place_ref, doc_ref, *refs):
    a0, a1, a2, a3 = refs[:4]
    far = refs[4:8]
    out_ref, key_ref, value_ref = refs[-3:]
    own = (a0, a1, a2, a3)
    heads = out_ref.shape[1] // HD
    for n, rows_ref in enumerate((key_ref, value_ref)):
        at = 128 + 128 * n
        for part in range(2):
            rows_ref[128 * part : 128 * part + 128, :] = own[2 * half + part][at : at + 128, :]
            rows_ref[256 + 64 * part : 320 + 64 * part, :] = halve(own[2 - 2 * half + part][at : at + 128, :])
        for j in range(4):
            rows_ref[384 + 32 * j : 416 + 32 * j, :] = far[j][32 * n : 32 * n + 32, :]
            rows_ref[512 + 16 * j : 528 + 16 * j, :] = far[j][64 + 16 * n : 80 + 16 * n, :]
            rows_ref[576 + 16 * j : 592 + 16 * j, :] = far[j][96 + 16 * n : 112 + 16 * n, :]
    row = lax.broadcasted_iota(jnp.int32, (1, 640), 1)
    document = jnp.zeros((1, 640), jnp.int32)
    for first, mask in key_places(half):
        document = jnp.where(row >= first, doc_ref[jnp.bitwise_xor(place_ref[2], mask)], document)
    bias = [
        jnp.where(document == doc_ref[jnp.bitwise_xor(place_ref[2], 2 * half + part)], 0.0, -jnp.inf)
        for part in range(2)
    ]
    for head in range(heads):
        columns = slice(head * HD, (head + 1) * HD)
        for part in range(2):
            query = own[2 * half + part][0:128, columns]
            score = lax.dot_general(
                query, key_ref[:, columns], (((1,), (1,)), ((), ())), preferred_element_type=jnp.float32
            )
            score = score + bias[part]
            raised = jnp.exp2((score - jnp.max(score, axis=-1, keepdims=True)) * (HD ** (-0.5) * LOG2_E))
            mixed = jnp.dot(
                raised.astype(jnp.bfloat16), value_ref[:, columns], preferred_element_type=jnp.float32
            )
            mixed = mixed * (1.0 / jnp.sum(raised, axis=-1, keepdims=True))
            out_ref[128 * part : 128 * part + 128, columns] = mixed.astype(jnp.bfloat16)


def gather_kernel(place_ref, *refs):
    mixed, rows_ref = refs[:8], refs[8]
    share = mixed[0].shape[1]
    for j in range(4):
        columns = columns_of(place_ref[0], j, share)
        for r in range(4):
            piece = mixed[2 * j + ((r ^ j) >> 1)]
            at = ((r ^ j) & 1) * BLOCK
            rows_ref[r * BLOCK : (r + 1) * BLOCK, columns] = piece[at : at + BLOCK, :]


def project_kernel(place_ref, rows_ref, *refs):
    blocks, outs = list(refs[:-4]), refs[-4:]
    depth = rows_ref.shape[1]
    half = depth // 2
    group = place_ref[1]
    q = 0
    while blocks:
        block = blocks.pop(0)
        if block.shape[0] == depth:
            total = jnp.dot(rows_ref[...], block[...], preferred_element_type=jnp.float32)
        else:
            ours = rows_ref[:, pl.ds(pl.multiple_of(group * half, half), half)]
            theirs = rows_ref[:, pl.ds(pl.multiple_of((1 - group) * half, half), half)]
            total = jnp.dot(ours, block[...], preferred_element_type=jnp.float32)
            total += jnp.dot(theirs, blocks.pop(0)[...], preferred_element_type=jnp.float32)
        wide = block.shape[1]
        for r in range(4):
            outs[r][:, q * wide : (q + 1) * wide] = total[r * BLOCK : (r + 1) * BLOCK, :].astype(jnp.bfloat16)
        q += 1


def place_kernel(place_ref, *refs):
    sources, out_ref, sems = refs[:-2], refs[-2], refs[-1]
    wide = out_ref.shape[1] // 16
    copies = []
    for n, source in enumerate(sources):
        masks = ((0, HIGH), (LOW, LOW | HIGH))[n // 4]
        for q, mask in enumerate(masks):
            at = pl.multiple_of(jnp.bitwise_xor(place_ref[2], mask | n % 4) * wide, wide)
            copies.append(
                pltpu.make_async_copy(
                    source.at[:, q * wide : (q + 1) * wide], out_ref.at[:, pl.ds(at, wide)], sems.at[len(copies)]
                )
            )
    run_copies(copies)


def key_places(half):
    places = [(128 * part, 2 * half + part) for part in range(2)]
    places += [(256 + 64 * part, 2 - 2 * half + part) for part in range(2)]
    places += [(384 + 32 * j, j | LOW) for j in range(4)]
    places += [(512 + 16 * j, j | HIGH) for j in range(4)]
    places += [(576 + 16 * j, j | LOW | HIGH) for j in range(4)]
    return places


def per_device_fast(queries, keys, values, doc_start, out_weight):
    length, width = queries.shape
    share = width // 4
    depth, wide = out_weight.shape
    group = lax.axis_index("groups")
    position = lax.axis_index("ctx")
    places = jnp.stack([position & 3, group, position]).astype(jnp.int32)

    queries, keys, values, out_weight = (
        pltpu.with_memory_space_constraint(array, pltpu.HBM) for array in (queries, keys, values, out_weight)
    )
    third, fourth, *across = call(
        pack_kernel,
        [(length // 2, width), (length // 4, width)] + [(3 * length, share)] * 2,
        anywhere(3),
        scratch_shapes=[pltpu.VMEM((2 * length, width), jnp.bfloat16), pltpu.SemaphoreType.DMA((12,))],
        name="pack",
    )(places, queries, keys, values)
    *near, ours, theirs = call(
        pack_rest_kernel,
        [(3 * length, share)] * 2 + [(depth // 2, wide)] * 2,
        anywhere(4) + loose(1),
        scratch_shapes=[pltpu.SemaphoreType.DMA((8,))],
        work=2 * 10**9,
        name="rest",
    )(places, queries, keys, values, out_weight, fourth)
    from_l, from_h, from_lh = swap(third, LOW), swap(fourth, HIGH), swap(fourth, LOW | HIGH)
    own = [near[0], swap(after(near[1], from_lh), 1), swap(across[0], 2), swap(across[1], 3)]
    half_h = swap(after(ours, from_h), HIGH)
    ours_l = swap(after(ours, (from_l, from_lh)), LOW)
    extra = call(repack_kernel, [(length, share)] * 4, vmem(3), name="repack")(places, from_l, from_h, from_lh)
    far = [
        extra[0],
        swap(after(extra[1], own[3]), 1),
        swap(after(extra[2], own[2]), 2),
        swap(after(extra[3], own[3]), 3),
    ]

    pieces = [[None] * 2 for _ in range(4)]
    before = near[0]
    for n in range(2):
        (attended,) = call(
            functools.partial(attention_kernel, n),
            [(2 * length, share)],
            [pl.BlockSpec(memory_space=pltpu.SMEM)] + vmem(8) + loose(1),
            scratch_shapes=[pltpu.VMEM((640, share), jnp.bfloat16)] * 2,
            work=10**6,
            name="attend%d" % n,
        )(places, doc_start, *own, *far, before)
        before = attended
        pieces[0][n] = attended
        pieces[2][n] = swap(attended if n == 0 else after(attended, pieces[2][0]), 2)
    half_h = after(half_h, pieces[0][0])
    other_h = swap_groups(half_h)
    half_d = swap(after(half_h, ours_l), LOW)
    other_d = swap_groups(after(half_d, other_h))
    theirs_l = swap(after(theirs, half_d), LOW)
    for n in range(2):
        pieces[1][n] = swap(after(pieces[0][n], pieces[2][0]), 1)
        pieces[3][n] = swap(pieces[2][n], 1)
    mixed = [piece for pair in pieces for piece in pair]

    (rows,) = call(gather_kernel, [(4 * length, width)], vmem(8), name="gather")(places, *mixed)
    received = []
    for n, blocks in enumerate(((out_weight, half_h, other_h), (ours_l, theirs_l, half_d, other_d))):
        parts = call(project_kernel, [(length, 2 * wide)] * 4, vmem(1 + len(blocks)), name="project%d" % n)(
            places, rows, *blocks
        )
        received += [parts[0]] + [swap(parts[j], j) for j in (1, 2, 3)]
    (out,) = call(
        place_kernel,
        [(length, 16 * wide)],
        anywhere(8),
        anywhere(1),
        scratch_shapes=[pltpu.SemaphoreType.DMA((16,))],
        name="place",
    )(places, *received)
    return out


def partner(value, axis, apart):
    mask = 2**apart
    pairs = [(source, source ^ mask) for source in range(lax.axis_size(axis))]
    return lax.ppermute(value, axis, pairs)


def pair_mean(array):
    halves = array.reshape(array.shape[0] // 2, 2, array.shape[1]).astype(jnp.float32)
    return ((halves[:, 0] + halves[:, 1]) * 0.5).astype(jnp.bfloat16)


def doc_lookup(blocks, table):
    labels = jnp.arange(table.shape[0], dtype=jnp.int32)
    return jnp.sum(jnp.where(blocks[..., None] == labels, table, 0), axis=-1)


def covered(first_token, factor):
    return (first_token // BLOCK, (first_token + factor - 1) // BLOCK)


def trade(pair, bit):
    return partner((pair[0], pair[1]), "ctx", bit)


def per_device(queries, keys, values, doc_start, out_weight):
    length, width = queries.shape
    heads = width // HD
    blocks = length // BLOCK
    local_depth = blocks.bit_length() - 1
    devices = lax.axis_size("ctx")
    position = lax.axis_index("ctx")
    bit_count = devices.bit_length() - 1
    scale = HD ** (-0.5)
    offsets = jnp.arange(BLOCK, dtype=jnp.int32)
    block_ids = position * blocks + jnp.arange(blocks, dtype=jnp.int32)
    own_docs = doc_lookup(block_ids, doc_start)
    level_keys = [keys]
    level_values = [values]
    near_keys = keys.reshape(blocks, BLOCK, width)
    near_values = values.reshape(blocks, BLOCK, width)
    near_first = jnp.broadcast_to(block_ids[:, None], (blocks, BLOCK))
    near_last = jnp.broadcast_to(block_ids[:, None], (blocks, BLOCK))
    local_allowed = (doc_lookup(near_first, doc_start) == own_docs[:, None]) & (
        doc_lookup(near_last, doc_start) == own_docs[:, None]
    )
    query_blocks = queries.reshape(blocks, BLOCK, heads, HD)
    local_scores = (
        jnp.einsum(
            "bqhd,bkhd->bhqk",
            query_blocks,
            near_keys.reshape(blocks, -1, heads, HD),
            preferred_element_type=jnp.float32,
        )
        * scale
    )
    local_scores = jnp.where(local_allowed[:, None, None, :], local_scores, -jnp.inf)
    far_keys = []
    far_values = []
    far_first = []
    far_last = []

    def record(other_keys, other_values, bit):
        factor = 2 ** (local_depth + bit)
        sibling = jnp.bitwise_xor(position // 2**bit, 1)
        first_token = sibling * 2**bit * length + offsets * factor
        lower, upper = covered(first_token, factor)
        far_keys.append(other_keys)
        far_values.append(other_values)
        far_first.append(lower)
        far_last.append(upper)

    rep_keys = level_keys[local_depth]
    rep_values = level_values[local_depth]
    for bit in range(bit_count):
        other_keys, other_values = trade((rep_keys, rep_values), bit)
        record(other_keys, other_values, bit)
        if bit + 1 < bit_count:
            upper_half = position // 2**bit % 2 == 1
            low_keys = jnp.where(upper_half, other_keys, rep_keys)
            high_keys = jnp.where(upper_half, rep_keys, other_keys)
            low_values = jnp.where(upper_half, other_values, rep_values)
            high_values = jnp.where(upper_half, rep_values, other_values)
            rep_keys = jnp.concatenate([pair_mean(low_keys), pair_mean(high_keys)], 0)
            rep_values = jnp.concatenate([pair_mean(low_values), pair_mean(high_values)], 0)
    far_key_set = jnp.concatenate(far_keys, 0).reshape(-1, heads, HD)
    far_value_set = jnp.concatenate(far_values, 0).reshape(-1, heads, HD)
    far_lower = doc_lookup(jnp.concatenate(far_first, 0), doc_start)
    far_upper = doc_lookup(jnp.concatenate(far_last, 0), doc_start)
    far_allowed = (far_lower[None, :] == own_docs[:, None]) & (
        far_upper[None, :] == own_docs[:, None]
    )
    far_scores = (
        jnp.einsum("bqhd,khd->bhqk", query_blocks, far_key_set, preferred_element_type=jnp.float32)
        * scale
    )
    far_scores = jnp.where(far_allowed[:, None, None, :], far_scores, -jnp.inf)
    row_max = jnp.maximum(
        jnp.max(local_scores, axis=-1, keepdims=True), jnp.max(far_scores, axis=-1, keepdims=True)
    )
    local_raised = jnp.exp(local_scores - row_max)
    far_raised = jnp.exp(far_scores - row_max)
    total = jnp.sum(local_raised, axis=-1, keepdims=True) + jnp.sum(
        far_raised, axis=-1, keepdims=True
    )
    local_weights = (local_raised / total).astype(jnp.bfloat16)
    far_weights = (far_raised / total).astype(jnp.bfloat16)
    attended = jnp.einsum(
        "bhqk,bkhd->bqhd",
        local_weights,
        near_values.reshape(blocks, -1, heads, HD),
        preferred_element_type=jnp.float32,
    )
    attended = attended + jnp.einsum(
        "bhqk,khd->bqhd", far_weights, far_value_set, preferred_element_type=jnp.float32
    )
    attended = attended.reshape(length, width).astype(jnp.bfloat16)
    return jnp.dot(
        attended,
        lax.all_gather(out_weight, "ctx", axis=1, tiled=True),
        preferred_element_type=jnp.float32,
    ).astype(jnp.bfloat16)


def solution(mesh):
    fast = mesh.shape["groups"] == 2 and mesh.shape["ctx"] == 16
    placed = (
        P(("groups", "ctx"), None),
        P(("groups", "ctx"), None),
        P(("groups", "ctx"), None),
        P("groups"),
        P(None, "ctx"),
    )
    return jax.shard_map(
        per_device_fast if fast else per_device,
        mesh=mesh,
        in_specs=placed,
        out_specs=P(("groups", "ctx"), None),
        check_vma=False,
    )
```

```python
import functools

import jax
import jax.numpy as jnp
from jax import lax
from jax.experimental import pallas as pl
from jax.experimental.pallas import tpu as pltpu
from jax.sharding import PartitionSpec as P

HD = 128
BLOCK = 128

LOW, HIGH = 4, 8
LOG2_E = 1.4426950408889634
VMEM_LIMIT = 48 * 2**20


def swap(value, mask):
    pairs = [(source, source ^ mask) for source in range(lax.axis_size("ctx"))]
    return lax.ppermute(value, "ctx", pairs)


def swap_groups(value):
    return lax.ppermute(value, "groups", [(0, 1), (1, 0)])


def after(value, other):
    return lax.optimization_barrier((value, other))[0]


def vmem(count):
    return [pl.BlockSpec(memory_space=pltpu.VMEM)] * count


def anywhere(count):
    return [pl.BlockSpec(memory_space=pltpu.HBM)] * count


def loose(count):
    return [pl.BlockSpec(memory_space=pl.ANY)] * count


def call(kernel, outs, in_specs, out_specs=None, work=None, **more):
    return pl.pallas_call(
        kernel,
        out_shape=[jax.ShapeDtypeStruct(shape, jnp.bfloat16) for shape in outs],
        in_specs=[pl.BlockSpec(memory_space=pltpu.SMEM)] + in_specs,
        out_specs=vmem(len(outs)) if out_specs is None else out_specs,
        compiler_params=pltpu.CompilerParams(vmem_limit_bytes=VMEM_LIMIT),
        cost_estimate=None if work is None else pl.CostEstimate(flops=work, bytes_accessed=work // 50, transcendentals=0),
        **more,
    )


def halve(rows):
    count = rows.shape[0]
    row = lax.broadcasted_iota(jnp.int32, (count // 2, count), 0)
    column = lax.broadcasted_iota(jnp.int32, (count // 2, count), 1)
    pick = jnp.where(column // 2 == row, 0.5, 0.0).astype(jnp.bfloat16)
    return jnp.dot(pick, rows, preferred_element_type=jnp.float32).astype(jnp.bfloat16)


def columns_of(place, j, width):
    return pl.ds(pl.multiple_of(jnp.bitwise_xor(place, j) * width, width), width)


def run_copies(copies):
    for copy in copies:
        copy.start()
    for copy in copies:
        copy.wait()


def pack_kernel(places_of, place_ref, q_ref, k_ref, v_ref, other_ref, *refs):
    outs, sems = refs[:-1], refs[-1]
    copies = []
    if len(outs) > len(places_of):
        half = outs[0].shape[0]
        for n in range(2):
            rows = pl.ds(pl.multiple_of(place_ref[1] * half + n * (half // 2), half // 2), half // 2)
            to = outs[0].at[n * (half // 2) : (n + 1) * (half // 2), :]
            copies.append(pltpu.make_async_copy(other_ref.at[rows, :], to, sems.at[n]))
        outs = outs[1:]
    for j, out in zip(places_of, outs):
        columns = columns_of(place_ref[0], j, out.shape[1])
        for n, source in enumerate((q_ref, k_ref, v_ref)):
            to = out.at[n * BLOCK : (n + 1) * BLOCK, :]
            copies.append(pltpu.make_async_copy(source.at[:, columns], to, sems.at[len(copies)]))
    run_copies(copies)


def coarse_kernel(place_ref, a0, a1, a2, a3, third_ref, fourth_ref):
    del place_ref
    row = lax.broadcasted_iota(jnp.int32, (96, 256), 0)
    column = lax.broadcasted_iota(jnp.int32, (96, 256), 1)
    pick = jnp.where(
        row < 64,
        jnp.where(column // 4 == row, 0.25, 0.0),
        jnp.where(column // 8 == row - 64, 0.125, 0.0),
    ).astype(jnp.bfloat16)
    for j, source in enumerate((a0, a1, a2, a3)):
        means = jnp.dot(pick, source[BLOCK : 3 * BLOCK, :], preferred_element_type=jnp.float32).astype(jnp.bfloat16)
        for n in range(2):
            third_ref[n * 128 + 32 * j : n * 128 + 32 * j + 32, :] = means[32 * n : 32 * n + 32, :]
            fourth_ref[n * 64 + 16 * j : n * 64 + 16 * j + 16, :] = means[64 + 16 * n : 80 + 16 * n, :]


def attention_kernel(half, place_ref, doc_ref, *refs):
    a0, a1, a2, a3, l_ref, h_ref, lh_ref = refs[:7]
    out_ref, key_ref, value_ref = refs[-3:]
    own = (a0, a1, a2, a3)
    heads = out_ref.shape[1] // HD
    for n, rows_ref in enumerate((key_ref, value_ref)):
        at = 128 + 128 * n
        for part in range(2):
            rows_ref[128 * part : 128 * part + 128, :] = own[2 * half + part][at : at + 128, :]
            rows_ref[256 + 64 * part : 320 + 64 * part, :] = halve(own[2 - 2 * half + part][at : at + 128, :])
        rows_ref[384:512, :] = l_ref[128 * n : 128 * n + 128, :]
        rows_ref[512:576, :] = h_ref[64 * n : 64 * n + 64, :]
        rows_ref[576:640, :] = lh_ref[64 * n : 64 * n + 64, :]
    row = lax.broadcasted_iota(jnp.int32, (1, 640), 1)
    document = jnp.zeros((1, 640), jnp.int32)
    for first, mask in key_places(half):
        document = jnp.where(row >= first, doc_ref[jnp.bitwise_xor(place_ref[2], mask)], document)
    bias = [
        jnp.where(document == doc_ref[jnp.bitwise_xor(place_ref[2], 2 * half + part)], 0.0, -jnp.inf)
        for part in range(2)
    ]
    for head in range(heads):
        columns = slice(head * HD, (head + 1) * HD)
        for part in range(2):
            query = own[2 * half + part][0:128, columns]
            score = lax.dot_general(
                query, key_ref[:, columns], (((1,), (1,)), ((), ())), preferred_element_type=jnp.float32
            )
            score = score + bias[part]
            raised = jnp.exp2((score - jnp.max(score, axis=-1, keepdims=True)) * (HD ** (-0.5) * LOG2_E))
            mixed = jnp.dot(
                raised.astype(jnp.bfloat16), value_ref[:, columns], preferred_element_type=jnp.float32
            )
            mixed = mixed * (1.0 / jnp.sum(raised, axis=-1, keepdims=True))
            out_ref[128 * part : 128 * part + 128, columns] = mixed.astype(jnp.bfloat16)


def gather_kernel(place_ref, *refs):
    mixed, rows_ref = refs[:8], refs[8]
    share = mixed[0].shape[1]
    for j in range(4):
        columns = columns_of(place_ref[0], j, share)
        for r in range(4):
            piece = mixed[2 * j + ((r ^ j) >> 1)]
            at = ((r ^ j) & 1) * BLOCK
            rows_ref[r * BLOCK : (r + 1) * BLOCK, columns] = piece[at : at + BLOCK, :]


def project_kernel(place_ref, rows_ref, *refs):
    blocks, outs = list(refs[:-4]), refs[-4:]
    depth = rows_ref.shape[1]
    half = depth // 2
    group = place_ref[1]
    q = 0
    while blocks:
        block = blocks.pop(0)
        if block.shape[0] == depth:
            total = jnp.dot(rows_ref[...], block[...], preferred_element_type=jnp.float32)
        else:
            ours = rows_ref[:, pl.ds(pl.multiple_of(group * half, half), half)]
            theirs = rows_ref[:, pl.ds(pl.multiple_of((1 - group) * half, half), half)]
            total = jnp.dot(ours, block[...], preferred_element_type=jnp.float32)
            total += jnp.dot(theirs, blocks.pop(0)[...], preferred_element_type=jnp.float32)
        wide = block.shape[1]
        for r in range(4):
            outs[r][:, q * wide : (q + 1) * wide] = total[r * BLOCK : (r + 1) * BLOCK, :].astype(jnp.bfloat16)
        q += 1


def place_kernel(place_ref, *refs):
    sources, out_ref, sems = refs[:-2], refs[-2], refs[-1]
    wide = out_ref.shape[1] // 16
    copies = []
    for n, source in enumerate(sources):
        masks = ((0, HIGH), (LOW, LOW | HIGH))[n // 4]
        for q, mask in enumerate(masks):
            at = pl.multiple_of(jnp.bitwise_xor(place_ref[2], mask | n % 4) * wide, wide)
            copies.append(
                pltpu.make_async_copy(
                    source.at[:, q * wide : (q + 1) * wide], out_ref.at[:, pl.ds(at, wide)], sems.at[len(copies)]
                )
            )
    run_copies(copies)


def key_places(half):
    places = [(128 * part, 2 * half + part) for part in range(2)]
    places += [(256 + 64 * part, 2 - 2 * half + part) for part in range(2)]
    places += [(384 + 32 * j, j | LOW) for j in range(4)]
    places += [(512 + 16 * j, j | HIGH) for j in range(4)]
    places += [(576 + 16 * j, j | LOW | HIGH) for j in range(4)]
    return places


def per_device_fast(queries, keys, values, doc_start, out_weight):
    length, width = queries.shape
    share = width // 4
    depth, wide = out_weight.shape
    group = lax.axis_index("groups")
    position = lax.axis_index("ctx")
    places = jnp.stack([position & 3, group, position]).astype(jnp.int32)

    queries, keys, values, out_weight = (
        pltpu.with_memory_space_constraint(array, pltpu.HBM) for array in (queries, keys, values, out_weight)
    )
    ours, *across = call(
        functools.partial(pack_kernel, (2, 3)),
        [(depth // 2, wide)] + [(3 * length, share)] * 2,
        anywhere(4),
        scratch_shapes=[pltpu.SemaphoreType.DMA((8,))],
        name="pack0",
    )(places, queries, keys, values, out_weight)
    near = call(
        functools.partial(pack_kernel, (1, 0)),
        [(3 * length, share)] * 2,
        anywhere(3) + loose(1),
        scratch_shapes=[pltpu.SemaphoreType.DMA((6,))],
        work=2 * 10**9,
        name="pack1",
    )(places, queries, keys, values, across[0])
    own = [near[1], swap(near[0], 1), swap(across[0], 2), swap(across[1], 3)]
    half_h = swap(ours, HIGH)
    ours_l = swap(ours, LOW)
    third, fourth = call(
        coarse_kernel, [(2 * length, share), (length, share)], vmem(4), name="coarse"
    )(places, *own)
    third, fourth = after((third, fourth), (half_h, ours_l))
    far = [swap(third, LOW), swap(fourth, HIGH), swap(fourth, LOW | HIGH)]
    other_h = swap_groups(after(half_h, third))
    half_d = swap(after(half_h, far[0]), LOW)
    other_l = swap_groups(after(ours_l, other_h))
    other_d = swap_groups(after(half_d, other_l))

    pieces = [[None] * 2 for _ in range(4)]
    before = near[1]
    for n in range(2):
        (attended,) = call(
            functools.partial(attention_kernel, n),
            [(2 * length, share)],
            [pl.BlockSpec(memory_space=pltpu.SMEM)] + vmem(7) + loose(1),
            scratch_shapes=[pltpu.VMEM((640, share), jnp.bfloat16)] * 2,
            work=2 * 10**9,
            name="attend%d" % n,
        )(places, doc_start, *own, *far, before)
        before = attended
        pieces[0][n] = attended
        pieces[2][n] = swap(attended, 2)
    for n in range(2):
        pieces[1][n] = swap(after(pieces[0][n], (pieces[2][0], half_d)), 1)
    pieces[3][0] = swap(after(pieces[2][0], half_d), 1)
    pieces[3][1] = swap(after(pieces[2][1], pieces[3][0]), 1)
    mixed = [piece for pair in pieces for piece in pair]

    (rows,) = call(gather_kernel, [(4 * length, width)], vmem(8), name="gather")(places, *mixed)
    received = []
    for n, blocks in enumerate(((out_weight, half_h, other_h), (ours_l, other_l, half_d, other_d))):
        parts = call(project_kernel, [(length, 2 * wide)] * 4, vmem(1 + len(blocks)), name="project%d" % n)(
            places, rows, *blocks
        )
        received += [parts[0]] + [swap(parts[j], j) for j in (1, 2, 3)]
    (out,) = call(
        place_kernel,
        [(length, 16 * wide)],
        anywhere(8),
        anywhere(1),
        scratch_shapes=[pltpu.SemaphoreType.DMA((16,))],
        name="place",
    )(places, *received)
    return out


def partner(value, axis, apart):
    mask = 2**apart
    pairs = [(source, source ^ mask) for source in range(lax.axis_size(axis))]
    return lax.ppermute(value, axis, pairs)


def pair_mean(array):
    halves = array.reshape(array.shape[0] // 2, 2, array.shape[1]).astype(jnp.float32)
    return ((halves[:, 0] + halves[:, 1]) * 0.5).astype(jnp.bfloat16)


def doc_lookup(blocks, table):
    labels = jnp.arange(table.shape[0], dtype=jnp.int32)
    return jnp.sum(jnp.where(blocks[..., None] == labels, table, 0), axis=-1)


def covered(first_token, factor):
    return (first_token // BLOCK, (first_token + factor - 1) // BLOCK)


def trade(pair, bit):
    return partner((pair[0], pair[1]), "ctx", bit)


def per_device(queries, keys, values, doc_start, out_weight):
    length, width = queries.shape
    heads = width // HD
    blocks = length // BLOCK
    local_depth = blocks.bit_length() - 1
    devices = lax.axis_size("ctx")
    position = lax.axis_index("ctx")
    bit_count = devices.bit_length() - 1
    scale = HD ** (-0.5)
    offsets = jnp.arange(BLOCK, dtype=jnp.int32)
    block_ids = position * blocks + jnp.arange(blocks, dtype=jnp.int32)
    own_docs = doc_lookup(block_ids, doc_start)
    level_keys = [keys]
    level_values = [values]
    near_keys = keys.reshape(blocks, BLOCK, width)
    near_values = values.reshape(blocks, BLOCK, width)
    near_first = jnp.broadcast_to(block_ids[:, None], (blocks, BLOCK))
    near_last = jnp.broadcast_to(block_ids[:, None], (blocks, BLOCK))
    local_allowed = (doc_lookup(near_first, doc_start) == own_docs[:, None]) & (
        doc_lookup(near_last, doc_start) == own_docs[:, None]
    )
    query_blocks = queries.reshape(blocks, BLOCK, heads, HD)
    local_scores = (
        jnp.einsum(
            "bqhd,bkhd->bhqk",
            query_blocks,
            near_keys.reshape(blocks, -1, heads, HD),
            preferred_element_type=jnp.float32,
        )
        * scale
    )
    local_scores = jnp.where(local_allowed[:, None, None, :], local_scores, -jnp.inf)
    far_keys = []
    far_values = []
    far_first = []
    far_last = []

    def record(other_keys, other_values, bit):
        factor = 2 ** (local_depth + bit)
        sibling = jnp.bitwise_xor(position // 2**bit, 1)
        first_token = sibling * 2**bit * length + offsets * factor
        lower, upper = covered(first_token, factor)
        far_keys.append(other_keys)
        far_values.append(other_values)
        far_first.append(lower)
        far_last.append(upper)

    rep_keys = level_keys[local_depth]
    rep_values = level_values[local_depth]
    for bit in range(bit_count):
        other_keys, other_values = trade((rep_keys, rep_values), bit)
        record(other_keys, other_values, bit)
        if bit + 1 < bit_count:
            upper_half = position // 2**bit % 2 == 1
            low_keys = jnp.where(upper_half, other_keys, rep_keys)
            high_keys = jnp.where(upper_half, rep_keys, other_keys)
            low_values = jnp.where(upper_half, other_values, rep_values)
            high_values = jnp.where(upper_half, rep_values, other_values)
            rep_keys = jnp.concatenate([pair_mean(low_keys), pair_mean(high_keys)], 0)
            rep_values = jnp.concatenate([pair_mean(low_values), pair_mean(high_values)], 0)
    far_key_set = jnp.concatenate(far_keys, 0).reshape(-1, heads, HD)
    far_value_set = jnp.concatenate(far_values, 0).reshape(-1, heads, HD)
    far_lower = doc_lookup(jnp.concatenate(far_first, 0), doc_start)
    far_upper = doc_lookup(jnp.concatenate(far_last, 0), doc_start)
    far_allowed = (far_lower[None, :] == own_docs[:, None]) & (
        far_upper[None, :] == own_docs[:, None]
    )
    far_scores = (
        jnp.einsum("bqhd,khd->bhqk", query_blocks, far_key_set, preferred_element_type=jnp.float32)
        * scale
    )
    far_scores = jnp.where(far_allowed[:, None, None, :], far_scores, -jnp.inf)
    row_max = jnp.maximum(
        jnp.max(local_scores, axis=-1, keepdims=True), jnp.max(far_scores, axis=-1, keepdims=True)
    )
    local_raised = jnp.exp(local_scores - row_max)
    far_raised = jnp.exp(far_scores - row_max)
    total = jnp.sum(local_raised, axis=-1, keepdims=True) + jnp.sum(
        far_raised, axis=-1, keepdims=True
    )
    local_weights = (local_raised / total).astype(jnp.bfloat16)
    far_weights = (far_raised / total).astype(jnp.bfloat16)
    attended = jnp.einsum(
        "bhqk,bkhd->bqhd",
        local_weights,
        near_values.reshape(blocks, -1, heads, HD),
        preferred_element_type=jnp.float32,
    )
    attended = attended + jnp.einsum(
        "bhqk,khd->bqhd", far_weights, far_value_set, preferred_element_type=jnp.float32
    )
    attended = attended.reshape(length, width).astype(jnp.bfloat16)
    return jnp.dot(
        attended,
        lax.all_gather(out_weight, "ctx", axis=1, tiled=True),
        preferred_element_type=jnp.float32,
    ).astype(jnp.bfloat16)


def solution(mesh):
    fast = mesh.shape["groups"] == 2 and mesh.shape["ctx"] == 16
    placed = (
        P(("groups", "ctx"), None),
        P(("groups", "ctx"), None),
        P(("groups", "ctx"), None),
        P("groups"),
        P(None, "ctx"),
    )
    return jax.shard_map(
        per_device_fast if fast else per_device,
        mesh=mesh,
        in_specs=placed,
        out_specs=P(("groups", "ctx"), None),
        check_vma=False,
    )
```

```python
import functools

import jax
import jax.numpy as jnp
from jax import lax
from jax.experimental import pallas as pl
from jax.experimental.pallas import tpu as pltpu
from jax.sharding import PartitionSpec as P

HD = 128
BLOCK = 128

LOW, HIGH = 4, 8
LOG2_E = 1.4426950408889634
VMEM_LIMIT = 48 * 2**20


def swap(value, mask):
    pairs = [(source, source ^ mask) for source in range(lax.axis_size("ctx"))]
    return lax.ppermute(value, "ctx", pairs)


def swap_groups(value):
    return lax.ppermute(value, "groups", [(0, 1), (1, 0)])


def after(value, other):
    return lax.optimization_barrier((value, other))[0]


def vmem(count):
    return [pl.BlockSpec(memory_space=pltpu.VMEM)] * count


def anywhere(count):
    return [pl.BlockSpec(memory_space=pltpu.HBM)] * count


def loose(count):
    return [pl.BlockSpec(memory_space=pl.ANY)] * count


def call(kernel, outs, in_specs, out_specs=None, work=None, **more):
    return pl.pallas_call(
        kernel,
        out_shape=[jax.ShapeDtypeStruct(shape, jnp.bfloat16) for shape in outs],
        in_specs=[pl.BlockSpec(memory_space=pltpu.SMEM)] + in_specs,
        out_specs=vmem(len(outs)) if out_specs is None else out_specs,
        compiler_params=pltpu.CompilerParams(vmem_limit_bytes=VMEM_LIMIT),
        cost_estimate=None if work is None else pl.CostEstimate(flops=work, bytes_accessed=work // 50, transcendentals=0),
        **more,
    )


def halve(rows):
    count = rows.shape[0]
    row = lax.broadcasted_iota(jnp.int32, (count // 2, count), 0)
    column = lax.broadcasted_iota(jnp.int32, (count // 2, count), 1)
    pick = jnp.where(column // 2 == row, 0.5, 0.0).astype(jnp.bfloat16)
    return jnp.dot(pick, rows, preferred_element_type=jnp.float32).astype(jnp.bfloat16)


def columns_of(place, j, width):
    return pl.ds(pl.multiple_of(jnp.bitwise_xor(place, j) * width, width), width)


def run_copies(copies):
    for copy in copies:
        copy.start()
    for copy in copies:
        copy.wait()


def pack_kernel(places_of, place_ref, q_ref, k_ref, v_ref, other_ref, *refs):
    outs, sems = refs[:-1], refs[-1]
    copies = []
    if len(outs) > len(places_of):
        half = outs[0].shape[0]
        for n in range(2):
            rows = pl.ds(pl.multiple_of(place_ref[1] * half + n * (half // 2), half // 2), half // 2)
            to = outs[0].at[n * (half // 2) : (n + 1) * (half // 2), :]
            copies.append(pltpu.make_async_copy(other_ref.at[rows, :], to, sems.at[n]))
        outs = outs[1:]
    for j, out in zip(places_of, outs):
        columns = columns_of(place_ref[0], j, out.shape[1])
        for n, source in enumerate((q_ref, k_ref, v_ref)):
            to = out.at[n * BLOCK : (n + 1) * BLOCK, :]
            copies.append(pltpu.make_async_copy(source.at[:, columns], to, sems.at[len(copies)]))
    run_copies(copies)


def coarse_kernel(place_ref, a0, a1, a2, a3, third_ref, fourth_ref):
    del place_ref
    row = lax.broadcasted_iota(jnp.int32, (96, 256), 0)
    column = lax.broadcasted_iota(jnp.int32, (96, 256), 1)
    pick = jnp.where(
        row < 64,
        jnp.where(column // 4 == row, 0.25, 0.0),
        jnp.where(column // 8 == row - 64, 0.125, 0.0),
    ).astype(jnp.bfloat16)
    for j, source in enumerate((a0, a1, a2, a3)):
        means = jnp.dot(pick, source[BLOCK : 3 * BLOCK, :], preferred_element_type=jnp.float32).astype(jnp.bfloat16)
        for n in range(2):
            third_ref[n * 128 + 32 * j : n * 128 + 32 * j + 32, :] = means[32 * n : 32 * n + 32, :]
            fourth_ref[n * 64 + 16 * j : n * 64 + 16 * j + 16, :] = means[64 + 16 * n : 80 + 16 * n, :]


def attention_kernel(half, place_ref, doc_ref, *refs):
    a0, a1, a2, a3, l_ref, h_ref, lh_ref = refs[:7]
    out_ref, key_ref, value_ref = refs[-3:]
    own = (a0, a1, a2, a3)
    heads = out_ref.shape[1] // HD
    for n, rows_ref in enumerate((key_ref, value_ref)):
        at = 128 + 128 * n
        for part in range(2):
            rows_ref[128 * part : 128 * part + 128, :] = own[2 * half + part][at : at + 128, :]
            rows_ref[256 + 64 * part : 320 + 64 * part, :] = halve(own[2 - 2 * half + part][at : at + 128, :])
        rows_ref[384:512, :] = l_ref[128 * n : 128 * n + 128, :]
        rows_ref[512:576, :] = h_ref[64 * n : 64 * n + 64, :]
        rows_ref[576:640, :] = lh_ref[64 * n : 64 * n + 64, :]
    row = lax.broadcasted_iota(jnp.int32, (1, 640), 1)
    document = jnp.zeros((1, 640), jnp.int32)
    for first, mask in key_places(half):
        document = jnp.where(row >= first, doc_ref[jnp.bitwise_xor(place_ref[2], mask)], document)
    bias = [
        jnp.where(document == doc_ref[jnp.bitwise_xor(place_ref[2], 2 * half + part)], 0.0, -jnp.inf)
        for part in range(2)
    ]
    for head in range(heads):
        columns = slice(head * HD, (head + 1) * HD)
        query = jnp.concatenate([own[2 * half + part][0:128, columns] for part in range(2)], 0)
        score = lax.dot_general(
            query, key_ref[:, columns], (((1,), (1,)), ((), ())), preferred_element_type=jnp.float32
        )
        raised, inverse = [], []
        for part in range(2):
            biased = score[128 * part : 128 * part + 128, :] + bias[part]
            power = jnp.exp2((biased - jnp.max(biased, axis=-1, keepdims=True)) * (HD ** (-0.5) * LOG2_E))
            raised.append(power.astype(jnp.bfloat16))
            inverse.append(1.0 / jnp.sum(power, axis=-1, keepdims=True))
        mixed = jnp.dot(jnp.concatenate(raised, 0), value_ref[:, columns], preferred_element_type=jnp.float32)
        for part in range(2):
            run = slice(128 * part, 128 * part + 128)
            out_ref[run, columns] = (mixed[run, :] * inverse[part]).astype(jnp.bfloat16)


def gather_kernel(place_ref, *refs):
    mixed, rows_ref = refs[:8], refs[8]
    share = mixed[0].shape[1]
    for j in range(4):
        columns = columns_of(place_ref[0], j, share)
        for r in range(4):
            piece = mixed[2 * j + ((r ^ j) >> 1)]
            at = ((r ^ j) & 1) * BLOCK
            rows_ref[r * BLOCK : (r + 1) * BLOCK, columns] = piece[at : at + BLOCK, :]


def project_kernel(place_ref, rows_ref, *refs):
    blocks, outs = list(refs[:-4]), refs[-4:]
    depth = rows_ref.shape[1]
    half = depth // 2
    q = 0
    while blocks:
        total, done = None, 0
        wide = blocks[0].shape[1]
        while done < depth:
            block = blocks.pop(0)
            run = block.shape[0]
            if run == depth:
                rows = rows_ref[...]
            else:
                first = jnp.bitwise_xor(place_ref[1], done // half) * half + done % half
                rows = rows_ref[:, pl.ds(pl.multiple_of(first, HD), run)]
            product = jnp.dot(rows, block[...], preferred_element_type=jnp.float32)
            total = product if total is None else total + product
            done += run
        for r in range(4):
            outs[r][:, q * wide : (q + 1) * wide] = total[r * BLOCK : (r + 1) * BLOCK, :].astype(jnp.bfloat16)
        q += 1


def place_kernel(place_ref, *refs):
    sources, out_ref, sems = refs[:-2], refs[-2], refs[-1]
    wide = out_ref.shape[1] // 16
    copies = []
    for n, source in enumerate(sources):
        masks = ((0, HIGH), (LOW, LOW | HIGH))[n // 4]
        for q, mask in enumerate(masks):
            at = pl.multiple_of(jnp.bitwise_xor(place_ref[2], mask | n % 4) * wide, wide)
            copies.append(
                pltpu.make_async_copy(
                    source.at[:, q * wide : (q + 1) * wide], out_ref.at[:, pl.ds(at, wide)], sems.at[len(copies)]
                )
            )
    run_copies(copies)


def key_places(half):
    places = [(128 * part, 2 * half + part) for part in range(2)]
    places += [(256 + 64 * part, 2 - 2 * half + part) for part in range(2)]
    places += [(384 + 32 * j, j | LOW) for j in range(4)]
    places += [(512 + 16 * j, j | HIGH) for j in range(4)]
    places += [(576 + 16 * j, j | LOW | HIGH) for j in range(4)]
    return places


def per_device_fast(queries, keys, values, doc_start, out_weight):
    length, width = queries.shape
    share = width // 4
    depth, wide = out_weight.shape
    group = lax.axis_index("groups")
    position = lax.axis_index("ctx")
    places = jnp.stack([position & 3, group, position]).astype(jnp.int32)

    own_block = out_weight
    queries, keys, values, out_weight = (
        pltpu.with_memory_space_constraint(array, pltpu.HBM) for array in (queries, keys, values, out_weight)
    )
    (ours,) = call(
        functools.partial(pack_kernel, ()),
        [(depth // 2, wide)],
        anywhere(4),
        scratch_shapes=[pltpu.SemaphoreType.DMA((2,))],
        name="pack",
    )(places, queries, keys, values, out_weight)
    across = call(
        functools.partial(pack_kernel, (2, 3)),
        [(3 * length, share)] * 2,
        anywhere(3) + loose(1),
        scratch_shapes=[pltpu.SemaphoreType.DMA((6,))],
        name="pack0",
    )(places, queries, keys, values, ours)
    near = call(
        functools.partial(pack_kernel, (1, 0)),
        [(3 * length, share)] * 2,
        anywhere(3) + loose(1),
        scratch_shapes=[pltpu.SemaphoreType.DMA((6,))],
        work=2 * 10**9,
        name="pack1",
    )(places, queries, keys, values, across[0])
    own = [near[1], swap(near[0], 1), swap(across[0], 2), swap(across[1], 3)]
    half_h = swap(ours, HIGH)
    ours_l = swap(ours, LOW)
    third, fourth = call(
        coarse_kernel, [(2 * length, share), (length, share)], vmem(4), name="coarse"
    )(places, *own)
    third, fourth = after((third, fourth), (half_h, ours_l))
    far = [swap(third, LOW), swap(fourth, HIGH), swap(fourth, LOW | HIGH)]
    other_h = swap_groups(after(half_h, third))
    half_d = swap(after(half_h, far[0]), LOW)
    other_l = swap_groups(after(ours_l, other_h))
    quarter = depth // 4
    other_d = [swap_groups(after(half_d, other_l)[:quarter]), swap(after(other_h, half_d)[quarter:], LOW)]

    pieces = [[None] * 2 for _ in range(4)]
    before = near[1]
    for n in range(2):
        (attended,) = call(
            functools.partial(attention_kernel, n),
            [(2 * length, share)],
            [pl.BlockSpec(memory_space=pltpu.SMEM)] + vmem(7) + loose(1),
            scratch_shapes=[pltpu.VMEM((640, share), jnp.bfloat16)] * 2,
            work=2 * 10**9,
            name="attend%d" % n,
        )(places, doc_start, *own, *far, before)
        before = attended
        pieces[0][n] = attended
        pieces[2][n] = swap(attended, 2)
    for n in range(2):
        pieces[1][n] = swap(after(pieces[0][n], (pieces[2][0], half_d)), 1)
    pieces[3][0] = swap(after(pieces[2][0], half_d), 1)
    pieces[3][1] = swap(after(pieces[2][1], pieces[3][0]), 1)
    mixed = [piece for pair in pieces for piece in pair]

    (rows,) = call(gather_kernel, [(4 * length, width)], vmem(8), name="gather")(places, *mixed)
    received = []
    for n, blocks in enumerate(((own_block, half_h, other_h), (ours_l, other_l, half_d, *other_d))):
        parts = call(project_kernel, [(length, 2 * wide)] * 4, vmem(1 + len(blocks)), name="project%d" % n)(
            places, rows, *blocks
        )
        received += [parts[0]] + [swap(parts[j], j) for j in (1, 2, 3)]
    (out,) = call(
        place_kernel,
        [(length, 16 * wide)],
        anywhere(8),
        anywhere(1),
        scratch_shapes=[pltpu.SemaphoreType.DMA((16,))],
        name="place",
    )(places, *received)
    return out


def partner(value, axis, apart):
    mask = 2**apart
    pairs = [(source, source ^ mask) for source in range(lax.axis_size(axis))]
    return lax.ppermute(value, axis, pairs)


def pair_mean(array):
    halves = array.reshape(array.shape[0] // 2, 2, array.shape[1]).astype(jnp.float32)
    return ((halves[:, 0] + halves[:, 1]) * 0.5).astype(jnp.bfloat16)


def doc_lookup(blocks, table):
    labels = jnp.arange(table.shape[0], dtype=jnp.int32)
    return jnp.sum(jnp.where(blocks[..., None] == labels, table, 0), axis=-1)


def covered(first_token, factor):
    return (first_token // BLOCK, (first_token + factor - 1) // BLOCK)


def trade(pair, bit):
    return partner((pair[0], pair[1]), "ctx", bit)


def per_device(queries, keys, values, doc_start, out_weight):
    length, width = queries.shape
    heads = width // HD
    blocks = length // BLOCK
    local_depth = blocks.bit_length() - 1
    devices = lax.axis_size("ctx")
    position = lax.axis_index("ctx")
    bit_count = devices.bit_length() - 1
    scale = HD ** (-0.5)
    offsets = jnp.arange(BLOCK, dtype=jnp.int32)
    block_ids = position * blocks + jnp.arange(blocks, dtype=jnp.int32)
    own_docs = doc_lookup(block_ids, doc_start)
    level_keys = [keys]
    level_values = [values]
    near_keys = keys.reshape(blocks, BLOCK, width)
    near_values = values.reshape(blocks, BLOCK, width)
    near_first = jnp.broadcast_to(block_ids[:, None], (blocks, BLOCK))
    near_last = jnp.broadcast_to(block_ids[:, None], (blocks, BLOCK))
    local_allowed = (doc_lookup(near_first, doc_start) == own_docs[:, None]) & (
        doc_lookup(near_last, doc_start) == own_docs[:, None]
    )
    query_blocks = queries.reshape(blocks, BLOCK, heads, HD)
    local_scores = (
        jnp.einsum(
            "bqhd,bkhd->bhqk",
            query_blocks,
            near_keys.reshape(blocks, -1, heads, HD),
            preferred_element_type=jnp.float32,
        )
        * scale
    )
    local_scores = jnp.where(local_allowed[:, None, None, :], local_scores, -jnp.inf)
    far_keys = []
    far_values = []
    far_first = []
    far_last = []

    def record(other_keys, other_values, bit):
        factor = 2 ** (local_depth + bit)
        sibling = jnp.bitwise_xor(position // 2**bit, 1)
        first_token = sibling * 2**bit * length + offsets * factor
        lower, upper = covered(first_token, factor)
        far_keys.append(other_keys)
        far_values.append(other_values)
        far_first.append(lower)
        far_last.append(upper)

    rep_keys = level_keys[local_depth]
    rep_values = level_values[local_depth]
    for bit in range(bit_count):
        other_keys, other_values = trade((rep_keys, rep_values), bit)
        record(other_keys, other_values, bit)
        if bit + 1 < bit_count:
            upper_half = position // 2**bit % 2 == 1
            low_keys = jnp.where(upper_half, other_keys, rep_keys)
            high_keys = jnp.where(upper_half, rep_keys, other_keys)
            low_values = jnp.where(upper_half, other_values, rep_values)
            high_values = jnp.where(upper_half, rep_values, other_values)
            rep_keys = jnp.concatenate([pair_mean(low_keys), pair_mean(high_keys)], 0)
            rep_values = jnp.concatenate([pair_mean(low_values), pair_mean(high_values)], 0)
    far_key_set = jnp.concatenate(far_keys, 0).reshape(-1, heads, HD)
    far_value_set = jnp.concatenate(far_values, 0).reshape(-1, heads, HD)
    far_lower = doc_lookup(jnp.concatenate(far_first, 0), doc_start)
    far_upper = doc_lookup(jnp.concatenate(far_last, 0), doc_start)
    far_allowed = (far_lower[None, :] == own_docs[:, None]) & (
        far_upper[None, :] == own_docs[:, None]
    )
    far_scores = (
        jnp.einsum("bqhd,khd->bhqk", query_blocks, far_key_set, preferred_element_type=jnp.float32)
        * scale
    )
    far_scores = jnp.where(far_allowed[:, None, None, :], far_scores, -jnp.inf)
    row_max = jnp.maximum(
        jnp.max(local_scores, axis=-1, keepdims=True), jnp.max(far_scores, axis=-1, keepdims=True)
    )
    local_raised = jnp.exp(local_scores - row_max)
    far_raised = jnp.exp(far_scores - row_max)
    total = jnp.sum(local_raised, axis=-1, keepdims=True) + jnp.sum(
        far_raised, axis=-1, keepdims=True
    )
    local_weights = (local_raised / total).astype(jnp.bfloat16)
    far_weights = (far_raised / total).astype(jnp.bfloat16)
    attended = jnp.einsum(
        "bhqk,bkhd->bqhd",
        local_weights,
        near_values.reshape(blocks, -1, heads, HD),
        preferred_element_type=jnp.float32,
    )
    attended = attended + jnp.einsum(
        "bhqk,khd->bqhd", far_weights, far_value_set, preferred_element_type=jnp.float32
    )
    attended = attended.reshape(length, width).astype(jnp.bfloat16)
    return jnp.dot(
        attended,
        lax.all_gather(out_weight, "ctx", axis=1, tiled=True),
        preferred_element_type=jnp.float32,
    ).astype(jnp.bfloat16)


def solution(mesh):
    fast = mesh.shape["groups"] == 2 and mesh.shape["ctx"] == 16
    placed = (
        P(("groups", "ctx"), None),
        P(("groups", "ctx"), None),
        P(("groups", "ctx"), None),
        P("groups"),
        P(None, "ctx"),
    )
    return jax.shard_map(
        per_device_fast if fast else per_device,
        mesh=mesh,
        in_specs=placed,
        out_specs=P(("groups", "ctx"), None),
        check_vma=False,
    )
```

```python
import functools

import jax
import jax.numpy as jnp
from jax import lax
from jax.experimental import pallas as pl
from jax.experimental.pallas import tpu as pltpu
from jax.sharding import PartitionSpec as P

HD = 128
BLOCK = 128

LOW, HIGH = 4, 8
LOG2_E = 1.4426950408889634
VMEM_LIMIT = 48 * 2**20


def swap(value, mask):
    pairs = [(source, source ^ mask) for source in range(lax.axis_size("ctx"))]
    return lax.ppermute(value, "ctx", pairs)


def swap_groups(value):
    return lax.ppermute(value, "groups", [(0, 1), (1, 0)])


def after(value, other):
    return lax.optimization_barrier((value, other))[0]


def vmem(count):
    return [pl.BlockSpec(memory_space=pltpu.VMEM)] * count


def anywhere(count):
    return [pl.BlockSpec(memory_space=pltpu.HBM)] * count


def loose(count):
    return [pl.BlockSpec(memory_space=pl.ANY)] * count


def call(kernel, outs, in_specs, out_specs=None, work=None, **more):
    return pl.pallas_call(
        kernel,
        out_shape=[jax.ShapeDtypeStruct(shape, jnp.bfloat16) for shape in outs],
        in_specs=[pl.BlockSpec(memory_space=pltpu.SMEM)] + in_specs,
        out_specs=vmem(len(outs)) if out_specs is None else out_specs,
        compiler_params=pltpu.CompilerParams(vmem_limit_bytes=VMEM_LIMIT),
        cost_estimate=None if work is None else pl.CostEstimate(flops=work, bytes_accessed=work // 50, transcendentals=0),
        **more,
    )


def halve(rows):
    count = rows.shape[0]
    row = lax.broadcasted_iota(jnp.int32, (count // 2, count), 0)
    column = lax.broadcasted_iota(jnp.int32, (count // 2, count), 1)
    pick = jnp.where(column // 2 == row, 0.5, 0.0).astype(jnp.bfloat16)
    return jnp.dot(pick, rows, preferred_element_type=jnp.float32).astype(jnp.bfloat16)


def columns_of(place, j, width):
    return pl.ds(pl.multiple_of(jnp.bitwise_xor(place, j) * width, width), width)


def run_copies(copies):
    for copy in copies:
        copy.start()
    for copy in copies:
        copy.wait()


def pack_kernel(places_of, place_ref, q_ref, k_ref, v_ref, other_ref, *refs):
    outs, sems = refs[:-1], refs[-1]
    copies = []
    if len(outs) > len(places_of):
        half = outs[0].shape[0]
        for n in range(2):
            rows = pl.ds(pl.multiple_of(place_ref[1] * half + n * (half // 2), half // 2), half // 2)
            to = outs[0].at[n * (half // 2) : (n + 1) * (half // 2), :]
            copies.append(pltpu.make_async_copy(other_ref.at[rows, :], to, sems.at[n]))
        outs = outs[1:]
    for j, out in zip(places_of, outs):
        columns = columns_of(place_ref[0], j, out.shape[1])
        for n, source in enumerate((q_ref, k_ref, v_ref)):
            to = out.at[n * BLOCK : (n + 1) * BLOCK, :]
            copies.append(pltpu.make_async_copy(source.at[:, columns], to, sems.at[len(copies)]))
    run_copies(copies)


def coarse_kernel(place_ref, a0, a1, a2, a3, third_ref, fourth_ref):
    del place_ref
    row = lax.broadcasted_iota(jnp.int32, (96, 256), 0)
    column = lax.broadcasted_iota(jnp.int32, (96, 256), 1)
    pick = jnp.where(
        row < 64,
        jnp.where(column // 4 == row, 0.25, 0.0),
        jnp.where(column // 8 == row - 64, 0.125, 0.0),
    ).astype(jnp.bfloat16)
    for j, source in enumerate((a0, a1, a2, a3)):
        means = jnp.dot(pick, source[BLOCK : 3 * BLOCK, :], preferred_element_type=jnp.float32).astype(jnp.bfloat16)
        for n in range(2):
            third_ref[n * 128 + 32 * j : n * 128 + 32 * j + 32, :] = means[32 * n : 32 * n + 32, :]
            fourth_ref[n * 64 + 16 * j : n * 64 + 16 * j + 16, :] = means[64 + 16 * n : 80 + 16 * n, :]


def attention_kernel(half, place_ref, doc_ref, *refs):
    a0, a1, a2, a3, l_ref, h_ref, lh_ref = refs[:7]
    out_ref, key_ref, value_ref = refs[-3:]
    own = (a0, a1, a2, a3)
    heads = out_ref.shape[1] // HD
    for n, rows_ref in enumerate((key_ref, value_ref)):
        at = 128 + 128 * n
        for part in range(2):
            rows_ref[128 * part : 128 * part + 128, :] = own[2 * half + part][at : at + 128, :]
            rows_ref[256 + 64 * part : 320 + 64 * part, :] = halve(own[2 - 2 * half + part][at : at + 128, :])
        rows_ref[384:512, :] = l_ref[128 * n : 128 * n + 128, :]
        rows_ref[512:576, :] = h_ref[64 * n : 64 * n + 64, :]
        rows_ref[576:640, :] = lh_ref[64 * n : 64 * n + 64, :]
    row = lax.broadcasted_iota(jnp.int32, (1, 640), 1)
    document = jnp.zeros((1, 640), jnp.int32)
    for first, mask in key_places(half):
        document = jnp.where(row >= first, doc_ref[jnp.bitwise_xor(place_ref[2], mask)], document)
    bias = [
        jnp.where(document == doc_ref[jnp.bitwise_xor(place_ref[2], 2 * half + part)], 0.0, -jnp.inf)
        for part in range(2)
    ]
    for head in range(heads):
        columns = slice(head * HD, (head + 1) * HD)
        query = jnp.concatenate([own[2 * half + part][0:128, columns] for part in range(2)], 0)
        score = lax.dot_general(
            query, key_ref[:, columns], (((1,), (1,)), ((), ())), preferred_element_type=jnp.float32
        )
        raised, inverse = [], []
        for part in range(2):
            biased = score[128 * part : 128 * part + 128, :] + bias[part]
            power = jnp.exp2((biased - jnp.max(biased, axis=-1, keepdims=True)) * (HD ** (-0.5) * LOG2_E))
            raised.append(power.astype(jnp.bfloat16))
            inverse.append(1.0 / jnp.sum(power, axis=-1, keepdims=True))
        mixed = jnp.dot(jnp.concatenate(raised, 0), value_ref[:, columns], preferred_element_type=jnp.float32)
        for part in range(2):
            run = slice(128 * part, 128 * part + 128)
            out_ref[run, columns] = (mixed[run, :] * inverse[part]).astype(jnp.bfloat16)


def gather_kernel(place_ref, *refs):
    mixed, rows_ref = refs[:8], refs[8]
    share = mixed[0].shape[1]
    for j in range(4):
        columns = columns_of(place_ref[0], j, share)
        for r in range(4):
            piece = mixed[2 * j + ((r ^ j) >> 1)]
            at = ((r ^ j) & 1) * BLOCK
            rows_ref[r * BLOCK : (r + 1) * BLOCK, columns] = piece[at : at + BLOCK, :]


def project_kernel(place_ref, rows_ref, *refs):
    blocks, outs = list(refs[:-4]), refs[-4:]
    depth = rows_ref.shape[1]
    half = depth // 2
    q = 0
    while blocks:
        total, done = None, 0
        wide = blocks[0].shape[1]
        while done < depth:
            block = blocks.pop(0)
            run = block.shape[0]
            if run == depth:
                rows = rows_ref[...]
            else:
                first = jnp.bitwise_xor(place_ref[1], done // half) * half + done % half
                rows = rows_ref[:, pl.ds(pl.multiple_of(first, HD), run)]
            product = jnp.dot(rows, block[...], preferred_element_type=jnp.float32)
            total = product if total is None else total + product
            done += run
        for r in range(4):
            outs[r][:, q * wide : (q + 1) * wide] = total[r * BLOCK : (r + 1) * BLOCK, :].astype(jnp.bfloat16)
        q += 1


def place_kernel(group, place_ref, *refs):
    sources, out_ref, sems = refs[:4], refs[-2], refs[-1]
    wide = sources[0].shape[1] // 2
    copies = []
    for j, source in enumerate(sources):
        for q, mask in enumerate(((0, HIGH), (LOW, LOW | HIGH))[group]):
            at = pl.multiple_of(jnp.bitwise_xor(place_ref[2], mask | j) * wide, wide)
            to = out_ref.at[:, pl.ds(at, wide)]
            copies.append(pltpu.make_async_copy(source.at[:, q * wide : (q + 1) * wide], to, sems.at[2 * j + q]))
    run_copies(copies)


def key_places(half):
    places = [(128 * part, 2 * half + part) for part in range(2)]
    places += [(256 + 64 * part, 2 - 2 * half + part) for part in range(2)]
    places += [(384 + 32 * j, j | LOW) for j in range(4)]
    places += [(512 + 16 * j, j | HIGH) for j in range(4)]
    places += [(576 + 16 * j, j | LOW | HIGH) for j in range(4)]
    return places


def per_device_fast(queries, keys, values, doc_start, out_weight):
    length, width = queries.shape
    share = width // 4
    depth, wide = out_weight.shape
    group = lax.axis_index("groups")
    position = lax.axis_index("ctx")
    places = jnp.stack([position & 3, group, position]).astype(jnp.int32)

    own_block = out_weight
    queries, keys, values, out_weight = (
        pltpu.with_memory_space_constraint(array, pltpu.HBM) for array in (queries, keys, values, out_weight)
    )
    (ours,) = call(
        functools.partial(pack_kernel, ()),
        [(depth // 2, wide)],
        anywhere(4),
        scratch_shapes=[pltpu.SemaphoreType.DMA((2,))],
        name="pack",
    )(places, queries, keys, values, out_weight)
    across = call(
        functools.partial(pack_kernel, (2, 3)),
        [(3 * length, share)] * 2,
        anywhere(3) + loose(1),
        scratch_shapes=[pltpu.SemaphoreType.DMA((6,))],
        name="pack0",
    )(places, queries, keys, values, ours)
    near = call(
        functools.partial(pack_kernel, (1, 0)),
        [(3 * length, share)] * 2,
        anywhere(3) + loose(1),
        scratch_shapes=[pltpu.SemaphoreType.DMA((6,))],
        work=2 * 10**9,
        name="pack1",
    )(places, queries, keys, values, across[0])
    own = [near[1], swap(near[0], 1), swap(across[0], 2), swap(across[1], 3)]
    half_h = swap(ours, HIGH)
    ours_l = swap(ours, LOW)
    third, fourth = call(
        coarse_kernel, [(2 * length, share), (length, share)], vmem(4), name="coarse"
    )(places, *own)
    third, fourth = after((third, fourth), (half_h, ours_l))
    from_h, from_lh = swap(fourth, HIGH), swap(fourth, LOW | HIGH)
    far = [swap(third, LOW), from_h, from_lh]
    other_h = swap_groups(after(half_h, third))
    half_d = swap(after(half_h, far[1]), LOW)
    other_l = swap_groups(after(ours_l, other_h))
    quarter = depth // 4
    other_d = [swap_groups(after(half_d, other_l)[:quarter]), swap(after(other_h, half_d)[quarter:], LOW)]

    pieces = [[None] * 2 for _ in range(4)]
    before = near[1]
    for n in range(2):
        (attended,) = call(
            functools.partial(attention_kernel, n),
            [(2 * length, share)],
            [pl.BlockSpec(memory_space=pltpu.SMEM)] + vmem(7) + loose(1),
            scratch_shapes=[pltpu.VMEM((640, share), jnp.bfloat16)] * 2,
            work=2 * 10**9,
            name="attend%d" % n,
        )(places, doc_start, *own, *far, before)
        before = attended
        pieces[0][n] = attended
        pieces[2][n] = swap(attended, 2)
    for n in range(2):
        pieces[1][n] = swap(after(pieces[0][n], (pieces[2][0], half_d)), 1)
    pieces[3][0] = swap(after(pieces[2][0], half_d), 1)
    pieces[3][1] = swap(after(pieces[2][1], pieces[3][0]), 1)
    mixed = [piece for pair in pieces for piece in pair]

    (rows,) = call(gather_kernel, [(4 * length, width)], vmem(8), name="gather")(places, *mixed)
    received = []
    for n, blocks in enumerate(((own_block, half_h, other_h), (ours_l, other_l, half_d, *other_d))):
        parts = call(project_kernel, [(length, 2 * wide)] * 4, vmem(1 + len(blocks)), name="project%d" % n)(
            places, rows, *blocks
        )
        received += [parts[0]] + [swap(parts[j], j) for j in (1, 2, 3)]
    for n in range(2):
        earlier = [] if n == 0 else [out]
        (out,) = call(
            functools.partial(place_kernel, n),
            [(length, 16 * wide)],
            anywhere(4 + len(earlier)),
            anywhere(1),
            scratch_shapes=[pltpu.SemaphoreType.DMA((8,))],
            input_output_aliases={5: 0} if earlier else {},
            name="place%d" % n,
        )(places, *received[4 * n : 4 * n + 4], *earlier)
    return out


def partner(value, axis, apart):
    mask = 2**apart
    pairs = [(source, source ^ mask) for source in range(lax.axis_size(axis))]
    return lax.ppermute(value, axis, pairs)


def pair_mean(array):
    halves = array.reshape(array.shape[0] // 2, 2, array.shape[1]).astype(jnp.float32)
    return ((halves[:, 0] + halves[:, 1]) * 0.5).astype(jnp.bfloat16)


def doc_lookup(blocks, table):
    labels = jnp.arange(table.shape[0], dtype=jnp.int32)
    return jnp.sum(jnp.where(blocks[..., None] == labels, table, 0), axis=-1)


def covered(first_token, factor):
    return (first_token // BLOCK, (first_token + factor - 1) // BLOCK)


def trade(pair, bit):
    return partner((pair[0], pair[1]), "ctx", bit)


def per_device(queries, keys, values, doc_start, out_weight):
    length, width = queries.shape
    heads = width // HD
    blocks = length // BLOCK
    local_depth = blocks.bit_length() - 1
    devices = lax.axis_size("ctx")
    position = lax.axis_index("ctx")
    bit_count = devices.bit_length() - 1
    scale = HD ** (-0.5)
    offsets = jnp.arange(BLOCK, dtype=jnp.int32)
    block_ids = position * blocks + jnp.arange(blocks, dtype=jnp.int32)
    own_docs = doc_lookup(block_ids, doc_start)
    level_keys = [keys]
    level_values = [values]
    near_keys = keys.reshape(blocks, BLOCK, width)
    near_values = values.reshape(blocks, BLOCK, width)
    near_first = jnp.broadcast_to(block_ids[:, None], (blocks, BLOCK))
    near_last = jnp.broadcast_to(block_ids[:, None], (blocks, BLOCK))
    local_allowed = (doc_lookup(near_first, doc_start) == own_docs[:, None]) & (
        doc_lookup(near_last, doc_start) == own_docs[:, None]
    )
    query_blocks = queries.reshape(blocks, BLOCK, heads, HD)
    local_scores = (
        jnp.einsum(
            "bqhd,bkhd->bhqk",
            query_blocks,
            near_keys.reshape(blocks, -1, heads, HD),
            preferred_element_type=jnp.float32,
        )
        * scale
    )
    local_scores = jnp.where(local_allowed[:, None, None, :], local_scores, -jnp.inf)
    far_keys = []
    far_values = []
    far_first = []
    far_last = []

    def record(other_keys, other_values, bit):
        factor = 2 ** (local_depth + bit)
        sibling = jnp.bitwise_xor(position // 2**bit, 1)
        first_token = sibling * 2**bit * length + offsets * factor
        lower, upper = covered(first_token, factor)
        far_keys.append(other_keys)
        far_values.append(other_values)
        far_first.append(lower)
        far_last.append(upper)

    rep_keys = level_keys[local_depth]
    rep_values = level_values[local_depth]
    for bit in range(bit_count):
        other_keys, other_values = trade((rep_keys, rep_values), bit)
        record(other_keys, other_values, bit)
        if bit + 1 < bit_count:
            upper_half = position // 2**bit % 2 == 1
            low_keys = jnp.where(upper_half, other_keys, rep_keys)
            high_keys = jnp.where(upper_half, rep_keys, other_keys)
            low_values = jnp.where(upper_half, other_values, rep_values)
            high_values = jnp.where(upper_half, rep_values, other_values)
            rep_keys = jnp.concatenate([pair_mean(low_keys), pair_mean(high_keys)], 0)
            rep_values = jnp.concatenate([pair_mean(low_values), pair_mean(high_values)], 0)
    far_key_set = jnp.concatenate(far_keys, 0).reshape(-1, heads, HD)
    far_value_set = jnp.concatenate(far_values, 0).reshape(-1, heads, HD)
    far_lower = doc_lookup(jnp.concatenate(far_first, 0), doc_start)
    far_upper = doc_lookup(jnp.concatenate(far_last, 0), doc_start)
    far_allowed = (far_lower[None, :] == own_docs[:, None]) & (
        far_upper[None, :] == own_docs[:, None]
    )
    far_scores = (
        jnp.einsum("bqhd,khd->bhqk", query_blocks, far_key_set, preferred_element_type=jnp.float32)
        * scale
    )
    far_scores = jnp.where(far_allowed[:, None, None, :], far_scores, -jnp.inf)
    row_max = jnp.maximum(
        jnp.max(local_scores, axis=-1, keepdims=True), jnp.max(far_scores, axis=-1, keepdims=True)
    )
    local_raised = jnp.exp(local_scores - row_max)
    far_raised = jnp.exp(far_scores - row_max)
    total = jnp.sum(local_raised, axis=-1, keepdims=True) + jnp.sum(
        far_raised, axis=-1, keepdims=True
    )
    local_weights = (local_raised / total).astype(jnp.bfloat16)
    far_weights = (far_raised / total).astype(jnp.bfloat16)
    attended = jnp.einsum(
        "bhqk,bkhd->bqhd",
        local_weights,
        near_values.reshape(blocks, -1, heads, HD),
        preferred_element_type=jnp.float32,
    )
    attended = attended + jnp.einsum(
        "bhqk,khd->bqhd", far_weights, far_value_set, preferred_element_type=jnp.float32
    )
    attended = attended.reshape(length, width).astype(jnp.bfloat16)
    return jnp.dot(
        attended,
        lax.all_gather(out_weight, "ctx", axis=1, tiled=True),
        preferred_element_type=jnp.float32,
    ).astype(jnp.bfloat16)


def solution(mesh):
    fast = mesh.shape["groups"] == 2 and mesh.shape["ctx"] == 16
    placed = (
        P(("groups", "ctx"), None),
        P(("groups", "ctx"), None),
        P(("groups", "ctx"), None),
        P("groups"),
        P(None, "ctx"),
    )
    return jax.shard_map(
        per_device_fast if fast else per_device,
        mesh=mesh,
        in_specs=placed,
        out_specs=P(("groups", "ctx"), None),
        check_vma=False,
    )
```

```python
import functools

import jax
import jax.numpy as jnp
from jax import lax
from jax.experimental import pallas as pl
from jax.experimental.pallas import tpu as pltpu
from jax.sharding import PartitionSpec as P

HD = 128
BLOCK = 128

LOW, HIGH = 4, 8
LOG2_E = 1.4426950408889634
VMEM_LIMIT = 48 * 2**20


def swap(value, mask):
    pairs = [(source, source ^ mask) for source in range(lax.axis_size("ctx"))]
    return lax.ppermute(value, "ctx", pairs)


def swap_groups(value):
    return lax.ppermute(value, "groups", [(0, 1), (1, 0)])


def after(value, other):
    return lax.optimization_barrier((value, other))[0]


def vmem(count):
    return [pl.BlockSpec(memory_space=pltpu.VMEM)] * count


def anywhere(count):
    return [pl.BlockSpec(memory_space=pltpu.HBM)] * count


def loose(count):
    return [pl.BlockSpec(memory_space=pl.ANY)] * count


def call(kernel, outs, in_specs, out_specs=None, work=None, **more):
    return pl.pallas_call(
        kernel,
        out_shape=[jax.ShapeDtypeStruct(shape, jnp.bfloat16) for shape in outs],
        in_specs=[pl.BlockSpec(memory_space=pltpu.SMEM)] + in_specs,
        out_specs=vmem(len(outs)) if out_specs is None else out_specs,
        compiler_params=pltpu.CompilerParams(vmem_limit_bytes=VMEM_LIMIT),
        cost_estimate=None if work is None else pl.CostEstimate(flops=work, bytes_accessed=work // 50, transcendentals=0),
        **more,
    )


def halve(rows):
    count = rows.shape[0]
    row = lax.broadcasted_iota(jnp.int32, (count // 2, count), 0)
    column = lax.broadcasted_iota(jnp.int32, (count // 2, count), 1)
    pick = jnp.where(column // 2 == row, 0.5, 0.0).astype(jnp.bfloat16)
    return jnp.dot(pick, rows, preferred_element_type=jnp.float32).astype(jnp.bfloat16)


def columns_of(place, j, width):
    return pl.ds(pl.multiple_of(jnp.bitwise_xor(place, j) * width, width), width)


def run_copies(copies):
    for copy in copies:
        copy.start()
    for copy in copies:
        copy.wait()


def pack_kernel(places_of, place_ref, q_ref, k_ref, v_ref, other_ref, *refs):
    outs, sems = refs[:-1], refs[-1]
    copies = []
    if len(outs) > len(places_of):
        half = outs[0].shape[0]
        for n in range(2):
            rows = pl.ds(pl.multiple_of(place_ref[1] * half + n * (half // 2), half // 2), half // 2)
            to = outs[0].at[n * (half // 2) : (n + 1) * (half // 2), :]
            copies.append(pltpu.make_async_copy(other_ref.at[rows, :], to, sems.at[n]))
        outs = outs[1:]
    for j, out in zip(places_of, outs):
        columns = columns_of(place_ref[0], j, out.shape[1])
        for n, source in enumerate((q_ref, k_ref, v_ref)):
            to = out.at[n * BLOCK : (n + 1) * BLOCK, :]
            copies.append(pltpu.make_async_copy(source.at[:, columns], to, sems.at[len(copies)]))
    run_copies(copies)


def coarse_kernel(place_ref, a0, a1, a2, a3, third_ref, fourth_ref):
    del place_ref
    row = lax.broadcasted_iota(jnp.int32, (96, 256), 0)
    column = lax.broadcasted_iota(jnp.int32, (96, 256), 1)
    pick = jnp.where(
        row < 64,
        jnp.where(column // 4 == row, 0.25, 0.0),
        jnp.where(column // 8 == row - 64, 0.125, 0.0),
    ).astype(jnp.bfloat16)
    for j, source in enumerate((a0, a1, a2, a3)):
        means = jnp.dot(pick, source[BLOCK : 3 * BLOCK, :], preferred_element_type=jnp.float32).astype(jnp.bfloat16)
        for n in range(2):
            third_ref[n * 128 + 32 * j : n * 128 + 32 * j + 32, :] = means[32 * n : 32 * n + 32, :]
            fourth_ref[n * 64 + 16 * j : n * 64 + 16 * j + 16, :] = means[64 + 16 * n : 80 + 16 * n, :]


def attention_kernel(half, place_ref, doc_ref, *refs):
    a0, a1, a2, a3, l_ref, h_ref, lh_ref = refs[:7]
    out_ref, key_ref, value_ref = refs[-3:]
    own = (a0, a1, a2, a3)
    heads = out_ref.shape[1] // HD
    for n, rows_ref in enumerate((key_ref, value_ref)):
        at = 128 + 128 * n
        for part in range(2):
            rows_ref[128 * part : 128 * part + 128, :] = own[2 * half + part][at : at + 128, :]
            rows_ref[256 + 64 * part : 320 + 64 * part, :] = halve(own[2 - 2 * half + part][at : at + 128, :])
        rows_ref[384:512, :] = l_ref[128 * n : 128 * n + 128, :]
        rows_ref[512:576, :] = h_ref[64 * n : 64 * n + 64, :]
        rows_ref[576:640, :] = lh_ref[64 * n : 64 * n + 64, :]
    row = lax.broadcasted_iota(jnp.int32, (1, 640), 1)
    document = jnp.zeros((1, 640), jnp.int32)
    for first, mask in key_places(half):
        document = jnp.where(row >= first, doc_ref[jnp.bitwise_xor(place_ref[2], mask)], document)
    bias = [
        jnp.where(document == doc_ref[jnp.bitwise_xor(place_ref[2], 2 * half + part)], 0.0, -jnp.inf)
        for part in range(2)
    ]
    for head in range(heads):
        columns = slice(head * HD, (head + 1) * HD)
        query = jnp.concatenate([own[2 * half + part][0:128, columns] for part in range(2)], 0)
        score = lax.dot_general(
            query, key_ref[:, columns], (((1,), (1,)), ((), ())), preferred_element_type=jnp.float32
        )
        raised, inverse = [], []
        for part in range(2):
            biased = score[128 * part : 128 * part + 128, :] + bias[part]
            power = jnp.exp2((biased - jnp.max(biased, axis=-1, keepdims=True)) * (HD ** (-0.5) * LOG2_E))
            raised.append(power.astype(jnp.bfloat16))
            inverse.append(1.0 / jnp.sum(power, axis=-1, keepdims=True))
        mixed = jnp.dot(jnp.concatenate(raised, 0), value_ref[:, columns], preferred_element_type=jnp.float32)
        for part in range(2):
            run = slice(128 * part, 128 * part + 128)
            out_ref[run, columns] = (mixed[run, :] * inverse[part]).astype(jnp.bfloat16)


def gather_kernel(place_ref, *refs):
    mixed, rows_ref = refs[:8], refs[8]
    share = mixed[0].shape[1]
    for j in range(4):
        columns = columns_of(place_ref[0], j, share)
        for r in range(4):
            piece = mixed[2 * j + ((r ^ j) >> 1)]
            at = ((r ^ j) & 1) * BLOCK
            rows_ref[r * BLOCK : (r + 1) * BLOCK, columns] = piece[at : at + BLOCK, :]


def project_kernel(place_ref, rows_ref, *refs):
    blocks, outs = list(refs[:-4]), refs[-4:]
    depth = rows_ref.shape[1]
    half = depth // 2
    q = 0
    while blocks:
        total, done = None, 0
        wide = blocks[0].shape[1]
        while done < depth:
            block = blocks.pop(0)
            run = block.shape[0]
            if run == depth:
                rows = rows_ref[...]
            else:
                first = jnp.bitwise_xor(place_ref[1], done // half) * half + done % half
                rows = rows_ref[:, pl.ds(pl.multiple_of(first, HD), run)]
            product = jnp.dot(rows, block[...], preferred_element_type=jnp.float32)
            total = product if total is None else total + product
            done += run
        for r in range(4):
            outs[r][:, q * wide : (q + 1) * wide] = total[r * BLOCK : (r + 1) * BLOCK, :].astype(jnp.bfloat16)
        q += 1


def place_kernel(group, place_ref, *refs):
    sources, out_ref, sems = refs[:4], refs[-2], refs[-1]
    wide = out_ref.shape[1] // 16
    copies = []
    for j, source in enumerate(sources):
        for q, mask in enumerate(((0, HIGH, LOW), (LOW | HIGH,))[group]):
            at = pl.multiple_of(jnp.bitwise_xor(place_ref[2], mask | j) * wide, wide)
            to = out_ref.at[:, pl.ds(at, wide)]
            copies.append(pltpu.make_async_copy(source.at[:, q * wide : (q + 1) * wide], to, sems.at[len(copies)]))
    run_copies(copies)


def key_places(half):
    places = [(128 * part, 2 * half + part) for part in range(2)]
    places += [(256 + 64 * part, 2 - 2 * half + part) for part in range(2)]
    places += [(384 + 32 * j, j | LOW) for j in range(4)]
    places += [(512 + 16 * j, j | HIGH) for j in range(4)]
    places += [(576 + 16 * j, j | LOW | HIGH) for j in range(4)]
    return places


def per_device_fast(queries, keys, values, doc_start, out_weight):
    length, width = queries.shape
    share = width // 4
    depth, wide = out_weight.shape
    group = lax.axis_index("groups")
    position = lax.axis_index("ctx")
    places = jnp.stack([position & 3, group, position]).astype(jnp.int32)

    own_block = out_weight
    queries, keys, values, out_weight = (
        pltpu.with_memory_space_constraint(array, pltpu.HBM) for array in (queries, keys, values, out_weight)
    )
    (ours,) = call(
        functools.partial(pack_kernel, ()),
        [(depth // 2, wide)],
        anywhere(4),
        scratch_shapes=[pltpu.SemaphoreType.DMA((2,))],
        name="pack",
    )(places, queries, keys, values, out_weight)
    across = call(
        functools.partial(pack_kernel, (2, 3)),
        [(3 * length, share)] * 2,
        anywhere(3) + loose(1),
        scratch_shapes=[pltpu.SemaphoreType.DMA((6,))],
        name="pack0",
    )(places, queries, keys, values, ours)
    near = call(
        functools.partial(pack_kernel, (1, 0)),
        [(3 * length, share)] * 2,
        anywhere(3) + loose(1),
        scratch_shapes=[pltpu.SemaphoreType.DMA((6,))],
        work=2 * 10**9,
        name="pack1",
    )(places, queries, keys, values, across[0])
    own = [near[1], swap(near[0], 1), swap(across[0], 2), swap(across[1], 3)]
    half_h = swap(ours, HIGH)
    ours_l = swap(ours, LOW)
    third, fourth = call(
        coarse_kernel, [(2 * length, share), (length, share)], vmem(4), name="coarse"
    )(places, *own)
    third, fourth = after((third, fourth), (half_h, ours_l))
    from_h, from_lh = swap(fourth, HIGH), swap(fourth, LOW | HIGH)
    far = [swap(third, LOW), from_h, from_lh]
    other_h = swap_groups(after(half_h, third))
    half_d = swap(after(half_h, far[1]), LOW)
    other_l = swap_groups(after(ours_l, other_h))
    quarter = depth // 4
    other_d = [swap_groups(after(half_d, other_l)[:quarter]), swap(after(other_h, half_d)[quarter:], LOW)]

    pieces = [[None] * 2 for _ in range(4)]
    before = near[1]
    for n in range(2):
        (attended,) = call(
            functools.partial(attention_kernel, n),
            [(2 * length, share)],
            [pl.BlockSpec(memory_space=pltpu.SMEM)] + vmem(7) + loose(1),
            scratch_shapes=[pltpu.VMEM((640, share), jnp.bfloat16)] * 2,
            work=2 * 10**9,
            name="attend%d" % n,
        )(places, doc_start, *own, *far, before)
        before = attended
        pieces[0][n] = attended
        pieces[2][n] = swap(attended, 2)
    for n in range(2):
        pieces[1][n] = swap(after(pieces[0][n], (pieces[2][0], half_d)), 1)
    pieces[3][0] = swap(after(pieces[2][0], half_d), 1)
    pieces[3][1] = swap(after(pieces[2][1], pieces[3][0]), 1)
    mixed = [piece for pair in pieces for piece in pair]

    (rows,) = call(gather_kernel, [(4 * length, width)], vmem(8), name="gather")(places, *mixed)
    received = []
    for count, blocks in ((3, (own_block, half_h, other_h, ours_l, other_l)), (1, (half_d, *other_d))):
        parts = call(project_kernel, [(length, count * wide)] * 4, vmem(1 + len(blocks)), name="project%d" % count)(
            places, rows, *blocks
        )
        received += [parts[0]] + [swap(parts[j], j) for j in (1, 2, 3)]
    for n in range(2):
        earlier = [] if n == 0 else [out]
        (out,) = call(
            functools.partial(place_kernel, n),
            [(length, 16 * wide)],
            anywhere(4 + len(earlier)),
            anywhere(1),
            scratch_shapes=[pltpu.SemaphoreType.DMA((4 if earlier else 12,))],
            input_output_aliases={5: 0} if earlier else {},
            name="place%d" % n,
        )(places, *received[4 * n : 4 * n + 4], *earlier)
    return out


def partner(value, axis, apart):
    mask = 2**apart
    pairs = [(source, source ^ mask) for source in range(lax.axis_size(axis))]
    return lax.ppermute(value, axis, pairs)


def pair_mean(array):
    halves = array.reshape(array.shape[0] // 2, 2, array.shape[1]).astype(jnp.float32)
    return ((halves[:, 0] + halves[:, 1]) * 0.5).astype(jnp.bfloat16)


def doc_lookup(blocks, table):
    labels = jnp.arange(table.shape[0], dtype=jnp.int32)
    return jnp.sum(jnp.where(blocks[..., None] == labels, table, 0), axis=-1)


def covered(first_token, factor):
    return (first_token // BLOCK, (first_token + factor - 1) // BLOCK)


def trade(pair, bit):
    return partner((pair[0], pair[1]), "ctx", bit)


def per_device(queries, keys, values, doc_start, out_weight):
    length, width = queries.shape
    heads = width // HD
    blocks = length // BLOCK
    local_depth = blocks.bit_length() - 1
    devices = lax.axis_size("ctx")
    position = lax.axis_index("ctx")
    bit_count = devices.bit_length() - 1
    scale = HD ** (-0.5)
    offsets = jnp.arange(BLOCK, dtype=jnp.int32)
    block_ids = position * blocks + jnp.arange(blocks, dtype=jnp.int32)
    own_docs = doc_lookup(block_ids, doc_start)
    level_keys = [keys]
    level_values = [values]
    near_keys = keys.reshape(blocks, BLOCK, width)
    near_values = values.reshape(blocks, BLOCK, width)
    near_first = jnp.broadcast_to(block_ids[:, None], (blocks, BLOCK))
    near_last = jnp.broadcast_to(block_ids[:, None], (blocks, BLOCK))
    local_allowed = (doc_lookup(near_first, doc_start) == own_docs[:, None]) & (
        doc_lookup(near_last, doc_start) == own_docs[:, None]
    )
    query_blocks = queries.reshape(blocks, BLOCK, heads, HD)
    local_scores = (
        jnp.einsum(
            "bqhd,bkhd->bhqk",
            query_blocks,
            near_keys.reshape(blocks, -1, heads, HD),
            preferred_element_type=jnp.float32,
        )
        * scale
    )
    local_scores = jnp.where(local_allowed[:, None, None, :], local_scores, -jnp.inf)
    far_keys = []
    far_values = []
    far_first = []
    far_last = []

    def record(other_keys, other_values, bit):
        factor = 2 ** (local_depth + bit)
        sibling = jnp.bitwise_xor(position // 2**bit, 1)
        first_token = sibling * 2**bit * length + offsets * factor
        lower, upper = covered(first_token, factor)
        far_keys.append(other_keys)
        far_values.append(other_values)
        far_first.append(lower)
        far_last.append(upper)

    rep_keys = level_keys[local_depth]
    rep_values = level_values[local_depth]
    for bit in range(bit_count):
        other_keys, other_values = trade((rep_keys, rep_values), bit)
        record(other_keys, other_values, bit)
        if bit + 1 < bit_count:
            upper_half = position // 2**bit % 2 == 1
            low_keys = jnp.where(upper_half, other_keys, rep_keys)
            high_keys = jnp.where(upper_half, rep_keys, other_keys)
            low_values = jnp.where(upper_half, other_values, rep_values)
            high_values = jnp.where(upper_half, rep_values, other_values)
            rep_keys = jnp.concatenate([pair_mean(low_keys), pair_mean(high_keys)], 0)
            rep_values = jnp.concatenate([pair_mean(low_values), pair_mean(high_values)], 0)
    far_key_set = jnp.concatenate(far_keys, 0).reshape(-1, heads, HD)
    far_value_set = jnp.concatenate(far_values, 0).reshape(-1, heads, HD)
    far_lower = doc_lookup(jnp.concatenate(far_first, 0), doc_start)
    far_upper = doc_lookup(jnp.concatenate(far_last, 0), doc_start)
    far_allowed = (far_lower[None, :] == own_docs[:, None]) & (
        far_upper[None, :] == own_docs[:, None]
    )
    far_scores = (
        jnp.einsum("bqhd,khd->bhqk", query_blocks, far_key_set, preferred_element_type=jnp.float32)
        * scale
    )
    far_scores = jnp.where(far_allowed[:, None, None, :], far_scores, -jnp.inf)
    row_max = jnp.maximum(
        jnp.max(local_scores, axis=-1, keepdims=True), jnp.max(far_scores, axis=-1, keepdims=True)
    )
    local_raised = jnp.exp(local_scores - row_max)
    far_raised = jnp.exp(far_scores - row_max)
    total = jnp.sum(local_raised, axis=-1, keepdims=True) + jnp.sum(
        far_raised, axis=-1, keepdims=True
    )
    local_weights = (local_raised / total).astype(jnp.bfloat16)
    far_weights = (far_raised / total).astype(jnp.bfloat16)
    attended = jnp.einsum(
        "bhqk,bkhd->bqhd",
        local_weights,
        near_values.reshape(blocks, -1, heads, HD),
        preferred_element_type=jnp.float32,
    )
    attended = attended + jnp.einsum(
        "bhqk,khd->bqhd", far_weights, far_value_set, preferred_element_type=jnp.float32
    )
    attended = attended.reshape(length, width).astype(jnp.bfloat16)
    return jnp.dot(
        attended,
        lax.all_gather(out_weight, "ctx", axis=1, tiled=True),
        preferred_element_type=jnp.float32,
    ).astype(jnp.bfloat16)


def solution(mesh):
    fast = mesh.shape["groups"] == 2 and mesh.shape["ctx"] == 16
    placed = (
        P(("groups", "ctx"), None),
        P(("groups", "ctx"), None),
        P(("groups", "ctx"), None),
        P("groups"),
        P(None, "ctx"),
    )
    return jax.shard_map(
        per_device_fast if fast else per_device,
        mesh=mesh,
        in_specs=placed,
        out_specs=P(("groups", "ctx"), None),
        check_vma=False,
    )
```

```python
import functools

import jax
import jax.numpy as jnp
from jax import lax
from jax.experimental import pallas as pl
from jax.experimental.pallas import tpu as pltpu
from jax.sharding import PartitionSpec as P

HD = 128
BLOCK = 128

LOW, HIGH = 4, 8
LOG2_E = 1.4426950408889634
VMEM_LIMIT = 48 * 2**20


def swap(value, mask):
    pairs = [(source, source ^ mask) for source in range(lax.axis_size("ctx"))]
    return lax.ppermute(value, "ctx", pairs)


def swap_groups(value):
    return lax.ppermute(value, "groups", [(0, 1), (1, 0)])


def after(value, other):
    return lax.optimization_barrier((value, other))[0]


def vmem(count):
    return [pl.BlockSpec(memory_space=pltpu.VMEM)] * count


def anywhere(count):
    return [pl.BlockSpec(memory_space=pltpu.HBM)] * count


def loose(count):
    return [pl.BlockSpec(memory_space=pl.ANY)] * count


def call(kernel, outs, in_specs, out_specs=None, work=None, **more):
    return pl.pallas_call(
        kernel,
        out_shape=[jax.ShapeDtypeStruct(shape, jnp.bfloat16) for shape in outs],
        in_specs=[pl.BlockSpec(memory_space=pltpu.SMEM)] + in_specs,
        out_specs=vmem(len(outs)) if out_specs is None else out_specs,
        compiler_params=pltpu.CompilerParams(vmem_limit_bytes=VMEM_LIMIT),
        cost_estimate=None if work is None else pl.CostEstimate(flops=work, bytes_accessed=work // 50, transcendentals=0),
        **more,
    )


def halve(rows):
    count = rows.shape[0]
    row = lax.broadcasted_iota(jnp.int32, (count // 2, count), 0)
    column = lax.broadcasted_iota(jnp.int32, (count // 2, count), 1)
    pick = jnp.where(column // 2 == row, 0.5, 0.0).astype(jnp.bfloat16)
    return jnp.dot(pick, rows, preferred_element_type=jnp.float32).astype(jnp.bfloat16)


def columns_of(place, j, width):
    return pl.ds(pl.multiple_of(jnp.bitwise_xor(place, j) * width, width), width)


def run_copies(copies):
    for copy in copies:
        copy.start()
    for copy in copies:
        copy.wait()


def pack_kernel(places_of, place_ref, q_ref, k_ref, v_ref, other_ref, *refs):
    outs, sems = refs[:-1], refs[-1]
    copies = []
    if len(outs) > len(places_of):
        half = outs[0].shape[0]
        for n in range(2):
            rows = pl.ds(pl.multiple_of(place_ref[1] * half + n * (half // 2), half // 2), half // 2)
            to = outs[0].at[n * (half // 2) : (n + 1) * (half // 2), :]
            copies.append(pltpu.make_async_copy(other_ref.at[rows, :], to, sems.at[n]))
        outs = outs[1:]
    for j, out in zip(places_of, outs):
        columns = columns_of(place_ref[0], j, out.shape[1])
        for n, source in enumerate((q_ref, k_ref, v_ref)):
            to = out.at[n * BLOCK : (n + 1) * BLOCK, :]
            copies.append(pltpu.make_async_copy(source.at[:, columns], to, sems.at[len(copies)]))
    run_copies(copies)


def coarse_kernel(place_ref, a0, a1, a2, a3, third_ref, fourth_ref):
    del place_ref
    row = lax.broadcasted_iota(jnp.int32, (96, 256), 0)
    column = lax.broadcasted_iota(jnp.int32, (96, 256), 1)
    pick = jnp.where(
        row < 64,
        jnp.where(column // 4 == row, 0.25, 0.0),
        jnp.where(column // 8 == row - 64, 0.125, 0.0),
    ).astype(jnp.bfloat16)
    for j, source in enumerate((a0, a1, a2, a3)):
        means = jnp.dot(pick, source[BLOCK : 3 * BLOCK, :], preferred_element_type=jnp.float32).astype(jnp.bfloat16)
        for n in range(2):
            third_ref[n * 128 + 32 * j : n * 128 + 32 * j + 32, :] = means[32 * n : 32 * n + 32, :]
            fourth_ref[n * 64 + 16 * j : n * 64 + 16 * j + 16, :] = means[64 + 16 * n : 80 + 16 * n, :]


def attention_kernel(half, place_ref, doc_ref, *refs):
    a0, a1, a2, a3, l_ref, h_ref, lh_ref = refs[:7]
    out_ref, key_ref, value_ref = refs[-3:]
    own = (a0, a1, a2, a3)
    heads = out_ref.shape[1] // HD
    for n, rows_ref in enumerate((key_ref, value_ref)):
        at = 128 + 128 * n
        for part in range(2):
            rows_ref[128 * part : 128 * part + 128, :] = own[2 * half + part][at : at + 128, :]
            rows_ref[256 + 64 * part : 320 + 64 * part, :] = halve(own[2 - 2 * half + part][at : at + 128, :])
        rows_ref[384:512, :] = l_ref[128 * n : 128 * n + 128, :]
        rows_ref[512:576, :] = h_ref[64 * n : 64 * n + 64, :]
        rows_ref[576:640, :] = lh_ref[64 * n : 64 * n + 64, :]
    row = lax.broadcasted_iota(jnp.int32, (1, 640), 1)
    document = jnp.zeros((1, 640), jnp.int32)
    for first, mask in key_places(half):
        document = jnp.where(row >= first, doc_ref[jnp.bitwise_xor(place_ref[2], mask)], document)
    bias = [
        jnp.where(document == doc_ref[jnp.bitwise_xor(place_ref[2], 2 * half + part)], 0.0, -jnp.inf)
        for part in range(2)
    ]
    def score_of(head):
        columns = slice(head * HD, (head + 1) * HD)
        query = jnp.concatenate([own[2 * half + part][0:128, columns] for part in range(2)], 0)
        return lax.dot_general(
            query, key_ref[:, columns], (((1,), (1,)), ((), ())), preferred_element_type=jnp.float32
        )

    following = score_of(0)
    for head in range(heads):
        columns = slice(head * HD, (head + 1) * HD)
        score = following
        if head + 1 < heads:
            following = score_of(head + 1)
        raised, inverse = [], []
        for part in range(2):
            biased = score[128 * part : 128 * part + 128, :] + bias[part]
            power = jnp.exp2((biased - jnp.max(biased, axis=-1, keepdims=True)) * (HD ** (-0.5) * LOG2_E))
            raised.append(power.astype(jnp.bfloat16))
            inverse.append(1.0 / jnp.sum(power, axis=-1, keepdims=True))
        mixed = jnp.dot(jnp.concatenate(raised, 0), value_ref[:, columns], preferred_element_type=jnp.float32)
        for part in range(2):
            run = slice(128 * part, 128 * part + 128)
            out_ref[run, columns] = (mixed[run, :] * inverse[part]).astype(jnp.bfloat16)


def gather_kernel(place_ref, *refs):
    mixed, rows_ref = refs[:8], refs[8]
    share = mixed[0].shape[1]
    for j in range(4):
        columns = columns_of(place_ref[0], j, share)
        for r in range(4):
            piece = mixed[2 * j + ((r ^ j) >> 1)]
            at = ((r ^ j) & 1) * BLOCK
            rows_ref[r * BLOCK : (r + 1) * BLOCK, columns] = piece[at : at + BLOCK, :]


def project_kernel(place_ref, rows_ref, *refs):
    blocks, outs = list(refs[:-4]), refs[-4:]
    depth = rows_ref.shape[1]
    half = depth // 2
    q = 0
    while blocks:
        total, done = None, 0
        wide = blocks[0].shape[1]
        while done < depth:
            block = blocks.pop(0)
            run = block.shape[0]
            if run == depth:
                rows = rows_ref[...]
            else:
                first = jnp.bitwise_xor(place_ref[1], done // half) * half + done % half
                rows = rows_ref[:, pl.ds(pl.multiple_of(first, HD), run)]
            product = jnp.dot(rows, block[...], preferred_element_type=jnp.float32)
            total = product if total is None else total + product
            done += run
        for r in range(4):
            outs[r][:, q * wide : (q + 1) * wide] = total[r * BLOCK : (r + 1) * BLOCK, :].astype(jnp.bfloat16)
        q += 1


def place_kernel(group, place_ref, *refs):
    sources, out_ref, sems = refs[:4], refs[-2], refs[-1]
    wide = out_ref.shape[1] // 16
    copies = []
    for j, source in enumerate(sources):
        for q, mask in enumerate(((0, HIGH, LOW), (LOW | HIGH,))[group]):
            at = pl.multiple_of(jnp.bitwise_xor(place_ref[2], mask | j) * wide, wide)
            to = out_ref.at[:, pl.ds(at, wide)]
            copies.append(pltpu.make_async_copy(source.at[:, q * wide : (q + 1) * wide], to, sems.at[len(copies)]))
    run_copies(copies)


def key_places(half):
    places = [(128 * part, 2 * half + part) for part in range(2)]
    places += [(256 + 64 * part, 2 - 2 * half + part) for part in range(2)]
    places += [(384 + 32 * j, j | LOW) for j in range(4)]
    places += [(512 + 16 * j, j | HIGH) for j in range(4)]
    places += [(576 + 16 * j, j | LOW | HIGH) for j in range(4)]
    return places


def per_device_fast(queries, keys, values, doc_start, out_weight):
    length, width = queries.shape
    share = width // 4
    depth, wide = out_weight.shape
    group = lax.axis_index("groups")
    position = lax.axis_index("ctx")
    places = jnp.stack([position & 3, group, position]).astype(jnp.int32)

    own_block = out_weight
    queries, keys, values, out_weight = (
        pltpu.with_memory_space_constraint(array, pltpu.HBM) for array in (queries, keys, values, out_weight)
    )
    (ours,) = call(
        functools.partial(pack_kernel, ()),
        [(depth // 2, wide)],
        anywhere(4),
        scratch_shapes=[pltpu.SemaphoreType.DMA((2,))],
        name="pack",
    )(places, queries, keys, values, out_weight)
    across = call(
        functools.partial(pack_kernel, (2, 3)),
        [(3 * length, share)] * 2,
        anywhere(3) + loose(1),
        scratch_shapes=[pltpu.SemaphoreType.DMA((6,))],
        name="pack0",
    )(places, queries, keys, values, ours)
    near = call(
        functools.partial(pack_kernel, (1, 0)),
        [(3 * length, share)] * 2,
        anywhere(3) + loose(1),
        scratch_shapes=[pltpu.SemaphoreType.DMA((6,))],
        work=2 * 10**9,
        name="pack1",
    )(places, queries, keys, values, across[0])
    own = [near[1], swap(near[0], 1), swap(across[0], 2), swap(across[1], 3)]
    half_h = swap(ours, HIGH)
    ours_l = swap(ours, LOW)
    third, fourth = call(
        coarse_kernel, [(2 * length, share), (length, share)], vmem(4), name="coarse"
    )(places, *own)
    third, fourth = after((third, fourth), (half_h, ours_l))
    from_h, from_lh = swap(fourth, HIGH), swap(fourth, LOW | HIGH)
    far = [swap(third, LOW), from_h, from_lh]
    other_h = swap_groups(after(half_h, third))
    half_d = swap(after(half_h, far[1]), LOW)
    other_l = swap_groups(after(ours_l, other_h))
    quarter = depth // 4
    other_d = [swap_groups(after(half_d, other_l)[:quarter]), swap(after(other_h, half_d)[quarter:], LOW)]

    pieces = [[None] * 2 for _ in range(4)]
    before = near[1]
    for n in range(2):
        (attended,) = call(
            functools.partial(attention_kernel, n),
            [(2 * length, share)],
            [pl.BlockSpec(memory_space=pltpu.SMEM)] + vmem(7) + loose(1),
            scratch_shapes=[pltpu.VMEM((640, share), jnp.bfloat16)] * 2,
            work=2 * 10**9,
            name="attend%d" % n,
        )(places, doc_start, *own, *far, before)
        before = attended
        pieces[0][n] = attended
        pieces[2][n] = swap(attended, 2)
    for n in range(2):
        pieces[1][n] = swap(after(pieces[0][n], (pieces[2][0], half_d)), 1)
    pieces[3][0] = swap(after(pieces[2][0], half_d), 1)
    pieces[3][1] = swap(after(pieces[2][1], pieces[3][0]), 1)
    mixed = [piece for pair in pieces for piece in pair]

    (rows,) = call(gather_kernel, [(4 * length, width)], vmem(8), name="gather")(places, *mixed)
    received = []
    for count, blocks in ((3, (own_block, half_h, other_h, ours_l, other_l)), (1, (half_d, *other_d))):
        parts = call(project_kernel, [(length, count * wide)] * 4, vmem(1 + len(blocks)), name="project%d" % count)(
            places, rows, *blocks
        )
        received += [parts[0]] + [swap(parts[j], j) for j in (1, 2, 3)]
    for n in range(2):
        earlier = [] if n == 0 else [out]
        (out,) = call(
            functools.partial(place_kernel, n),
            [(length, 16 * wide)],
            anywhere(4 + len(earlier)),
            anywhere(1),
            scratch_shapes=[pltpu.SemaphoreType.DMA((4 if earlier else 12,))],
            input_output_aliases={5: 0} if earlier else {},
            name="place%d" % n,
        )(places, *received[4 * n : 4 * n + 4], *earlier)
    return out


def partner(value, axis, apart):
    mask = 2**apart
    pairs = [(source, source ^ mask) for source in range(lax.axis_size(axis))]
    return lax.ppermute(value, axis, pairs)


def pair_mean(array):
    halves = array.reshape(array.shape[0] // 2, 2, array.shape[1]).astype(jnp.float32)
    return ((halves[:, 0] + halves[:, 1]) * 0.5).astype(jnp.bfloat16)


def doc_lookup(blocks, table):
    labels = jnp.arange(table.shape[0], dtype=jnp.int32)
    return jnp.sum(jnp.where(blocks[..., None] == labels, table, 0), axis=-1)


def covered(first_token, factor):
    return (first_token // BLOCK, (first_token + factor - 1) // BLOCK)


def trade(pair, bit):
    return partner((pair[0], pair[1]), "ctx", bit)


def per_device(queries, keys, values, doc_start, out_weight):
    length, width = queries.shape
    heads = width // HD
    blocks = length // BLOCK
    local_depth = blocks.bit_length() - 1
    devices = lax.axis_size("ctx")
    position = lax.axis_index("ctx")
    bit_count = devices.bit_length() - 1
    scale = HD ** (-0.5)
    offsets = jnp.arange(BLOCK, dtype=jnp.int32)
    block_ids = position * blocks + jnp.arange(blocks, dtype=jnp.int32)
    own_docs = doc_lookup(block_ids, doc_start)
    level_keys = [keys]
    level_values = [values]
    near_keys = keys.reshape(blocks, BLOCK, width)
    near_values = values.reshape(blocks, BLOCK, width)
    near_first = jnp.broadcast_to(block_ids[:, None], (blocks, BLOCK))
    near_last = jnp.broadcast_to(block_ids[:, None], (blocks, BLOCK))
    local_allowed = (doc_lookup(near_first, doc_start) == own_docs[:, None]) & (
        doc_lookup(near_last, doc_start) == own_docs[:, None]
    )
    query_blocks = queries.reshape(blocks, BLOCK, heads, HD)
    local_scores = (
        jnp.einsum(
            "bqhd,bkhd->bhqk",
            query_blocks,
            near_keys.reshape(blocks, -1, heads, HD),
            preferred_element_type=jnp.float32,
        )
        * scale
    )
    local_scores = jnp.where(local_allowed[:, None, None, :], local_scores, -jnp.inf)
    far_keys = []
    far_values = []
    far_first = []
    far_last = []

    def record(other_keys, other_values, bit):
        factor = 2 ** (local_depth + bit)
        sibling = jnp.bitwise_xor(position // 2**bit, 1)
        first_token = sibling * 2**bit * length + offsets * factor
        lower, upper = covered(first_token, factor)
        far_keys.append(other_keys)
        far_values.append(other_values)
        far_first.append(lower)
        far_last.append(upper)

    rep_keys = level_keys[local_depth]
    rep_values = level_values[local_depth]
    for bit in range(bit_count):
        other_keys, other_values = trade((rep_keys, rep_values), bit)
        record(other_keys, other_values, bit)
        if bit + 1 < bit_count:
            upper_half = position // 2**bit % 2 == 1
            low_keys = jnp.where(upper_half, other_keys, rep_keys)
            high_keys = jnp.where(upper_half, rep_keys, other_keys)
            low_values = jnp.where(upper_half, other_values, rep_values)
            high_values = jnp.where(upper_half, rep_values, other_values)
            rep_keys = jnp.concatenate([pair_mean(low_keys), pair_mean(high_keys)], 0)
            rep_values = jnp.concatenate([pair_mean(low_values), pair_mean(high_values)], 0)
    far_key_set = jnp.concatenate(far_keys, 0).reshape(-1, heads, HD)
    far_value_set = jnp.concatenate(far_values, 0).reshape(-1, heads, HD)
    far_lower = doc_lookup(jnp.concatenate(far_first, 0), doc_start)
    far_upper = doc_lookup(jnp.concatenate(far_last, 0), doc_start)
    far_allowed = (far_lower[None, :] == own_docs[:, None]) & (
        far_upper[None, :] == own_docs[:, None]
    )
    far_scores = (
        jnp.einsum("bqhd,khd->bhqk", query_blocks, far_key_set, preferred_element_type=jnp.float32)
        * scale
    )
    far_scores = jnp.where(far_allowed[:, None, None, :], far_scores, -jnp.inf)
    row_max = jnp.maximum(
        jnp.max(local_scores, axis=-1, keepdims=True), jnp.max(far_scores, axis=-1, keepdims=True)
    )
    local_raised = jnp.exp(local_scores - row_max)
    far_raised = jnp.exp(far_scores - row_max)
    total = jnp.sum(local_raised, axis=-1, keepdims=True) + jnp.sum(
        far_raised, axis=-1, keepdims=True
    )
    local_weights = (local_raised / total).astype(jnp.bfloat16)
    far_weights = (far_raised / total).astype(jnp.bfloat16)
    attended = jnp.einsum(
        "bhqk,bkhd->bqhd",
        local_weights,
        near_values.reshape(blocks, -1, heads, HD),
        preferred_element_type=jnp.float32,
    )
    attended = attended + jnp.einsum(
        "bhqk,khd->bqhd", far_weights, far_value_set, preferred_element_type=jnp.float32
    )
    attended = attended.reshape(length, width).astype(jnp.bfloat16)
    return jnp.dot(
        attended,
        lax.all_gather(out_weight, "ctx", axis=1, tiled=True),
        preferred_element_type=jnp.float32,
    ).astype(jnp.bfloat16)


def solution(mesh):
    fast = mesh.shape["groups"] == 2 and mesh.shape["ctx"] == 16
    placed = (
        P(("groups", "ctx"), None),
        P(("groups", "ctx"), None),
        P(("groups", "ctx"), None),
        P("groups"),
        P(None, "ctx"),
    )
    return jax.shard_map(
        per_device_fast if fast else per_device,
        mesh=mesh,
        in_specs=placed,
        out_specs=P(("groups", "ctx"), None),
        check_vma=False,
    )
```

```python
import functools

import jax
import jax.numpy as jnp
from jax import lax
from jax.experimental import pallas as pl
from jax.experimental.pallas import tpu as pltpu
from jax.sharding import PartitionSpec as P

HD = 128
BLOCK = 128

LOW, HIGH = 4, 8
LOG2_E = 1.4426950408889634
VMEM_LIMIT = 48 * 2**20


def swap(value, mask):
    pairs = [(source, source ^ mask) for source in range(lax.axis_size("ctx"))]
    return lax.ppermute(value, "ctx", pairs)


def swap_groups(value):
    return lax.ppermute(value, "groups", [(0, 1), (1, 0)])


def after(value, other):
    return lax.optimization_barrier((value, other))[0]


def vmem(count):
    return [pl.BlockSpec(memory_space=pltpu.VMEM)] * count


def anywhere(count):
    return [pl.BlockSpec(memory_space=pltpu.HBM)] * count


def loose(count):
    return [pl.BlockSpec(memory_space=pl.ANY)] * count


def call(kernel, outs, in_specs, out_specs=None, work=None, **more):
    return pl.pallas_call(
        kernel,
        out_shape=[jax.ShapeDtypeStruct(shape, jnp.bfloat16) for shape in outs],
        in_specs=[pl.BlockSpec(memory_space=pltpu.SMEM)] + in_specs,
        out_specs=vmem(len(outs)) if out_specs is None else out_specs,
        compiler_params=pltpu.CompilerParams(vmem_limit_bytes=VMEM_LIMIT),
        cost_estimate=None if work is None else pl.CostEstimate(flops=work, bytes_accessed=work // 50, transcendentals=0),
        **more,
    )


def halve(rows):
    count = rows.shape[0]
    row = lax.broadcasted_iota(jnp.int32, (count // 2, count), 0)
    column = lax.broadcasted_iota(jnp.int32, (count // 2, count), 1)
    pick = jnp.where(column // 2 == row, 0.5, 0.0).astype(jnp.bfloat16)
    return jnp.dot(pick, rows, preferred_element_type=jnp.float32).astype(jnp.bfloat16)


def columns_of(place, j, width):
    return pl.ds(pl.multiple_of(jnp.bitwise_xor(place, j) * width, width), width)


def run_copies(copies):
    for copy in copies:
        copy.start()
    for copy in copies:
        copy.wait()


def pack_kernel(places_of, place_ref, q_ref, k_ref, v_ref, other_ref, *refs):
    outs, sems = refs[:-1], refs[-1]
    copies = []
    if len(outs) > len(places_of):
        half = outs[0].shape[0]
        for n in range(2):
            rows = pl.ds(pl.multiple_of(place_ref[1] * half + n * (half // 2), half // 2), half // 2)
            to = outs[0].at[n * (half // 2) : (n + 1) * (half // 2), :]
            copies.append(pltpu.make_async_copy(other_ref.at[rows, :], to, sems.at[n]))
        outs = outs[1:]
    for j, out in zip(places_of, outs):
        columns = columns_of(place_ref[0], j, out.shape[1])
        for n, source in enumerate((q_ref, k_ref, v_ref)):
            to = out.at[n * BLOCK : (n + 1) * BLOCK, :]
            copies.append(pltpu.make_async_copy(source.at[:, columns], to, sems.at[len(copies)]))
    run_copies(copies)


def coarse_kernel(place_ref, a0, a1, a2, a3, third_ref, fourth_ref):
    del place_ref
    row = lax.broadcasted_iota(jnp.int32, (96, 256), 0)
    column = lax.broadcasted_iota(jnp.int32, (96, 256), 1)
    pick = jnp.where(
        row < 64,
        jnp.where(column // 4 == row, 0.25, 0.0),
        jnp.where(column // 8 == row - 64, 0.125, 0.0),
    ).astype(jnp.bfloat16)
    for j, source in enumerate((a0, a1, a2, a3)):
        means = jnp.dot(pick, source[BLOCK : 3 * BLOCK, :], preferred_element_type=jnp.float32).astype(jnp.bfloat16)
        for n in range(2):
            third_ref[n * 128 + 32 * j : n * 128 + 32 * j + 32, :] = means[32 * n : 32 * n + 32, :]
            fourth_ref[n * 64 + 16 * j : n * 64 + 16 * j + 16, :] = means[64 + 16 * n : 80 + 16 * n, :]


def attention_kernel(half, place_ref, doc_ref, *refs):
    a0, a1, a2, a3, l_ref, h_ref, lh_ref = refs[:7]
    out_ref, key_ref, value_ref = refs[-3:]
    own = (a0, a1, a2, a3)
    heads = out_ref.shape[1] // HD
    for n, rows_ref in enumerate((key_ref, value_ref)):
        at = 128 + 128 * n
        for part in range(2):
            if n == 1:
                rows_ref[128 * part : 128 * part + 128, :] = own[2 * half + part][at : at + 128, :]
            rows_ref[256 + 64 * part : 320 + 64 * part, :] = halve(own[2 - 2 * half + part][at : at + 128, :])
        rows_ref[384:512, :] = l_ref[128 * n : 128 * n + 128, :]
        rows_ref[512:576, :] = h_ref[64 * n : 64 * n + 64, :]
        rows_ref[576:640, :] = lh_ref[64 * n : 64 * n + 64, :]
    row = lax.broadcasted_iota(jnp.int32, (1, 640), 1)
    document = jnp.zeros((1, 640), jnp.int32)
    for first, mask in key_places(half):
        document = jnp.where(row >= first, doc_ref[jnp.bitwise_xor(place_ref[2], mask)], document)
    bias = [
        jnp.where(document == doc_ref[jnp.bitwise_xor(place_ref[2], 2 * half + part)], 0.0, -jnp.inf)
        for part in range(2)
    ]
    def score_of(head):
        columns = slice(head * HD, (head + 1) * HD)
        query = jnp.concatenate([own[2 * half + part][0:128, columns] for part in range(2)], 0)
        runs = [own[2 * half + part][128:256, columns] for part in range(2)] + [key_ref[256:640, columns]]
        return jnp.concatenate(
            [
                lax.dot_general(query, run, (((1,), (1,)), ((), ())), preferred_element_type=jnp.float32)
                for run in runs
            ],
            1,
        )

    following = score_of(0)
    for head in range(heads):
        columns = slice(head * HD, (head + 1) * HD)
        score = following
        if head + 1 < heads:
            following = score_of(head + 1)
        raised, inverse = [], []
        for part in range(2):
            biased = score[128 * part : 128 * part + 128, :] + bias[part]
            power = jnp.exp2((biased - jnp.max(biased, axis=-1, keepdims=True)) * (HD ** (-0.5) * LOG2_E))
            raised.append(power.astype(jnp.bfloat16))
            inverse.append(1.0 / jnp.sum(power, axis=-1, keepdims=True))
        mixed = jnp.dot(jnp.concatenate(raised, 0), value_ref[:, columns], preferred_element_type=jnp.float32)
        for part in range(2):
            run = slice(128 * part, 128 * part + 128)
            out_ref[run, columns] = (mixed[run, :] * inverse[part]).astype(jnp.bfloat16)


def gather_kernel(place_ref, *refs):
    mixed, rows_ref = refs[:8], refs[8]
    share = mixed[0].shape[1]
    for j in range(4):
        columns = columns_of(place_ref[0], j, share)
        for r in range(4):
            piece = mixed[2 * j + ((r ^ j) >> 1)]
            at = ((r ^ j) & 1) * BLOCK
            rows_ref[r * BLOCK : (r + 1) * BLOCK, columns] = piece[at : at + BLOCK, :]


def project_kernel(place_ref, rows_ref, *refs):
    blocks, outs = list(refs[:-4]), refs[-4:]
    depth = rows_ref.shape[1]
    half = depth // 2
    q = 0
    while blocks:
        total, done = None, 0
        wide = blocks[0].shape[1]
        while done < depth:
            block = blocks.pop(0)
            run = block.shape[0]
            if run == depth:
                rows = rows_ref[...]
            else:
                first = jnp.bitwise_xor(place_ref[1], done // half) * half + done % half
                rows = rows_ref[:, pl.ds(pl.multiple_of(first, HD), run)]
            product = jnp.dot(rows, block[...], preferred_element_type=jnp.float32)
            total = product if total is None else total + product
            done += run
        for r in range(4):
            outs[r][:, q * wide : (q + 1) * wide] = total[r * BLOCK : (r + 1) * BLOCK, :].astype(jnp.bfloat16)
        q += 1


def place_kernel(group, place_ref, *refs):
    sources, out_ref, sems = refs[:4], refs[-2], refs[-1]
    wide = out_ref.shape[1] // 16
    copies = []
    for j, source in enumerate(sources):
        for q, mask in enumerate(((0, HIGH, LOW), (LOW | HIGH,))[group]):
            at = pl.multiple_of(jnp.bitwise_xor(place_ref[2], mask | j) * wide, wide)
            to = out_ref.at[:, pl.ds(at, wide)]
            copies.append(pltpu.make_async_copy(source.at[:, q * wide : (q + 1) * wide], to, sems.at[len(copies)]))
    run_copies(copies)


def key_places(half):
    places = [(128 * part, 2 * half + part) for part in range(2)]
    places += [(256 + 64 * part, 2 - 2 * half + part) for part in range(2)]
    places += [(384 + 32 * j, j | LOW) for j in range(4)]
    places += [(512 + 16 * j, j | HIGH) for j in range(4)]
    places += [(576 + 16 * j, j | LOW | HIGH) for j in range(4)]
    return places


def per_device_fast(queries, keys, values, doc_start, out_weight):
    length, width = queries.shape
    share = width // 4
    depth, wide = out_weight.shape
    group = lax.axis_index("groups")
    position = lax.axis_index("ctx")
    places = jnp.stack([position & 3, group, position]).astype(jnp.int32)

    own_block = out_weight
    queries, keys, values, out_weight = (
        pltpu.with_memory_space_constraint(array, pltpu.HBM) for array in (queries, keys, values, out_weight)
    )
    (ours,) = call(
        functools.partial(pack_kernel, ()),
        [(depth // 2, wide)],
        anywhere(4),
        scratch_shapes=[pltpu.SemaphoreType.DMA((2,))],
        name="pack",
    )(places, queries, keys, values, out_weight)
    across = call(
        functools.partial(pack_kernel, (2, 3)),
        [(3 * length, share)] * 2,
        anywhere(3) + loose(1),
        scratch_shapes=[pltpu.SemaphoreType.DMA((6,))],
        name="pack0",
    )(places, queries, keys, values, ours)
    near = call(
        functools.partial(pack_kernel, (1, 0)),
        [(3 * length, share)] * 2,
        anywhere(3) + loose(1),
        scratch_shapes=[pltpu.SemaphoreType.DMA((6,))],
        work=2 * 10**9,
        name="pack1",
    )(places, queries, keys, values, across[0])
    own = [near[1], swap(near[0], 1), swap(across[0], 2), swap(across[1], 3)]
    half_h = swap(ours, HIGH)
    ours_l = swap(ours, LOW)
    third, fourth = call(
        coarse_kernel, [(2 * length, share), (length, share)], vmem(4), name="coarse"
    )(places, *own)
    third, fourth = after((third, fourth), (half_h, ours_l))
    from_h, from_lh = swap(fourth, HIGH), swap(fourth, LOW | HIGH)
    far = [swap(third, LOW), from_h, from_lh]
    other_h = swap_groups(after(half_h, third))
    half_d = swap(after(half_h, far[1]), LOW)
    other_l = swap_groups(after(ours_l, other_h))
    quarter = depth // 4
    other_d = [swap_groups(after(half_d, other_l)[:quarter]), swap(other_h[quarter:], LOW)]

    pieces = [[None] * 2 for _ in range(4)]
    before = near[1]
    for n in range(2):
        (attended,) = call(
            functools.partial(attention_kernel, n),
            [(2 * length, share)],
            [pl.BlockSpec(memory_space=pltpu.SMEM)] + vmem(7) + loose(1),
            scratch_shapes=[pltpu.VMEM((640, share), jnp.bfloat16)] * 2,
            work=2 * 10**9,
            name="attend%d" % n,
        )(places, doc_start, *own, *far, before)
        before = attended
        pieces[0][n] = attended
        pieces[2][n] = swap(attended, 2)
    for n in range(2):
        pieces[1][n] = swap(after(pieces[0][n], (pieces[2][0], half_d)), 1)
    pieces[3][0] = swap(after(pieces[2][0], half_d), 1)
    pieces[3][1] = swap(after(pieces[2][1], pieces[3][0]), 1)
    mixed = [piece for pair in pieces for piece in pair]

    (rows,) = call(gather_kernel, [(4 * length, width)], vmem(8), name="gather")(places, *mixed)
    received = []
    for count, blocks in ((3, (own_block, half_h, other_h, ours_l, other_l)), (1, (half_d, *other_d))):
        parts = call(project_kernel, [(length, count * wide)] * 4, vmem(1 + len(blocks)), name="project%d" % count)(
            places, rows, *blocks
        )
        received += [parts[0]] + [swap(parts[j], j) for j in (1, 2, 3)]
    for n in range(2):
        earlier = [] if n == 0 else [out]
        (out,) = call(
            functools.partial(place_kernel, n),
            [(length, 16 * wide)],
            anywhere(4 + len(earlier)),
            anywhere(1),
            scratch_shapes=[pltpu.SemaphoreType.DMA((4 if earlier else 12,))],
            input_output_aliases={5: 0} if earlier else {},
            name="place%d" % n,
        )(places, *received[4 * n : 4 * n + 4], *earlier)
    return out


def partner(value, axis, apart):
    mask = 2**apart
    pairs = [(source, source ^ mask) for source in range(lax.axis_size(axis))]
    return lax.ppermute(value, axis, pairs)


def pair_mean(array):
    halves = array.reshape(array.shape[0] // 2, 2, array.shape[1]).astype(jnp.float32)
    return ((halves[:, 0] + halves[:, 1]) * 0.5).astype(jnp.bfloat16)


def doc_lookup(blocks, table):
    labels = jnp.arange(table.shape[0], dtype=jnp.int32)
    return jnp.sum(jnp.where(blocks[..., None] == labels, table, 0), axis=-1)


def covered(first_token, factor):
    return (first_token // BLOCK, (first_token + factor - 1) // BLOCK)


def trade(pair, bit):
    return partner((pair[0], pair[1]), "ctx", bit)


def per_device(queries, keys, values, doc_start, out_weight):
    length, width = queries.shape
    heads = width // HD
    blocks = length // BLOCK
    local_depth = blocks.bit_length() - 1
    devices = lax.axis_size("ctx")
    position = lax.axis_index("ctx")
    bit_count = devices.bit_length() - 1
    scale = HD ** (-0.5)
    offsets = jnp.arange(BLOCK, dtype=jnp.int32)
    block_ids = position * blocks + jnp.arange(blocks, dtype=jnp.int32)
    own_docs = doc_lookup(block_ids, doc_start)
    level_keys = [keys]
    level_values = [values]
    near_keys = keys.reshape(blocks, BLOCK, width)
    near_values = values.reshape(blocks, BLOCK, width)
    near_first = jnp.broadcast_to(block_ids[:, None], (blocks, BLOCK))
    near_last = jnp.broadcast_to(block_ids[:, None], (blocks, BLOCK))
    local_allowed = (doc_lookup(near_first, doc_start) == own_docs[:, None]) & (
        doc_lookup(near_last, doc_start) == own_docs[:, None]
    )
    query_blocks = queries.reshape(blocks, BLOCK, heads, HD)
    local_scores = (
        jnp.einsum(
            "bqhd,bkhd->bhqk",
            query_blocks,
            near_keys.reshape(blocks, -1, heads, HD),
            preferred_element_type=jnp.float32,
        )
        * scale
    )
    local_scores = jnp.where(local_allowed[:, None, None, :], local_scores, -jnp.inf)
    far_keys = []
    far_values = []
    far_first = []
    far_last = []

    def record(other_keys, other_values, bit):
        factor = 2 ** (local_depth + bit)
        sibling = jnp.bitwise_xor(position // 2**bit, 1)
        first_token = sibling * 2**bit * length + offsets * factor
        lower, upper = covered(first_token, factor)
        far_keys.append(other_keys)
        far_values.append(other_values)
        far_first.append(lower)
        far_last.append(upper)

    rep_keys = level_keys[local_depth]
    rep_values = level_values[local_depth]
    for bit in range(bit_count):
        other_keys, other_values = trade((rep_keys, rep_values), bit)
        record(other_keys, other_values, bit)
        if bit + 1 < bit_count:
            upper_half = position // 2**bit % 2 == 1
            low_keys = jnp.where(upper_half, other_keys, rep_keys)
            high_keys = jnp.where(upper_half, rep_keys, other_keys)
            low_values = jnp.where(upper_half, other_values, rep_values)
            high_values = jnp.where(upper_half, rep_values, other_values)
            rep_keys = jnp.concatenate([pair_mean(low_keys), pair_mean(high_keys)], 0)
            rep_values = jnp.concatenate([pair_mean(low_values), pair_mean(high_values)], 0)
    far_key_set = jnp.concatenate(far_keys, 0).reshape(-1, heads, HD)
    far_value_set = jnp.concatenate(far_values, 0).reshape(-1, heads, HD)
    far_lower = doc_lookup(jnp.concatenate(far_first, 0), doc_start)
    far_upper = doc_lookup(jnp.concatenate(far_last, 0), doc_start)
    far_allowed = (far_lower[None, :] == own_docs[:, None]) & (
        far_upper[None, :] == own_docs[:, None]
    )
    far_scores = (
        jnp.einsum("bqhd,khd->bhqk", query_blocks, far_key_set, preferred_element_type=jnp.float32)
        * scale
    )
    far_scores = jnp.where(far_allowed[:, None, None, :], far_scores, -jnp.inf)
    row_max = jnp.maximum(
        jnp.max(local_scores, axis=-1, keepdims=True), jnp.max(far_scores, axis=-1, keepdims=True)
    )
    local_raised = jnp.exp(local_scores - row_max)
    far_raised = jnp.exp(far_scores - row_max)
    total = jnp.sum(local_raised, axis=-1, keepdims=True) + jnp.sum(
        far_raised, axis=-1, keepdims=True
    )
    local_weights = (local_raised / total).astype(jnp.bfloat16)
    far_weights = (far_raised / total).astype(jnp.bfloat16)
    attended = jnp.einsum(
        "bhqk,bkhd->bqhd",
        local_weights,
        near_values.reshape(blocks, -1, heads, HD),
        preferred_element_type=jnp.float32,
    )
    attended = attended + jnp.einsum(
        "bhqk,khd->bqhd", far_weights, far_value_set, preferred_element_type=jnp.float32
    )
    attended = attended.reshape(length, width).astype(jnp.bfloat16)
    return jnp.dot(
        attended,
        lax.all_gather(out_weight, "ctx", axis=1, tiled=True),
        preferred_element_type=jnp.float32,
    ).astype(jnp.bfloat16)


def solution(mesh):
    fast = mesh.shape["groups"] == 2 and mesh.shape["ctx"] == 16
    placed = (
        P(("groups", "ctx"), None),
        P(("groups", "ctx"), None),
        P(("groups", "ctx"), None),
        P("groups"),
        P(None, "ctx"),
    )
    return jax.shard_map(
        per_device_fast if fast else per_device,
        mesh=mesh,
        in_specs=placed,
        out_specs=P(("groups", "ctx"), None),
        check_vma=False,
    )
```

```python
import functools

import jax
import jax.numpy as jnp
from jax import lax
from jax.experimental import pallas as pl
from jax.experimental.pallas import tpu as pltpu
from jax.sharding import PartitionSpec as P

HD = 128
BLOCK = 128

LOW, HIGH = 4, 8
LOG2_E = 1.4426950408889634
VMEM_LIMIT = 48 * 2**20


def swap(value, mask):
    pairs = [(source, source ^ mask) for source in range(lax.axis_size("ctx"))]
    return lax.ppermute(value, "ctx", pairs)


def swap_groups(value):
    return lax.ppermute(value, "groups", [(0, 1), (1, 0)])


def after(value, other):
    return lax.optimization_barrier((value, other))[0]


def vmem(count):
    return [pl.BlockSpec(memory_space=pltpu.VMEM)] * count


def anywhere(count):
    return [pl.BlockSpec(memory_space=pltpu.HBM)] * count


def loose(count):
    return [pl.BlockSpec(memory_space=pl.ANY)] * count


def call(kernel, outs, in_specs, out_specs=None, work=None, **more):
    return pl.pallas_call(
        kernel,
        out_shape=[jax.ShapeDtypeStruct(shape, jnp.bfloat16) for shape in outs],
        in_specs=[pl.BlockSpec(memory_space=pltpu.SMEM)] + in_specs,
        out_specs=vmem(len(outs)) if out_specs is None else out_specs,
        compiler_params=pltpu.CompilerParams(vmem_limit_bytes=VMEM_LIMIT),
        cost_estimate=None if work is None else pl.CostEstimate(flops=work, bytes_accessed=work // 50, transcendentals=0),
        **more,
    )


def halve(rows):
    count = rows.shape[0]
    row = lax.broadcasted_iota(jnp.int32, (count // 2, count), 0)
    column = lax.broadcasted_iota(jnp.int32, (count // 2, count), 1)
    pick = jnp.where(column // 2 == row, 0.5, 0.0).astype(jnp.bfloat16)
    return jnp.dot(pick, rows, preferred_element_type=jnp.float32).astype(jnp.bfloat16)


def columns_of(place, j, width):
    return pl.ds(pl.multiple_of(jnp.bitwise_xor(place, j) * width, width), width)


def run_copies(copies):
    for copy in copies:
        copy.start()
    for copy in copies:
        copy.wait()


def pack_kernel(places_of, place_ref, q_ref, k_ref, v_ref, other_ref, *refs):
    outs, sems = refs[:-1], refs[-1]
    copies = []
    if len(outs) > len(places_of):
        half = outs[0].shape[0]
        for n in range(2):
            rows = pl.ds(pl.multiple_of(place_ref[1] * half + n * (half // 2), half // 2), half // 2)
            to = outs[0].at[n * (half // 2) : (n + 1) * (half // 2), :]
            copies.append(pltpu.make_async_copy(other_ref.at[rows, :], to, sems.at[n]))
        outs = outs[1:]
    for j, out in zip(places_of, outs):
        columns = columns_of(place_ref[0], j, out.shape[1])
        for n, source in enumerate((q_ref, k_ref, v_ref)):
            to = out.at[n * BLOCK : (n + 1) * BLOCK, :]
            copies.append(pltpu.make_async_copy(source.at[:, columns], to, sems.at[len(copies)]))
    run_copies(copies)


def coarse_kernel(place_ref, a0, a1, a2, a3, third_ref, fourth_ref):
    del place_ref
    row = lax.broadcasted_iota(jnp.int32, (96, 256), 0)
    column = lax.broadcasted_iota(jnp.int32, (96, 256), 1)
    pick = jnp.where(
        row < 64,
        jnp.where(column // 4 == row, 0.25, 0.0),
        jnp.where(column // 8 == row - 64, 0.125, 0.0),
    ).astype(jnp.bfloat16)
    for j, source in enumerate((a0, a1, a2, a3)):
        means = jnp.dot(pick, source[BLOCK : 3 * BLOCK, :], preferred_element_type=jnp.float32).astype(jnp.bfloat16)
        for n in range(2):
            third_ref[n * 128 + 32 * j : n * 128 + 32 * j + 32, :] = means[32 * n : 32 * n + 32, :]
            fourth_ref[n * 64 + 16 * j : n * 64 + 16 * j + 16, :] = means[64 + 16 * n : 80 + 16 * n, :]


def attention_kernel(half, place_ref, doc_ref, *refs):
    a0, a1, a2, a3, l_ref, h_ref, lh_ref = refs[:7]
    out_ref, key_ref, value_ref = refs[-3:]
    own = (a0, a1, a2, a3)
    heads = out_ref.shape[1] // HD
    for n, rows_ref in enumerate((key_ref, value_ref)):
        at = 128 + 128 * n
        for part in range(2):
            rows_ref[256 + 64 * part : 320 + 64 * part, :] = halve(own[2 - 2 * half + part][at : at + 128, :])
        rows_ref[384:512, :] = l_ref[128 * n : 128 * n + 128, :]
        rows_ref[512:576, :] = h_ref[64 * n : 64 * n + 64, :]
        rows_ref[576:640, :] = lh_ref[64 * n : 64 * n + 64, :]
    row = lax.broadcasted_iota(jnp.int32, (1, 640), 1)
    document = jnp.zeros((1, 640), jnp.int32)
    for first, mask in key_places(half):
        document = jnp.where(row >= first, doc_ref[jnp.bitwise_xor(place_ref[2], mask)], document)
    bias = [
        jnp.where(document == doc_ref[jnp.bitwise_xor(place_ref[2], 2 * half + part)], 0.0, -jnp.inf)
        for part in range(2)
    ]
    def score_of(head):
        columns = slice(head * HD, (head + 1) * HD)
        query = jnp.concatenate([own[2 * half + part][0:128, columns] for part in range(2)], 0)
        runs = [own[2 * half + part][128:256, columns] for part in range(2)] + [key_ref[256:640, columns]]
        return jnp.concatenate(
            [
                lax.dot_general(query, run, (((1,), (1,)), ((), ())), preferred_element_type=jnp.float32)
                for run in runs
            ],
            1,
        )

    following = score_of(0)
    for head in range(heads):
        columns = slice(head * HD, (head + 1) * HD)
        score = following
        if head + 1 < heads:
            following = score_of(head + 1)
        raised, inverse = [], []
        for part in range(2):
            biased = score[128 * part : 128 * part + 128, :] + bias[part]
            power = jnp.exp2((biased - jnp.max(biased, axis=-1, keepdims=True)) * (HD ** (-0.5) * LOG2_E))
            raised.append(power.astype(jnp.bfloat16))
            inverse.append(1.0 / jnp.sum(power, axis=-1, keepdims=True))
        raised = jnp.concatenate(raised, 0)
        mixed = jnp.dot(raised[:, 256:640], value_ref[256:640, columns], preferred_element_type=jnp.float32)
        for part in range(2):
            run = slice(128 * part, 128 * part + 128)
            values = own[2 * half + part][256:384, columns]
            mixed += jnp.dot(raised[:, run], values, preferred_element_type=jnp.float32)
        for part in range(2):
            run = slice(128 * part, 128 * part + 128)
            out_ref[run, columns] = (mixed[run, :] * inverse[part]).astype(jnp.bfloat16)


def gather_kernel(place_ref, *refs):
    mixed, rows_ref = refs[:8], refs[8]
    share = mixed[0].shape[1]
    for j in range(4):
        columns = columns_of(place_ref[0], j, share)
        for r in range(4):
            piece = mixed[2 * j + ((r ^ j) >> 1)]
            at = ((r ^ j) & 1) * BLOCK
            rows_ref[r * BLOCK : (r + 1) * BLOCK, columns] = piece[at : at + BLOCK, :]


def project_kernel(place_ref, rows_ref, *refs):
    blocks, outs = list(refs[:-4]), refs[-4:]
    depth = rows_ref.shape[1]
    half = depth // 2
    q = 0
    while blocks:
        total, done = None, 0
        wide = blocks[0].shape[1]
        while done < depth:
            block = blocks.pop(0)
            run = block.shape[0]
            if run == depth:
                rows = rows_ref[...]
            else:
                first = jnp.bitwise_xor(place_ref[1], done // half) * half + done % half
                rows = rows_ref[:, pl.ds(pl.multiple_of(first, HD), run)]
            product = jnp.dot(rows, block[...], preferred_element_type=jnp.float32)
            total = product if total is None else total + product
            done += run
        for r in range(4):
            outs[r][:, q * wide : (q + 1) * wide] = total[r * BLOCK : (r + 1) * BLOCK, :].astype(jnp.bfloat16)
        q += 1


def place_kernel(group, place_ref, *refs):
    sources, out_ref, sems = refs[:4], refs[-2], refs[-1]
    wide = out_ref.shape[1] // 16
    copies = []
    for j, source in enumerate(sources):
        for q, mask in enumerate(((0, HIGH, LOW), (LOW | HIGH,))[group]):
            at = pl.multiple_of(jnp.bitwise_xor(place_ref[2], mask | j) * wide, wide)
            to = out_ref.at[:, pl.ds(at, wide)]
            copies.append(pltpu.make_async_copy(source.at[:, q * wide : (q + 1) * wide], to, sems.at[len(copies)]))
    run_copies(copies)


def key_places(half):
    places = [(128 * part, 2 * half + part) for part in range(2)]
    places += [(256 + 64 * part, 2 - 2 * half + part) for part in range(2)]
    places += [(384 + 32 * j, j | LOW) for j in range(4)]
    places += [(512 + 16 * j, j | HIGH) for j in range(4)]
    places += [(576 + 16 * j, j | LOW | HIGH) for j in range(4)]
    return places


def per_device_fast(queries, keys, values, doc_start, out_weight):
    length, width = queries.shape
    share = width // 4
    depth, wide = out_weight.shape
    group = lax.axis_index("groups")
    position = lax.axis_index("ctx")
    places = jnp.stack([position & 3, group, position]).astype(jnp.int32)

    own_block = out_weight
    queries, keys, values, out_weight = (
        pltpu.with_memory_space_constraint(array, pltpu.HBM) for array in (queries, keys, values, out_weight)
    )
    (ours,) = call(
        functools.partial(pack_kernel, ()),
        [(depth // 2, wide)],
        anywhere(4),
        scratch_shapes=[pltpu.SemaphoreType.DMA((2,))],
        name="pack",
    )(places, queries, keys, values, out_weight)
    across = call(
        functools.partial(pack_kernel, (2, 3)),
        [(3 * length, share)] * 2,
        anywhere(3) + loose(1),
        scratch_shapes=[pltpu.SemaphoreType.DMA((6,))],
        name="pack0",
    )(places, queries, keys, values, ours)
    near = call(
        functools.partial(pack_kernel, (1, 0)),
        [(3 * length, share)] * 2,
        anywhere(3) + loose(1),
        scratch_shapes=[pltpu.SemaphoreType.DMA((6,))],
        work=2 * 10**9,
        name="pack1",
    )(places, queries, keys, values, across[0])
    own = [near[1], swap(near[0], 1), swap(across[0], 2), swap(across[1], 3)]
    half_h = swap(ours, HIGH)
    ours_l = swap(ours, LOW)
    third, fourth = call(
        coarse_kernel, [(2 * length, share), (length, share)], vmem(4), name="coarse"
    )(places, *own)
    third, fourth = after((third, fourth), (half_h, ours_l))
    from_h, from_lh = swap(fourth, HIGH), swap(fourth, LOW | HIGH)
    far = [swap(third, LOW), from_h, from_lh]
    other_h = swap_groups(after(half_h, third))
    half_d = swap(after(half_h, far[1]), LOW)
    other_l = swap_groups(after(ours_l, other_h))
    quarter = depth // 4
    other_d = [swap_groups(after(half_d, other_l)[:quarter]), swap(other_h[quarter:], LOW)]

    pieces = [[None] * 2 for _ in range(4)]
    before = near[1]
    for n in range(2):
        (attended,) = call(
            functools.partial(attention_kernel, n),
            [(2 * length, share)],
            [pl.BlockSpec(memory_space=pltpu.SMEM)] + vmem(7) + loose(1),
            scratch_shapes=[pltpu.VMEM((640, share), jnp.bfloat16)] * 2,
            work=2 * 10**9,
            name="attend%d" % n,
        )(places, doc_start, *own, *far, before)
        before = attended
        pieces[0][n] = attended
        pieces[2][n] = swap(attended, 2)
    for n in range(2):
        pieces[1][n] = swap(after(pieces[0][n], (pieces[2][0], half_d)), 1)
    pieces[3][0] = swap(after(pieces[2][0], half_d), 1)
    pieces[3][1] = swap(after(pieces[2][1], pieces[3][0]), 1)
    mixed = [piece for pair in pieces for piece in pair]

    (rows,) = call(gather_kernel, [(4 * length, width)], vmem(8), name="gather")(places, *mixed)
    received = []
    for count, blocks in ((3, (own_block, half_h, other_h, ours_l, other_l)), (1, (half_d, *other_d))):
        parts = call(project_kernel, [(length, count * wide)] * 4, vmem(1 + len(blocks)), name="project%d" % count)(
            places, rows, *blocks
        )
        received += [parts[0]] + [swap(parts[j], j) for j in (1, 2, 3)]
    for n in range(2):
        earlier = [] if n == 0 else [out]
        (out,) = call(
            functools.partial(place_kernel, n),
            [(length, 16 * wide)],
            anywhere(4 + len(earlier)),
            anywhere(1),
            scratch_shapes=[pltpu.SemaphoreType.DMA((4 if earlier else 12,))],
            input_output_aliases={5: 0} if earlier else {},
            name="place%d" % n,
        )(places, *received[4 * n : 4 * n + 4], *earlier)
    return out


def partner(value, axis, apart):
    mask = 2**apart
    pairs = [(source, source ^ mask) for source in range(lax.axis_size(axis))]
    return lax.ppermute(value, axis, pairs)


def pair_mean(array):
    halves = array.reshape(array.shape[0] // 2, 2, array.shape[1]).astype(jnp.float32)
    return ((halves[:, 0] + halves[:, 1]) * 0.5).astype(jnp.bfloat16)


def doc_lookup(blocks, table):
    labels = jnp.arange(table.shape[0], dtype=jnp.int32)
    return jnp.sum(jnp.where(blocks[..., None] == labels, table, 0), axis=-1)


def covered(first_token, factor):
    return (first_token // BLOCK, (first_token + factor - 1) // BLOCK)


def trade(pair, bit):
    return partner((pair[0], pair[1]), "ctx", bit)


def per_device(queries, keys, values, doc_start, out_weight):
    length, width = queries.shape
    heads = width // HD
    blocks = length // BLOCK
    local_depth = blocks.bit_length() - 1
    devices = lax.axis_size("ctx")
    position = lax.axis_index("ctx")
    bit_count = devices.bit_length() - 1
    scale = HD ** (-0.5)
    offsets = jnp.arange(BLOCK, dtype=jnp.int32)
    block_ids = position * blocks + jnp.arange(blocks, dtype=jnp.int32)
    own_docs = doc_lookup(block_ids, doc_start)
    level_keys = [keys]
    level_values = [values]
    near_keys = keys.reshape(blocks, BLOCK, width)
    near_values = values.reshape(blocks, BLOCK, width)
    near_first = jnp.broadcast_to(block_ids[:, None], (blocks, BLOCK))
    near_last = jnp.broadcast_to(block_ids[:, None], (blocks, BLOCK))
    local_allowed = (doc_lookup(near_first, doc_start) == own_docs[:, None]) & (
        doc_lookup(near_last, doc_start) == own_docs[:, None]
    )
    query_blocks = queries.reshape(blocks, BLOCK, heads, HD)
    local_scores = (
        jnp.einsum(
            "bqhd,bkhd->bhqk",
            query_blocks,
            near_keys.reshape(blocks, -1, heads, HD),
            preferred_element_type=jnp.float32,
        )
        * scale
    )
    local_scores = jnp.where(local_allowed[:, None, None, :], local_scores, -jnp.inf)
    far_keys = []
    far_values = []
    far_first = []
    far_last = []

    def record(other_keys, other_values, bit):
        factor = 2 ** (local_depth + bit)
        sibling = jnp.bitwise_xor(position // 2**bit, 1)
        first_token = sibling * 2**bit * length + offsets * factor
        lower, upper = covered(first_token, factor)
        far_keys.append(other_keys)
        far_values.append(other_values)
        far_first.append(lower)
        far_last.append(upper)

    rep_keys = level_keys[local_depth]
    rep_values = level_values[local_depth]
    for bit in range(bit_count):
        other_keys, other_values = trade((rep_keys, rep_values), bit)
        record(other_keys, other_values, bit)
        if bit + 1 < bit_count:
            upper_half = position // 2**bit % 2 == 1
            low_keys = jnp.where(upper_half, other_keys, rep_keys)
            high_keys = jnp.where(upper_half, rep_keys, other_keys)
            low_values = jnp.where(upper_half, other_values, rep_values)
            high_values = jnp.where(upper_half, rep_values, other_values)
            rep_keys = jnp.concatenate([pair_mean(low_keys), pair_mean(high_keys)], 0)
            rep_values = jnp.concatenate([pair_mean(low_values), pair_mean(high_values)], 0)
    far_key_set = jnp.concatenate(far_keys, 0).reshape(-1, heads, HD)
    far_value_set = jnp.concatenate(far_values, 0).reshape(-1, heads, HD)
    far_lower = doc_lookup(jnp.concatenate(far_first, 0), doc_start)
    far_upper = doc_lookup(jnp.concatenate(far_last, 0), doc_start)
    far_allowed = (far_lower[None, :] == own_docs[:, None]) & (
        far_upper[None, :] == own_docs[:, None]
    )
    far_scores = (
        jnp.einsum("bqhd,khd->bhqk", query_blocks, far_key_set, preferred_element_type=jnp.float32)
        * scale
    )
    far_scores = jnp.where(far_allowed[:, None, None, :], far_scores, -jnp.inf)
    row_max = jnp.maximum(
        jnp.max(local_scores, axis=-1, keepdims=True), jnp.max(far_scores, axis=-1, keepdims=True)
    )
    local_raised = jnp.exp(local_scores - row_max)
    far_raised = jnp.exp(far_scores - row_max)
    total = jnp.sum(local_raised, axis=-1, keepdims=True) + jnp.sum(
        far_raised, axis=-1, keepdims=True
    )
    local_weights = (local_raised / total).astype(jnp.bfloat16)
    far_weights = (far_raised / total).astype(jnp.bfloat16)
    attended = jnp.einsum(
        "bhqk,bkhd->bqhd",
        local_weights,
        near_values.reshape(blocks, -1, heads, HD),
        preferred_element_type=jnp.float32,
    )
    attended = attended + jnp.einsum(
        "bhqk,khd->bqhd", far_weights, far_value_set, preferred_element_type=jnp.float32
    )
    attended = attended.reshape(length, width).astype(jnp.bfloat16)
    return jnp.dot(
        attended,
        lax.all_gather(out_weight, "ctx", axis=1, tiled=True),
        preferred_element_type=jnp.float32,
    ).astype(jnp.bfloat16)


def solution(mesh):
    fast = mesh.shape["groups"] == 2 and mesh.shape["ctx"] == 16
    placed = (
        P(("groups", "ctx"), None),
        P(("groups", "ctx"), None),
        P(("groups", "ctx"), None),
        P("groups"),
        P(None, "ctx"),
    )
    return jax.shard_map(
        per_device_fast if fast else per_device,
        mesh=mesh,
        in_specs=placed,
        out_specs=P(("groups", "ctx"), None),
        check_vma=False,
    )
```
